32 devices in a mesh: theta: 16 (over z, x, core), xr: 2 (over y).
Axes of the slice: x: 2, y: 2, z: 4, core: 2. Of those that a mesh axis runs over, the one named last changes fastest.
Arguments:
- state: float32 [3, 2, 5, 128, 16, 128], P(None, None, None, 'theta', 'xr'), may hold values from -6 to 6
- source: float32 [3, 2, 5, 128, 16, 128], P(None, None, None, 'theta', 'xr'), may hold values from -6 to 6
- sigma: float32 [128, 16, 128], P('theta', 'xr'), may hold values from 0.25 to 4
- stagger: int32 [32], P('theta'), may hold values from 0 to 3
- a_theta: float32 [4, 5, 5], replicated, may hold values from -2.5 to 2.5
- a_axial: float32 [5, 5], replicated, may hold values from -2.5 to 2.5
- a_radial: float32 [5, 5], replicated, may hold values from -2.5 to 2.5
- mode_order: int32 [3, 128], replicated, may hold values from -32 to 32
- mode_radial: int32 [3, 128], replicated, may hold values from 0 to 7
- mode_plane: int32 [3, 128], replicated, may hold values from 0 to 1
- gust: float32 [3, 2, 128], replicated, may hold values from -6 to 6
- l_rows: float32 [2, 5], replicated, may hold values from -4 to 4
- r_cols: float32 [2, 5], replicated, may hold values from -4 to 4
Outputs:
- fields: float32 [3, 2, 5, 128, 16, 128], P(None, None, None, 'theta', 'xr')
- amplitudes: float32 [3, 2, 2, 128], replicated
The draws below stay inside these ranges and needn't reach their ends.
Inputs may be any that keep to these rules, and one draw needn't show every extreme that they name: `mode_plane`: 0 names the inlet plane, 1 the exit plane.
All inputs are finite; a program needn't handle non-finite values.
Results may differ from the reference program's by a relative error of at most 0.0003.
Values sent between devices are 32-bit elements; how exact they have to be, the bound alone decides.
A program may use at most 64 MiB of HBM per device.

```python
import math
import jax
import jax.numpy as jnp
from jax import lax

H = 3
V = 5
STAGGERS = 4
CPP = 4
NR = 128
MODES = 128
M_MAX = 32
NRAD = 8
PASSAGES = 32
NT = 128
NX = 16


def set_ends(array, stream_key, smallest, top_value):
    index_at = [jax.random.randint(jax.random.fold_in(stream_key, axis), (), 0, length) for axis, length in enumerate(array.shape)]
    longest = array.shape.index(max(array.shape))
    neighbour = index_at[:longest] + [(index_at[longest] + 1) % array.shape[longest]] + index_at[longest + 1:]
    return array.at[tuple(index_at)].set(smallest).at[tuple(neighbour)].set(top_value)


def steps_of(stream_key, dims, shards, low, top_value):
    def one(axis_at, blocks):
        steps = jax.random.uniform(jax.random.fold_in(jax.random.fold_in(stream_key, 6), axis_at), (blocks,), jnp.float32, low / len(shards), top_value / len(shards))
        return jnp.repeat(jnp.exp(steps), dims[axis_at] // blocks).reshape((-1,) + (1,) * (len(dims) - axis_at - 1))

    level = one(*shards[0])
    for cut in shards[1:]:
        level = level * one(*cut)
    return level


def bell_draw(key, dims, deviation, reach, split=(), dtype=jnp.bfloat16):
    entries = deviation * jax.random.normal(key, dims, jnp.float32)
    if split:
        entries = entries * steps_of(key, dims, split, -0.22, 0.18)
    return jnp.clip(entries, -reach, reach).astype(dtype)


def setup_inputs(seed: int = 0) -> dict:
    streams_of = jax.random.split(jax.random.key(seed), 14)
    return {
        "state": bell_draw(streams_of[0], (H, 2, V, NT, NX, NR), 1.0, 6.0, ((3, 16), (4, 2)), jnp.float32),
        "source": bell_draw(streams_of[1], (H, 2, V, NT, NX, NR), 1.0, 6.0, ((3, 16), (4, 2)), jnp.float32),
        "sigma": jnp.clip(jnp.exp(math.log(4.0) - 2.7725887 * jax.random.uniform(streams_of[2], (NT, NX, NR), jnp.float32) ** steps_of(streams_of[2], (NT, NX, NR), ((0, 16), (1, 2)), -0.2, 0.2)), 0.25, 4.0),
        "stagger": set_ends(jax.random.randint(streams_of[3], (PASSAGES,), 0, STAGGERS), jax.random.fold_in(streams_of[3], 1), 0, STAGGERS - 1).astype(jnp.int32),
        "a_theta": bell_draw(streams_of[4], (STAGGERS, V, V), V ** -0.5, 2.5, (), jnp.float32),
        "a_axial": bell_draw(streams_of[5], (V, V), V ** -0.5, 2.5, (), jnp.float32),
        "a_radial": bell_draw(streams_of[6], (V, V), V ** -0.5, 2.5, (), jnp.float32),
        "mode_order": set_ends(jax.random.randint(streams_of[7], (H, MODES), 0 - M_MAX, M_MAX + 1), jax.random.fold_in(streams_of[7], 1), 0 - M_MAX, M_MAX).astype(jnp.int32),
        "mode_radial": set_ends(jax.random.randint(streams_of[8], (H, MODES), 0, NRAD), jax.random.fold_in(streams_of[8], 1), 0, NRAD - 1).astype(jnp.int32),
        "mode_plane": set_ends(jax.random.randint(streams_of[9], (H, MODES), 0, 2), jax.random.fold_in(streams_of[9], 1), 0, 1).astype(jnp.int32),
        "gust": bell_draw(streams_of[10], (H, 2, MODES), 1.0, 6.0, (), jnp.float32),
        "l_rows": bell_draw(streams_of[11], (2, V), 1.0, 4.0, (), jnp.float32),
        "r_cols": bell_draw(streams_of[12], (2, V), 1.0, 4.0, (), jnp.float32),
    }


courant = 0.5
viscosity = 0.1
base_frequency = 0.5
highest = lax.Precision.HIGHEST

def reference(state, source, sigma, stagger, a_theta, a_axial, a_radial, mode_order, mode_radial, mode_plane, gust, l_rows, r_cols):
    cells = jnp.arange(NT).astype(jnp.int32)
    cell_matrix = a_theta[stagger[cells // CPP]]
    step_size = courant / (1.0 + sigma)
    scale = 1.0 / math.sqrt(NT * NR)
    radial_pos = jnp.arange(NR).astype(jnp.float32) + 0.5

    def residual(field, freq, forcing):
        diff_theta = (jnp.roll(field, -1, 2) - jnp.roll(field, 1, 2)) * 0.5
        lap_theta = jnp.roll(field, -1, 2) + jnp.roll(field, 1, 2) - 2.0 * field
        padded_x = jnp.pad(field, ((0, 0), (0, 0), (0, 0), (1, 1), (0, 0)))
        diff_axial = (padded_x[:, :, :, 2:] - padded_x[:, :, :, :-2]) * 0.5
        lap_axial = padded_x[:, :, :, 2:] + padded_x[:, :, :, :-2] - 2.0 * field
        padded_r = jnp.pad(field, ((0, 0), (0, 0), (0, 0), (0, 0), (1, 1)))
        diff_radial = (padded_r[..., 2:] - padded_r[..., :-2]) * 0.5
        lap_radial = padded_r[..., 2:] + padded_r[..., :-2] - 2.0 * field
        turned = jnp.stack([-field[1], field[0]])
        flux = jnp.einsum('tvw,pwtxr->pvtxr', cell_matrix, diff_theta, precision=highest)
        flux = flux + jnp.einsum('vw,pwtxr->pvtxr', a_axial, diff_axial, precision=highest)
        flux = flux + jnp.einsum('vw,pwtxr->pvtxr', a_radial, diff_radial, precision=highest)
        return freq * turned + flux - viscosity * (lap_theta + lap_axial + lap_radial) + sigma * field - forcing

    def one_harmonic(items):
        field, forcing, freq, orders, radial, planes, target = items
        first = field - 0.5 * step_size * residual(field, freq, forcing)
        second = field - step_size * residual(first, freq, forcing)
        inlet = jnp.einsum('v,pvtr->ptr', l_rows[0], second[:, :, :, 0, :], precision=highest)
        outlet = jnp.einsum('v,pvtr->ptr', l_rows[1], second[:, :, :, NX - 1, :], precision=highest)
        plane_values = jnp.stack([inlet, outlet])
        angle = 2.0 * math.pi * jnp.mod(orders[:, None] * cells[None, :], NT).astype(jnp.float32) / NT
        cos_table = jnp.cos(angle)
        sin_table = jnp.sin(angle)
        radial_table = jnp.where(radial[:, None] == 0, 1.0, math.sqrt(2.0) * jnp.cos(math.pi * radial[:, None].astype(jnp.float32) * radial_pos[None, :] / NR))
        projected = jnp.einsum('bptr,kr->bptk', plane_values, radial_table, precision=highest)
        amp_real = scale * (jnp.einsum('btk,kt->bk', projected[:, 0], cos_table, precision=highest) + jnp.einsum('btk,kt->bk', projected[:, 1], sin_table, precision=highest))
        amp_imag = scale * (jnp.einsum('btk,kt->bk', projected[:, 1], cos_table, precision=highest) - jnp.einsum('btk,kt->bk', projected[:, 0], sin_table, precision=highest))
        weight = (planes[None, :] == jnp.arange(2)[:, None]).astype(jnp.float32)
        miss_real = weight * (amp_real - target[0][None, :])
        miss_imag = weight * (amp_imag - target[1][None, :])
        coef_real = miss_real[:, :, None] * cos_table[None] - miss_imag[:, :, None] * sin_table[None]
        coef_imag = miss_real[:, :, None] * sin_table[None] + miss_imag[:, :, None] * cos_table[None]
        corr_real = jnp.einsum('bkt,kr->btr', coef_real, radial_table, precision=highest)
        corr_imag = jnp.einsum('bkt,kr->btr', coef_imag, radial_table, precision=highest)
        correction = scale * jnp.stack([corr_real, corr_imag], axis=1)
        second = second.at[:, :, :, 0, :].add(-r_cols[0][None, :, None, None] * correction[0][:, None])
        second = second.at[:, :, :, NX - 1, :].add(-r_cols[1][None, :, None, None] * correction[1][:, None])
        measured = jnp.stack([weight * amp_real, weight * amp_imag], axis=1)
        return (second, measured)
    freqs = base_frequency * (1.0 + jnp.arange(H).astype(jnp.float32))
    fields, amplitudes = lax.map(one_harmonic, (state, source, freqs, mode_order, mode_radial, mode_plane, gust))
    return (fields, amplitudes)
```

```python
import functools
import math

import jax
import jax.numpy as jnp
from jax import lax
from jax.experimental import pallas as pl
from jax.experimental.pallas import tpu as pltpu
from jax.sharding import PartitionSpec as P

courant = 0.5
viscosity = 0.1
base_frequency = 0.5
highest = lax.Precision.HIGHEST
MESH = pl.DeviceIdType.MESH


def kernel(
    dims,
    state_hbm,
    source_hbm,
    sigma_hbm,
    *refs,
):
    small_hbm, refs = refs[:10], refs[10:]
    out, amps, refs = refs[0], refs[1], refs[2:]
    small, refs = refs[:10], refs[10:]
    stagger, a_theta, a_axial, a_radial, l_rows, r_cols = small[:6]
    mode_order, mode_radial, mode_plane, gust = small[6:]
    (
        state,
        source,
        sigma,
        first,
        step,
        uhalo,
        fhalo,
        fsend,
        xuhalo,
        xusend,
        xfhalo,
        xfsend,
        xinfo,
        xinfo_send,
        corner,
        corner_send,
        crit,
        crit_send,
        info,
        info_send,
        ghost_step,
        ghost_matrix,
        planes,
        phi,
        cosines,
        sines,
        part,
        parts,
        load_sem,
        small_sem,
        send_sem,
        recv_sem,
        csend_sem,
        crecv_sem,
        psend_sem,
        precv_sem,
    ) = refs
    T, X, H, V, CT, CX, NR, NPASS, NMODE = dims
    F = 2 * V
    HF = H * F
    CPP = CT // NPASS
    N = T * X
    HP = 2 * H
    PR = 2 * CT
    th = lax.axis_index("theta")
    xr = lax.axis_index("xr")
    me = th * X + xr
    up = lax.rem(th + 1, T)
    down = lax.rem(th + T - 1, T)
    has_lo = xr > 0
    has_hi = xr < X - 1
    on_plane = jnp.logical_not(has_lo & has_hi)
    total_theta = CT * T
    scale = 1.0 / math.sqrt(total_theta * NR)
    U, FIRST, INFO, CRIT, XU, XF, XINFO = range(7)

    barrier = pltpu.get_barrier_semaphore()

    def for_others(act):
        def ring(t):
            for x in range(X):

                @pl.when((t != th) | (x != xr))
                def _():
                    act(t, x)

        if N <= 64:
            for t in range(T):
                ring(t)
        else:
            pl.loop(0, T)(ring)

    def greet(t, x):
        pl.semaphore_signal(barrier, inc=1, device_id=(t, x), device_id_type=MESH)

    little = [
        pltpu.make_async_copy(src, dst, small_sem.at[i])
        for i, (src, dst) in enumerate(zip(small_hbm, small))
    ]
    loads = [
        pltpu.make_async_copy(state_hbm, state.at[:, pl.ds(CX, CT * CX)], load_sem.at[0]),
        pltpu.make_async_copy(sigma_hbm, sigma, load_sem.at[1]),
        pltpu.make_async_copy(source_hbm, source, load_sem.at[2]),
    ]
    for copy in loads + little:
        copy.start()
    for_others(greet)

    zero = jnp.zeros((HF, CX, NR), jnp.float32)
    for buf in (state, first):
        buf[:, pl.ds(0, CX)] = zero
        buf[:, pl.ds(CX + CT * CX, CX)] = zero
    planes[...] = jnp.zeros_like(planes)
    part[...] = jnp.zeros_like(part)
    crit_rows = -(-HF // 8) * 8
    crit_send[...] = jnp.zeros_like(crit_send)
    if crit.shape[2] > crit_rows:
        rest = crit.shape[2] - crit_rows
        crit[:, :, pl.ds(crit_rows, rest)] = jnp.zeros((2, 3, rest, NR), jnp.float32)

    def x_rows(row):
        return pl.ds(row, CT, stride=CX)

    def neighbour(side):
        return (up if side == 0 else down, xr)

    def message(kind, side, src, dst, target):
        return pltpu.make_async_remote_copy(
            src_ref=src,
            dst_ref=dst,
            send_sem=send_sem.at[kind, side],
            recv_sem=recv_sem.at[kind, side],
            device_id=target,
            device_id_type=MESH,
        )

    def u_copy(side):
        rows = pl.ds(CX + ((CT - 1) * CX if side == 0 else 0), CX)
        return message(U, side, state.at[:, rows], uhalo.at[side], neighbour(side))

    def first_copy(side):
        return message(FIRST, side, fsend.at[side], fhalo.at[side], neighbour(side))

    def info_copy(side):
        return message(INFO, side, info_send.at[side], info.at[side], neighbour(side))

    def crit_copy(side):
        rows = pl.ds(0, crit_rows)
        return message(
            CRIT, side, crit_send.at[side, :, rows], crit.at[side, :, rows], neighbour(side)
        )

    def x_neighbour(side):
        return (th, xr + 1 if side == 0 else xr - 1)

    def x_copy(kind, side):
        src, dst = {
            XU: (xusend, xuhalo),
            XF: (xfsend, xfhalo),
            XINFO: (xinfo_send, xinfo),
        }[kind]
        return message(kind, side, src.at[side], dst.at[side], x_neighbour(side))

    def corner_copy(side, x_side):
        return pltpu.make_async_remote_copy(
            src_ref=corner_send.at[side, x_side],
            dst_ref=corner.at[side, x_side],
            send_sem=csend_sem.at[side, x_side],
            recv_sem=crecv_sem.at[side, x_side],
            device_id=(up if side == 0 else down, xr + 1 if x_side == 0 else xr - 1),
            device_id_type=MESH,
        )

    def when_x_target(side, act):
        pl.when(has_hi if side == 0 else has_lo)(act)

    def when_x_source(side, act):
        pl.when(has_lo if side == 0 else has_hi)(act)

    row_id = lax.broadcasted_iota(jnp.int32, (CX, NR), 0)
    lane_id = lax.broadcasted_iota(jnp.int32, (CX, NR), 1)
    first_row = row_id == 0
    last_row = row_id == CX - 1
    first_lane = lane_id == 0
    last_lane = lane_id == NR - 1

    SPAN = 128
    cells = lax.broadcasted_iota(jnp.int32, (PR, SPAN), 0)
    cells = th * CT + jnp.where(cells >= CT + 2, CT + 1 - cells, cells)
    orders = lax.broadcasted_iota(jnp.int32, (PR, SPAN), 1) - SPAN // 2
    turns = (orders * cells).astype(jnp.float32)
    turns = turns - jnp.floor(turns / total_theta) * total_theta
    angle = (2.0 * math.pi) * turns / total_theta
    cos_table = jnp.cos(angle)
    sin_table = jnp.sin(angle)
    radial = lax.broadcasted_iota(jnp.int32, (8, NR), 0)
    radial_pos = lax.broadcasted_iota(jnp.int32, (8, NR), 1).astype(jnp.float32) + 0.5
    phi_table = jnp.where(
        radial == 0,
        1.0,
        math.sqrt(2.0) * jnp.cos(math.pi * radial.astype(jnp.float32) * radial_pos / NR),
    )

    def dot(a, b, dims=(((1,), (0,)), ((), ()))):
        return lax.dot_general(
            a, b, dims, precision=highest, preferred_element_type=jnp.float32
        )

    for copy in little:
        copy.wait()
    order_id = lax.broadcasted_iota(jnp.int32, (SPAN, NMODE), 0) - SPAN // 2
    radial_id = lax.broadcasted_iota(jnp.int32, (8, NMODE), 0)
    for h in range(H):
        chosen = (mode_order[pl.ds(h, 1)] == order_id).astype(jnp.float32)
        cosines[h] = dot(cos_table, chosen)
        sines[h] = dot(sin_table, chosen)
        chosen = (mode_radial[pl.ds(h, 1)] == radial_id).astype(jnp.float32)
        phi[h] = dot(phi_table, chosen, (((0,), (0,)), ((), ())))

    loads[1].wait()
    step[...] = courant / (1.0 + sigma[...])
    for side in range(2):
        edge, second = (CT - 1, CT - 2) if side == 0 else (0, 1)
        info_send[side, pl.ds(0, CX)] = sigma[pl.ds(edge * CX, CX)]
        info_send[side, pl.ds(CX, CX)] = sigma[pl.ds(second * CX, CX)]
        kind = stagger[NPASS - 1 if side == 0 else 0].astype(jnp.float32)
        info_send[side, pl.ds(2 * CX, 8)] = jnp.full((8, NR), kind, jnp.float32)
    loads[0].wait()
    loads[2].wait()

    def update(field, result, result_offset, factor, t, h):
        freq = base_frequency * (h + 1).astype(jnp.float32)
        base = pl.multiple_of(t * CX, CX)
        kind = stagger[t // CPP]
        dt = step[pl.ds(base, CX)]
        if factor != 1.0:
            dt = factor * dt
        damp = sigma[pl.ds(base, CX)] + 6.0 * viscosity
        at = [[a_theta[v, kind, w] for w in range(V)] for v in range(V)]
        for p in range(2):
            flux = [None] * V
            sums = []
            for w in range(V):
                f = h * F + p * V + w
                u = field[f, pl.ds(base + CX, CX)]
                tm = field[f, pl.ds(base, CX)]
                tp = field[f, pl.ds(base + 2 * CX, CX)]
                xm = jnp.where(first_row, 0.0, pltpu.roll(u, 1, 0))
                xp = jnp.where(last_row, 0.0, pltpu.roll(u, CX - 1, 0))
                rm = jnp.where(first_lane, 0.0, pltpu.roll(u, 1, 1))
                rp = jnp.where(last_lane, 0.0, pltpu.roll(u, NR - 1, 1))
                dth, dx, dr = tp - tm, xp - xm, rp - rm
                sums.append(((tp + tm) + (xp + xm)) + (rp + rm))
                for v in range(V):
                    term = at[v][w] * dth + a_axial[v, w] * dx + a_radial[v, w] * dr
                    flux[v] = term if flux[v] is None else flux[v] + term
            for v in range(V):
                f = h * F + p * V + v
                u = field[f, pl.ds(base + CX, CX)]
                other = field[h * F + (1 - p) * V + v, pl.ds(base + CX, CX)]
                turned = -freq if p == 0 else freq
                res = (
                    0.5 * flux[v]
                    - viscosity * sums[v]
                    + damp * u
                    + turned * other
                    - source[f, pl.ds(base, CX)]
                )
                start = state[f, pl.ds(base + CX, CX)]
                result[f, pl.ds(base + result_offset, CX)] = start - dt * res

    def halo_terms(values, matrix, sign):
        terms = []
        for v in range(V):
            total = matrix(v, 0) * values[0]
            for w in range(1, V):
                total = total + matrix(v, w) * values[w]
            terms.append((sign * 0.5) * total - viscosity * values[v])
        return terms

    def pack_crit(side):
        t = CT - 1 if side == 0 else 0

        def pack(x, inner):
            for f in range(HF):
                at = pl.ds(f, 1)
                crit_send[side, 0, at] = state[f, pl.ds(CX + t * CX + x, 1)]
                crit_send[side, 1, at] = state[f, pl.ds(CX + t * CX + inner, 1)]
                crit_send[side, 2, at] = first[f, pl.ds(CX + t * CX + x, 1)]

        @pl.when(jnp.logical_not(has_lo))
        def _():
            pack(0, 1)

        @pl.when(jnp.logical_not(has_hi))
        def _():
            pack(CX - 1, CX - 2)

    def open_sends():
        pl.semaphore_wait(barrier, N - 1)
        for side in (1, 0):
            info_copy(side).start()
        pack_crit(1)

        @pl.when(on_plane & (th > 0))
        def _():
            crit_copy(1).start()

        for side in range(2):

            def _():
                x = CX - 1 if side == 0 else 0
                for f in range(HF):
                    xusend[side, f] = state[f, x_rows(CX + x), :]
                xinfo_send[side] = sigma[x_rows(x), :]
                x_copy(XU, side).start()
                x_copy(XINFO, side).start()
                for t_side in range(2):
                    row = CX + ((CT - 1) * CX if t_side == 0 else 0) + x
                    for f in range(HF):
                        corner_send[t_side, side, pl.ds(f, 1)] = state[f, pl.ds(row, 1)]
                    corner_copy(t_side, side).start()

            when_x_target(side, _)
        for side in range(2):
            u_copy(side).start()

    def edge_sends():
        pack_crit(0)

        @pl.when(on_plane & (th == T - 1))
        def _():
            crit_copy(0).start()

        for side in range(2):
            rows = pl.ds(CX + ((CT - 1) * CX if side == 0 else 0), CX)
            fsend[side] = first[:, rows]
            first_copy(side).start()

    early = th < T // 2
    open_at = jnp.where(early, CT - 1, 0)
    edge_at = jnp.where(early, CT - 1, 1)

    @pl.loop(0, CT)
    def _(i):
        t = jnp.where(i == 0, 0, jnp.where(i == 1, CT - 1, i - 1))

        @pl.loop(0, H)
        def _(h):
            update(state, first, CX, 0.5, t, h)

        pl.when(i == open_at)(open_sends)
        pl.when(i == edge_at)(edge_sends)

    for side in range(2):

        def _():
            x = CX - 1 if side == 0 else 0
            for f in range(HF):
                xfsend[side, f] = first[f, x_rows(CX + x), :]
            x_copy(XF, side).start()

        when_x_target(side, _)

    def own_planes(b):
        x = 0 if b == 0 else CX - 1
        inner = 1 if b == 0 else CX - 2
        lines = lax.broadcasted_iota(jnp.int32, (CT, NR), 0)
        lanes = lax.broadcasted_iota(jnp.int32, (CT, NR), 1)
        top, bottom = lines == 0, lines == CT - 1
        left, right = lanes == 0, lanes == NR - 1
        ls, gxs, grs, gts = [], [], [], []
        for w in range(V):
            ls.append(l_rows[b, w])
            gx = gr = 0.0
            for v in range(V):
                gx = gx + l_rows[b, v] * a_axial[v, w]
                gr = gr + l_rows[b, v] * a_radial[v, w]
            gt = None
            for k in range(NPASS):
                row = 0.0
                for v in range(V):
                    row = row + l_rows[b, v] * a_theta[v, stagger[k], w]
                gt = row if gt is None else jnp.where(lines >= k * CPP, row, gt)
            gxs.append(gx)
            grs.append(gr)
            gts.append(gt)
        damp = sigma[x_rows(x), :] + 6.0 * viscosity
        dt = step[x_rows(x), :]

        @pl.loop(0, H)
        def _(h):
            freq = base_frequency * (h + 1).astype(jnp.float32)
            fields = [0.0, 0.0]
            rest = []
            for p in range(2):
                along_t = start = forcing = inside = radial = 0.0
                flux = sums = 0.0
                for w in range(V):
                    f = h * F + p * V + w
                    u = first[f, x_rows(CX + x), :]
                    near = first[f, x_rows(CX + inner), :]
                    tm = jnp.where(top, 0.0, pltpu.roll(u, 1, 0))
                    tp = jnp.where(bottom, 0.0, pltpu.roll(u, CT - 1, 0))
                    dx = near if b == 0 else -near
                    flux = flux + (gts[w] * (tp - tm) + gxs[w] * dx)
                    sums = sums + ls[w] * ((tp + tm) + near)
                    fields[p] = fields[p] + ls[w] * u
                    radial = radial + grs[w] * u
                    forcing = forcing + ls[w] * source[f, x_rows(x), :]
                    start = start + ls[w] * state[f, x_rows(CX + x), :]
                for value, weight, sign in ((radial, 0.5, -1.0), (fields[p], -viscosity, 1.0)):
                    rm = jnp.where(left, 0.0, pltpu.roll(value, 1, 1))
                    rp = jnp.where(right, 0.0, pltpu.roll(value, NR - 1, 1))
                    inside = inside + weight * (rp + sign * rm)
                res = 0.5 * flux - viscosity * sums + inside + damp * fields[p] - forcing
                rest.append((start, res))
            for p in range(2):
                start, res = rest[p]
                turned = -freq if p == 0 else freq
                res = res + turned * fields[1 - p]
                at = pl.ds(pl.multiple_of((2 * h + p) * PR, PR), CT)
                planes[at] = start - dt * res

    @pl.when(jnp.logical_not(has_lo))
    def _():
        own_planes(0)

    @pl.when(jnp.logical_not(has_hi))
    def _():
        own_planes(1)

    for side in range(2):
        info_copy(side).wait_recv()
        ghost_step[side] = courant / (1.0 + info[side, pl.ds(0, 2 * CX)])
        kind = info[side, pl.ds(2 * CX, 8)]
        masks = [kind == float(k) for k in range(a_theta.shape[1])]
        for v in range(V):
            for w in range(V):
                entry = jnp.zeros((8, NR), jnp.float32)
                for k, mask in enumerate(masks):
                    entry = jnp.where(mask, a_theta[v, k, w], entry)
                ghost_matrix[side, v * V + w] = entry

    def cross(b, side):
        sign = 1.0 if side == 1 else -1.0
        x = 0 if b == 0 else CX - 1
        inner = 1 if b == 0 else CX - 2
        own_edge, own_next = (CT - 1, CT - 2) if side == 1 else (0, 1)
        ghost_edge, ghost_next = (CT, CT + 1) if side == 1 else (CT + 2, CT + 3)
        kind = stagger[own_edge // CPP]
        G = 8

        def rows_of(ref, which, j):
            return [ref[which, j, pl.ds(w, G, stride=V)] for w in range(V)]

        own_u, own_in, own_first = [rows_of(crit_send, 1 - side, j) for j in range(3)]
        ghost_u, ghost_in, ghost_first = [rows_of(crit, side, j) for j in range(3)]

        def wide(row):
            return jnp.broadcast_to(row, (G, NR))

        own_dt = wide(step[pl.ds(own_edge * CX + x, 1)])
        own_in_dt = wide(step[pl.ds(own_edge * CX + inner, 1)])
        own_next_dt = wide(step[pl.ds(own_next * CX + x, 1)])
        own_sigma = wide(sigma[pl.ds(own_edge * CX + x, 1)])
        ghost_dt = wide(ghost_step[side, pl.ds(x, 1)])
        ghost_in_dt = wide(ghost_step[side, pl.ds(inner, 1)])
        ghost_next_dt = wide(ghost_step[side, pl.ds(CX + x, 1)])
        ghost_sigma = wide(info[side, pl.ds(x, 1)])

        def own_matrix(v, w):
            return a_theta[v, kind, w]

        matrix = [[ghost_matrix[side, v * V + w] for w in range(V)] for v in range(V)]

        def changes(values, matrix, sign, dt):
            return [(-0.5 * dt) * term for term in halo_terms(values, matrix, sign)]

        def other_matrix(v, w):
            return matrix[v][w]

        own_d = changes(ghost_u, own_matrix, sign, own_dt)
        own_in_d = changes(ghost_in, own_matrix, sign, own_in_dt)
        ghost_d = changes(own_u, other_matrix, -sign, ghost_dt)
        ghost_in_d = changes(own_in, other_matrix, -sign, ghost_in_dt)
        ls = [l_rows[b, w] for w in range(V)]

        def contract(weights, values):
            total = weights[0] * values[0]
            for w in range(1, V):
                total = total + weights[w] * values[w]
            return total

        def column(matrix, w):
            total = ls[0] * matrix(0, w)
            for v in range(1, V):
                total = total + ls[v] * matrix(v, w)
            return total

        own_w = [(sign * 0.5) * column(own_matrix, w) - viscosity * ls[w] for w in range(V)]
        ghost_w = [(-sign * 0.5) * column(other_matrix, w) - viscosity * ls[w] for w in range(V)]
        flip = 0.5 if b == 0 else -0.5
        near_w = [
            flip * column(lambda v, w: a_axial[v, w], w) - viscosity * ls[w] for w in range(V)
        ]
        radial_w = [column(lambda v, w: a_radial[v, w], w) for w in range(V)]
        rows = lax.broadcasted_iota(jnp.int32, (G, NR), 0)
        lanes = lax.broadcasted_iota(jnp.int32, (G, NR), 1)
        odd = rows % 2 == 1
        freq = base_frequency * (rows // 2 + 1).astype(jnp.float32)
        freq = jnp.where(odd, freq, -freq)
        left, right = lanes == 0, lanes == NR - 1

        def local(d, d_in, damping):
            radial = contract(radial_w, d)
            fields = contract(ls, d)
            swapped = jnp.where(odd, pltpu.roll(fields, 1, 0), pltpu.roll(fields, G - 1, 0))
            total = contract(near_w, d_in) + freq * swapped
            total = total + (damping + 6.0 * viscosity) * fields
            for value, weight, sign in ((radial, 0.5, -1.0), (fields, -viscosity, 1.0)):
                rm = jnp.where(left, 0.0, pltpu.roll(value, 1, 1))
                rp = jnp.where(right, 0.0, pltpu.roll(value, NR - 1, 1))
                total = total + weight * (rp + sign * rm)
            return total

        total_ghost = [a + d for a, d in zip(ghost_first, ghost_d)]
        total_own = [a + d for a, d in zip(own_first, own_d)]
        found = {
            own_next: own_next_dt * contract(own_w, own_d),
            own_edge: own_dt * (local(own_d, own_in_d, own_sigma) + contract(own_w, total_ghost)),
            ghost_edge: ghost_dt
            * (local(ghost_d, ghost_in_d, ghost_sigma) + contract(ghost_w, total_own)),
            ghost_next: ghost_next_dt * contract(ghost_w, ghost_d),
        }
        for row, value in found.items():
            at = pl.ds(row, HP, stride=PR)
            planes[at, :] = planes[at, :] - value[:HP]

    def project(b):
        for h in range(H):
            projected = dot(planes[pl.ds(2 * h * PR, 2 * PR)], phi[h])
            real, imag = projected[:PR], projected[PR:]
            weight = jnp.where(mode_plane[pl.ds(h, 1)] == b, scale, 0.0)
            part_real = jnp.sum(real * cosines[h] + imag * sines[h], axis=0, keepdims=True)
            part_imag = jnp.sum(imag * cosines[h] - real * sines[h], axis=0, keepdims=True)
            part[pl.ds(2 * h, 1)] = weight * part_real
            part[pl.ds(2 * h + 1, 1)] = weight * part_imag

    def finish_plane(b):
        @pl.when(th < T - 1)
        def _():
            crit_copy(1).wait_recv()
            cross(b, 1)

        @pl.when(th == 0)
        def _():
            crit_copy(0).wait_recv()
            cross(b, 0)

        project(b)

    @pl.when(jnp.logical_not(has_lo))
    def _():
        finish_plane(0)

    @pl.when(jnp.logical_not(has_hi))
    def _():
        finish_plane(1)

    def share(t, x):
        pltpu.make_async_remote_copy(
            src_ref=part,
            dst_ref=parts.at[me],
            send_sem=psend_sem,
            recv_sem=precv_sem,
            device_id=(t, x),
            device_id_type=MESH,
        ).start()

    for_others(share)
    parts[me] = part[...]

    for side in range(2):

        def _():
            x_copy(XU, side).wait_recv()
            x = 0 if side == 0 else CX - 1
            dt = 0.5 * step[x_rows(x), :]

            @pl.loop(0, HP)
            def _(hp):
                values = [xuhalo[side, hp * V + w] for w in range(V)]
                terms = halo_terms(
                    values, lambda v, w: a_axial[v, w], -1.0 if side == 0 else 1.0
                )
                for v in range(V):
                    at = (hp * V + v, x_rows(CX + x), slice(None))
                    first[at] = first[at] - dt * terms[v]

        when_x_source(side, _)

    def t_fix(side):
        u_copy(side).wait_recv()
        t = 0 if side == 0 else CT - 1
        kind = stagger[t // CPP]
        dt = 0.5 * step[pl.ds(t * CX, CX)]

        @pl.loop(0, HP)
        def _(hp):
            values = [uhalo[side, hp * V + w] for w in range(V)]
            terms = halo_terms(
                values, lambda v, w: a_theta[v, kind, w], -1.0 if side == 0 else 1.0
            )
            for v in range(V):
                at = (hp * V + v, pl.ds(CX + t * CX, CX))
                first[at] = first[at] - dt * terms[v]

    @pl.loop(0, CT)
    def _(i):
        t = jnp.where(i + 2 >= CT, i + 2 - CT, i + 2)

        @pl.when(i == CT - 4)
        def _():
            t_fix(1)

        @pl.when(i == CT - 2)
        def _():
            t_fix(0)

        @pl.loop(0, H)
        def _(h):
            update(first, out, 0, 1.0, t, h)

    def corner_fix(side, x_side):
        corner_copy(side, x_side).wait_recv()
        t = 0 if side == 0 else CT - 1
        x = 0 if x_side == 0 else CX - 1
        kind = stagger[t // CPP]
        line_dt = 0.5 * courant / (1.0 + xinfo[x_side, pl.ds(t, 1)])
        edge_dt = 0.5 * ghost_step[side, pl.ds(x, 1)]

        @pl.loop(0, HP)
        def _(hp):
            values = [corner[side, x_side, pl.ds(hp * V + w, 1)] for w in range(V)]
            along_t = halo_terms(
                values, lambda v, w: a_theta[v, kind, w], -1.0 if side == 0 else 1.0
            )
            along_x = halo_terms(
                values, lambda v, w: a_axial[v, w], -1.0 if x_side == 0 else 1.0
            )
            for v in range(V):
                at = (x_side, hp * V + v, pl.ds(t, 1))
                xfhalo[at] = xfhalo[at] - line_dt * along_t[v]
                at = (side, hp * V + v, pl.ds(x, 1))
                fhalo[at] = fhalo[at] - edge_dt * along_x[v]

    def x_finish(side):
        x = 0 if side == 0 else CX - 1
        ghost_dt = 0.5 * courant / (1.0 + xinfo[side])
        dt = step[x_rows(x), :]
        away = -1.0 if side == 0 else 1.0

        @pl.loop(0, HP)
        def _(hp):
            mine = [state[hp * V + w, x_rows(CX + x), :] for w in range(V)]
            terms = halo_terms(mine, lambda v, w: a_axial[v, w], -away)
            values = [xfhalo[side, hp * V + v] - ghost_dt * terms[v] for v in range(V)]
            terms = halo_terms(values, lambda v, w: a_axial[v, w], away)
            for v in range(V):
                at = (hp * V + v, x_rows(x), slice(None))
                out[at] = out[at] - dt * terms[v]

    def t_finish(side):
        t = 0 if side == 0 else CT - 1
        kind = stagger[t // CPP]
        ghost_dt = 0.5 * ghost_step[side, pl.ds(0, CX)]
        dt = step[pl.ds(t * CX, CX)]
        away = -1.0 if side == 0 else 1.0

        @pl.loop(0, HP)
        def _(hp):
            mine = [state[hp * V + w, pl.ds(CX + t * CX, CX)] for w in range(V)]
            terms = halo_terms(mine, lambda v, w: ghost_matrix[side, v * V + w], -away)
            values = [fhalo[side, hp * V + v] - ghost_dt * terms[v] for v in range(V)]
            terms = halo_terms(values, lambda v, w: a_theta[v, kind, w], away)
            for v in range(V):
                at = (hp * V + v, pl.ds(t * CX, CX))
                out[at] = out[at] - dt * terms[v]

    for x_side in range(2):

        def _():
            x_copy(XF, x_side).wait_recv()
            x_copy(XINFO, x_side).wait_recv()

        when_x_source(x_side, _)
    for side in (1, 0):
        first_copy(side).wait_recv()
        for x_side in range(2):
            when_x_source(x_side, lambda: corner_fix(side, x_side))
        t_finish(side)
    for x_side in range(2):
        when_x_source(x_side, lambda: x_finish(x_side))

    everyone = pltpu.make_async_remote_copy(
        src_ref=parts.at[pl.ds(0, N - 1)],
        dst_ref=parts.at[pl.ds(0, N - 1)],
        send_sem=psend_sem,
        recv_sem=precv_sem,
        device_id=(up, xr),
        device_id_type=MESH,
    )
    everyone.wait_recv()
    total = parts[0]
    if N <= 64:
        for i in range(1, N):
            total = total + parts[i]
    else:
        total = lax.fori_loop(1, N, lambda i, acc: acc + parts[i], total)
    part_rows = [total[i : i + 1] for i in range(2 * H)]
    for h in range(H):
        for b in range(2):
            mine = mode_plane[pl.ds(h, 1)] == b
            for p in range(2):
                amps[h, b, pl.ds(p, 1)] = jnp.where(mine, part_rows[2 * h + p], 0.0)

    def correct(b, h):
        x = 0 if b == 0 else CX - 1
        weight = jnp.where(mode_plane[pl.ds(h, 1)] == b, scale, 0.0)
        real = weight * (part_rows[2 * h] - gust[h, pl.ds(0, 1)])
        imag = weight * (part_rows[2 * h + 1] - gust[h, pl.ds(1, 1)])
        cos, sin = cosines[h, pl.ds(0, CT)], sines[h, pl.ds(0, CT)]
        coef = jnp.concatenate(
            [real * cos - imag * sin, real * sin + imag * cos], axis=0
        )
        q = dot(coef, phi[h], (((1,), (1,)), ((), ())))
        for p in range(2):
            for v in range(V):
                at = (h * F + p * V + v, x_rows(x), slice(None))
                out[at] = out[at] - r_cols[b, v] * q[p * CT : (p + 1) * CT]

    @pl.when(jnp.logical_not(has_lo))
    def _():
        for h in range(H):
            correct(0, h)

    @pl.when(jnp.logical_not(has_hi))
    def _():
        for h in range(H):
            correct(1, h)

    everyone.wait_send()

    @pl.when(on_plane & (th > 0))
    def _():
        crit_copy(1).wait_send()

    @pl.when(on_plane & (th == T - 1))
    def _():
        crit_copy(0).wait_send()

    for side in range(2):
        info_copy(side).wait_send()
        u_copy(side).wait_send()
        first_copy(side).wait_send()

        def _():
            for kind in (XU, XF, XINFO):
                x_copy(kind, side).wait_send()
            for t_side in range(2):
                corner_copy(t_side, side).wait_send()

        when_x_target(side, _)


def store_kernel(fields, amps, fields_out, amps_out, sems):
    copies = [
        pltpu.make_async_copy(fields, fields_out, sems.at[0]),
        pltpu.make_async_copy(amps, amps_out, sems.at[1]),
    ]
    for copy in copies:
        copy.start()
    for copy in copies:
        copy.wait()


def store(fields, amps):
    vmem = pl.BlockSpec(memory_space=pl.ANY)
    hbm = pl.BlockSpec(memory_space=pltpu.HBM)
    return pl.pallas_call(
        store_kernel,
        out_shape=tuple(jax.ShapeDtypeStruct(a.shape, a.dtype) for a in (fields, amps)),
        in_specs=(vmem, vmem),
        out_specs=(hbm, hbm),
        compiler_params=pltpu.CompilerParams(vmem_limit_bytes=2**20),
        scratch_shapes=[pltpu.SemaphoreType.DMA((2,))],
        name="store",
    )(fields, amps)


def local(T, X, *args):
    state, source, sigma, stagger = args[:4]
    H, two, V, CT, CX, NR = state.shape
    F = two * V
    HF = H * F
    NMODE = args[7].shape[1]
    dims = (T, X, H, V, CT, CX, NR, stagger.shape[0], NMODE)
    N = T * X
    rows = CT * CX
    f32 = jnp.float32
    hbm = pl.BlockSpec(memory_space=pl.ANY)
    vmem = pl.BlockSpec(memory_space=pltpu.VMEM)
    DMA = pltpu.SemaphoreType.DMA
    stagger, a_theta, a_axial, a_radial, orders, radial, planes, gust, l_rows, r_cols = args[3:]
    small = [stagger, jnp.swapaxes(a_theta, 0, 1), a_axial, a_radial, l_rows, r_cols]
    small += [orders, radial, planes, gust]
    pad = -(-2 * H // 8) * 8
    sides = [
        (HF, CX, NR),
        (HF, CX, NR),
        (HF, CX, NR),
        (HF, CT, NR),
        (HF, CT, NR),
        (HF, CT, NR),
        (HF, CT, NR),
        (CT, NR),
        (CT, NR),
        (2, -(-HF // 8) * 8, NR),
        (2, -(-HF // 8) * 8, NR),
        (3, 8 * V, NR),
        (3, 8 * V, NR),
        (2 * CX + 8, NR),
        (2 * CX + 8, NR),
        (2 * CX, NR),
        (V * V, 8, NR),
    ]
    fields, amplitudes = pl.pallas_call(
        functools.partial(kernel, dims),
        out_shape=(
            jax.ShapeDtypeStruct((HF, rows, NR), f32),
            jax.ShapeDtypeStruct((H, 2, 2, NMODE), f32),
        ),
        in_specs=[hbm] * 13,
        out_specs=(vmem, vmem),
        scratch_shapes=[pltpu.SMEM(a.shape, a.dtype) for a in small[:6]]
        + [pltpu.VMEM(a.shape, a.dtype) for a in small[6:]]
        + [
            pltpu.VMEM((HF, rows + 2 * CX, NR), f32),
            pltpu.VMEM((HF, rows, NR), f32),
            pltpu.VMEM((rows, NR), f32),
            pltpu.VMEM((HF, rows + 2 * CX, NR), f32),
            pltpu.VMEM((rows, NR), f32),
        ]
        + [pltpu.VMEM((2, *shape), f32) for shape in sides]
        + [
            pltpu.VMEM((2 * H * 2 * CT, NR), f32),
            pltpu.VMEM((H, NR, NMODE), f32),
            pltpu.VMEM((H, 2 * CT, NMODE), f32),
            pltpu.VMEM((H, 2 * CT, NMODE), f32),
            pltpu.VMEM((pad, NMODE), f32),
            pltpu.VMEM((N, pad, NMODE), f32),
            DMA((3,)),
            DMA((10,)),
            DMA((7, 2)),
            DMA((7, 2)),
            DMA((2, 2)),
            DMA((2, 2)),
            DMA,
            DMA,
        ],
        compiler_params=pltpu.CompilerParams(
            collective_id=0, has_side_effects=True, vmem_limit_bytes=16 * 2**20
        ),
        name="wake",
    )(
        *(pltpu.with_memory_space_constraint(a, pltpu.HBM) for a in (state.reshape(HF, rows, NR),
        source.reshape(HF, rows, NR),
        sigma.reshape(rows, NR),
        *small)),
    )
    fields, amplitudes = store(fields, amplitudes)
    return fields.reshape(state.shape), amplitudes


def solution(mesh):
    field = P(None, None, None, "theta", "xr", None)
    placed = (field, field, P("theta", "xr", None), P("theta")) + (P(),) * 9
    return jax.shard_map(
        functools.partial(local, mesh.shape["theta"], mesh.shape["xr"]),
        mesh=mesh,
        in_specs=placed,
        out_specs=(field, P()),
        check_vma=False,
    )
```

```python
import functools
import math

import jax
import jax.numpy as jnp
from jax import lax
from jax.experimental import pallas as pl
from jax.experimental.pallas import tpu as pltpu
from jax.sharding import PartitionSpec as P

courant = 0.5
viscosity = 0.1
base_frequency = 0.5
highest = lax.Precision.HIGHEST
MESH = pl.DeviceIdType.MESH


def kernel(
    dims,
    state_hbm,
    source_hbm,
    sigma_hbm,
    *refs,
):
    small_hbm, refs = refs[:10], refs[10:]
    out, amps, refs = refs[0], refs[1], refs[2:]
    small, refs = refs[:10], refs[10:]
    stagger, a_theta, a_axial, a_radial, l_rows, r_cols = small[:6]
    mode_order, mode_radial, mode_plane, gust = small[6:]
    (
        state,
        source,
        sigma,
        first,
        step,
        uhalo,
        fhalo,
        fsend,
        xuhalo,
        xusend,
        xfhalo,
        xfsend,
        xinfo,
        xinfo_send,
        corner,
        corner_send,
        crit,
        crit_send,
        info,
        info_send,
        ghost_step,
        ghost_matrix,
        planes,
        phi,
        cosines,
        sines,
        part,
        parts,
        load_sem,
        small_sem,
        send_sem,
        recv_sem,
        csend_sem,
        crecv_sem,
        psend_sem,
        precv_sem,
        whole,
        wsend_sem,
        wrecv_sem,
    ) = refs
    T, X, H, V, CT, CX, NR, NPASS, NMODE = dims
    F = 2 * V
    HF = H * F
    CPP = CT // NPASS
    N = T * X
    HP = 2 * H
    PR = 2 * CT
    th = lax.axis_index("theta")
    xr = lax.axis_index("xr")
    me = th * X + xr
    up = lax.rem(th + 1, T)
    down = lax.rem(th + T - 1, T)
    has_lo = xr > 0
    has_hi = xr < X - 1
    on_plane = jnp.logical_not(has_lo & has_hi)
    total_theta = CT * T
    scale = 1.0 / math.sqrt(total_theta * NR)
    U, FIRST, INFO, CRIT, XU, XF, XINFO = range(7)

    barrier = pltpu.get_barrier_semaphore()

    Q = T // 4
    ROOTS = 2 * Q
    is_root = th < ROOTS

    def for_others(count, act):
        def ring(t):
            for x in range(X):

                @pl.when((t != th) | (x != xr))
                def _():
                    act(t, x)

        if count * X <= 64:
            for t in range(count):
                ring(t)
        else:
            pl.loop(0, count)(ring)

    def greet(t, x):
        pl.semaphore_signal(barrier, inc=1, device_id=(t, x), device_id_type=MESH)

    def greet_all():
        greeters = ROOTS * X - is_root.astype(jnp.int32)
        for dt in (-1, 0, 1):
            for dx in (-1, 0, 1):
                t, x = th + dt, xr + dx
                inside = (t >= 0) & (t < T) & (x >= 0) & (x < X)
                if dt or dx:
                    greeters += (inside & (t >= ROOTS)).astype(jnp.int32)
                    pl.when(inside & jnp.logical_not(is_root))(lambda: greet(t, x))

        @pl.when(is_root)
        def _():
            for_others(T, greet)

        return greeters

    little = [
        pltpu.make_async_copy(src, dst, small_sem.at[i])
        for i, (src, dst) in enumerate(zip(small_hbm, small))
    ]
    loads = [
        pltpu.make_async_copy(state_hbm, state.at[:, pl.ds(CX, CT * CX)], load_sem.at[0]),
        pltpu.make_async_copy(sigma_hbm, sigma, load_sem.at[1]),
        pltpu.make_async_copy(source_hbm, source, load_sem.at[2]),
    ]
    for copy in loads + little:
        copy.start()
    greeters = greet_all()

    zero = jnp.zeros((HF, CX, NR), jnp.float32)
    for buf in (state, first):
        buf[:, pl.ds(0, CX)] = zero
        buf[:, pl.ds(CX + CT * CX, CX)] = zero
    planes[...] = jnp.zeros_like(planes)
    part[...] = jnp.zeros_like(part)
    crit_rows = -(-HF // 8) * 8
    crit_send[...] = jnp.zeros_like(crit_send)
    if crit.shape[2] > crit_rows:
        rest = crit.shape[2] - crit_rows
        crit[:, :, pl.ds(crit_rows, rest)] = jnp.zeros((2, 3, rest, NR), jnp.float32)

    def x_rows(row):
        return pl.ds(row, CT, stride=CX)

    def neighbour(side):
        return (up if side == 0 else down, xr)

    def message(kind, side, src, dst, target):
        return pltpu.make_async_remote_copy(
            src_ref=src,
            dst_ref=dst,
            send_sem=send_sem.at[kind, side],
            recv_sem=recv_sem.at[kind, side],
            device_id=target,
            device_id_type=MESH,
        )

    def u_copy(side):
        rows = pl.ds(CX + ((CT - 1) * CX if side == 0 else 0), CX)
        return message(U, side, state.at[:, rows], uhalo.at[side], neighbour(side))

    def first_copy(side):
        return message(FIRST, side, fsend.at[side], fhalo.at[side], neighbour(side))

    def info_copy(side):
        return message(INFO, side, info_send.at[side], info.at[side], neighbour(side))

    def crit_copy(side):
        rows = pl.ds(0, crit_rows)
        return message(
            CRIT, side, crit_send.at[side, :, rows], crit.at[side, :, rows], neighbour(side)
        )

    def x_neighbour(side):
        return (th, xr + 1 if side == 0 else xr - 1)

    def x_copy(kind, side):
        src, dst = {
            XU: (xusend, xuhalo),
            XF: (xfsend, xfhalo),
            XINFO: (xinfo_send, xinfo),
        }[kind]
        return message(kind, side, src.at[side], dst.at[side], x_neighbour(side))

    def corner_copy(side, x_side):
        return pltpu.make_async_remote_copy(
            src_ref=corner_send.at[side, x_side],
            dst_ref=corner.at[side, x_side],
            send_sem=csend_sem.at[side, x_side],
            recv_sem=crecv_sem.at[side, x_side],
            device_id=(up if side == 0 else down, xr + 1 if x_side == 0 else xr - 1),
            device_id_type=MESH,
        )

    def when_x_target(side, act):
        pl.when(has_hi if side == 0 else has_lo)(act)

    def when_x_source(side, act):
        pl.when(has_lo if side == 0 else has_hi)(act)

    row_id = lax.broadcasted_iota(jnp.int32, (CX, NR), 0)
    lane_id = lax.broadcasted_iota(jnp.int32, (CX, NR), 1)
    first_row = row_id == 0
    last_row = row_id == CX - 1
    first_lane = lane_id == 0
    last_lane = lane_id == NR - 1

    BLOCK = 2
    SPAN = 128
    cells = lax.broadcasted_iota(jnp.int32, (PR, SPAN), 0)
    cells = th * CT + jnp.where(cells >= CT + 2, CT + 1 - cells, cells)
    orders = lax.broadcasted_iota(jnp.int32, (PR, SPAN), 1) - SPAN // 2
    turns = (orders * cells).astype(jnp.float32)
    turns = turns - jnp.floor(turns / total_theta) * total_theta
    angle = (2.0 * math.pi) * turns / total_theta
    cos_table = jnp.cos(angle)
    sin_table = jnp.sin(angle)
    radial = lax.broadcasted_iota(jnp.int32, (8, NR), 0)
    radial_pos = lax.broadcasted_iota(jnp.int32, (8, NR), 1).astype(jnp.float32) + 0.5
    phi_table = jnp.where(
        radial == 0,
        1.0,
        math.sqrt(2.0) * jnp.cos(math.pi * radial.astype(jnp.float32) * radial_pos / NR),
    )

    def dot(a, b, dims=(((1,), (0,)), ((), ()))):
        return lax.dot_general(
            a, b, dims, precision=highest, preferred_element_type=jnp.float32
        )

    for copy in little:
        copy.wait()
    order_id = lax.broadcasted_iota(jnp.int32, (SPAN, NMODE), 0) - SPAN // 2
    radial_id = lax.broadcasted_iota(jnp.int32, (8, NMODE), 0)
    for h in range(H):
        chosen = (mode_order[pl.ds(h, 1)] == order_id).astype(jnp.float32)
        cosines[h] = dot(cos_table, chosen)
        sines[h] = dot(sin_table, chosen)
        chosen = (mode_radial[pl.ds(h, 1)] == radial_id).astype(jnp.float32)
        phi[h] = dot(phi_table, chosen, (((0,), (0,)), ((), ())))

    loads[1].wait()
    step[...] = courant / (1.0 + sigma[...])
    for side in range(2):
        edge, second = (CT - 1, CT - 2) if side == 0 else (0, 1)
        info_send[side, pl.ds(0, CX)] = sigma[pl.ds(edge * CX, CX)]
        info_send[side, pl.ds(CX, CX)] = sigma[pl.ds(second * CX, CX)]
        kind = stagger[NPASS - 1 if side == 0 else 0].astype(jnp.float32)
        info_send[side, pl.ds(2 * CX, 8)] = jnp.full((8, NR), kind, jnp.float32)
    loads[0].wait()
    loads[2].wait()

    def update(field, result, result_offset, factor, t, h):
        freq = base_frequency * (h + 1).astype(jnp.float32)
        bases = [pl.multiple_of((t + j) * CX, CX) for j in range(BLOCK)]
        kind = stagger[t // CPP]
        damps = [2.0 * sigma[pl.ds(base, CX)] + 12.0 * viscosity for base in bases]
        groups = [(j, p) for j in range(BLOCK) for p in range(2)]
        flux = {g: [None] * V for g in groups}
        for w in range(V):
            values = {}
            for j, p in groups:
                f = h * F + p * V + w
                u, tm, tp = [field[f, pl.ds(bases[j] + k * CX, CX)] for k in (1, 0, 2)]
                xm = jnp.where(first_row, 0.0, pltpu.roll(u, 1, 0))
                xp = jnp.where(last_row, 0.0, pltpu.roll(u, CX - 1, 0))
                rm = jnp.where(first_lane, 0.0, pltpu.roll(u, 1, 1))
                rp = jnp.where(last_lane, 0.0, pltpu.roll(u, NR - 1, 1))
                sums = ((tp + tm) + (xp + xm)) + (rp + rm)
                values[j, p] = (u, tp - tm, xp - xm, rp - rm, sums)
            for v in range(V):
                at, ax, ar = a_theta[v, kind, w], a_axial[v, w], a_radial[v, w]
                for j, p in groups:
                    u, dth, dx, dr, sums = values[j, p]
                    term = at * dth + ax * dx + ar * dr
                    if v == w:
                        turned = 2.0 * freq if p == 1 else -2.0 * freq
                        term = term + (damps[j] * u - (2.0 * viscosity) * sums)
                        term = term + turned * values[j, 1 - p][0]
                    old = flux[j, p][v]
                    flux[j, p][v] = term if old is None else old + term
        for j, p in groups:
            dt = factor * step[pl.ds(bases[j], CX)]
            half = 0.5 * dt
            for v in range(V):
                f = h * F + p * V + v
                start = state[f, pl.ds(bases[j] + CX, CX)] + dt * source[f, pl.ds(bases[j], CX)]
                result[f, pl.ds(bases[j] + result_offset, CX)] = start - half * flux[j, p][v]

    def halo_terms(values, matrix, sign):
        terms = []
        for v in range(V):
            total = matrix(v, 0) * values[0]
            for w in range(1, V):
                total = total + matrix(v, w) * values[w]
            terms.append((sign * 0.5) * total - viscosity * values[v])
        return terms

    def pack_crit(side):
        t = CT - 1 if side == 0 else 0

        def pack(x, inner):
            for f in range(HF):
                at = pl.ds(f, 1)
                crit_send[side, 0, at] = state[f, pl.ds(CX + t * CX + x, 1)]
                crit_send[side, 1, at] = state[f, pl.ds(CX + t * CX + inner, 1)]
                crit_send[side, 2, at] = first[f, pl.ds(CX + t * CX + x, 1)]

        @pl.when(jnp.logical_not(has_lo))
        def _():
            pack(0, 1)

        @pl.when(jnp.logical_not(has_hi))
        def _():
            pack(CX - 1, CX - 2)

    def open_sends():
        pl.semaphore_wait(barrier, greeters)
        info_copy(0).start()

        @pl.when(th > 0)
        def _():
            info_copy(1).start()

        for side in range(2):

            def _():
                x = CX - 1 if side == 0 else 0
                for f in range(HF):
                    xusend[side, f] = state[f, x_rows(CX + x), :]
                xinfo_send[side] = sigma[x_rows(x), :]
                x_copy(XU, side).start()
                x_copy(XINFO, side).start()

            when_x_target(side, _)

    def low_sends():
        @pl.when(on_plane & (th > 0))
        def _():
            pack_crit(1)
            crit_copy(1).start()

        @pl.when(th > 0)
        def _():
            u_copy(1).start()

        u_copy(0).start()

    def edge_sends():
        pack_crit(0)

        @pl.when(on_plane & (th == 0))
        def _():
            pack_crit(1)

        @pl.when(on_plane & (th == T - 1))
        def _():
            crit_copy(0).start()

        for side in range(2):
            rows = pl.ds(CX + ((CT - 1) * CX if side == 0 else 0), CX)
            fsend[side] = first[:, rows]
        first_copy(0).start()

        @pl.when(th > 0)
        def _():
            first_copy(1).start()

        for side in range(2):

            def _():
                x = CX - 1 if side == 0 else 0
                for t_side in range(2):
                    row = CX + ((CT - 1) * CX if t_side == 0 else 0) + x
                    for f in range(HF):
                        corner_send[t_side, side, pl.ds(f, 1)] = state[f, pl.ds(row, 1)]
                corner_copy(0, side).start()

                @pl.when(th > 0)
                def _():
                    corner_copy(1, side).start()

            when_x_target(side, _)

    open_sends()
    blocks = CT // BLOCK

    @pl.loop(0, blocks)
    def _(i):
        t = BLOCK * jnp.where(i == 0, 0, jnp.where(i == 1, blocks - 1, i - 1))

        @pl.loop(0, H)
        def _(h):
            update(state, first, CX, 0.5, t, h)

        pl.when(i == 0)(low_sends)
        pl.when(i == 1)(edge_sends)

    for side in range(2):

        def _():
            x = CX - 1 if side == 0 else 0
            for f in range(HF):
                xfsend[side, f] = first[f, x_rows(CX + x), :]
            x_copy(XF, side).start()

        when_x_target(side, _)

    def own_planes(b):
        x = 0 if b == 0 else CX - 1
        inner = 1 if b == 0 else CX - 2
        lines = lax.broadcasted_iota(jnp.int32, (CT, NR), 0)
        lanes = lax.broadcasted_iota(jnp.int32, (CT, NR), 1)
        top, bottom = lines == 0, lines == CT - 1
        left, right = lanes == 0, lanes == NR - 1
        ls, gxs, grs, gts = [], [], [], []
        for w in range(V):
            ls.append(l_rows[b, w])
            gx = gr = 0.0
            for v in range(V):
                gx = gx + l_rows[b, v] * a_axial[v, w]
                gr = gr + l_rows[b, v] * a_radial[v, w]
            gt = None
            for k in range(NPASS):
                row = 0.0
                for v in range(V):
                    row = row + l_rows[b, v] * a_theta[v, stagger[k], w]
                gt = row if gt is None else jnp.where(lines >= k * CPP, row, gt)
            gxs.append(gx)
            grs.append(gr)
            gts.append(gt)
        damp = sigma[x_rows(x), :] + 6.0 * viscosity
        dt = step[x_rows(x), :]

        @pl.loop(0, H)
        def _(h):
            freq = base_frequency * (h + 1).astype(jnp.float32)
            fields = [0.0, 0.0]
            rest = []
            for p in range(2):
                along_t = start = forcing = inside = radial = 0.0
                flux = sums = 0.0
                for w in range(V):
                    f = h * F + p * V + w
                    u = first[f, x_rows(CX + x), :]
                    near = first[f, x_rows(CX + inner), :]
                    tm = jnp.where(top, 0.0, pltpu.roll(u, 1, 0))
                    tp = jnp.where(bottom, 0.0, pltpu.roll(u, CT - 1, 0))
                    dx = near if b == 0 else -near
                    flux = flux + (gts[w] * (tp - tm) + gxs[w] * dx)
                    sums = sums + ls[w] * ((tp + tm) + near)
                    fields[p] = fields[p] + ls[w] * u
                    radial = radial + grs[w] * u
                    forcing = forcing + ls[w] * source[f, x_rows(x), :]
                    start = start + ls[w] * state[f, x_rows(CX + x), :]
                for value, weight, sign in ((radial, 0.5, -1.0), (fields[p], -viscosity, 1.0)):
                    rm = jnp.where(left, 0.0, pltpu.roll(value, 1, 1))
                    rp = jnp.where(right, 0.0, pltpu.roll(value, NR - 1, 1))
                    inside = inside + weight * (rp + sign * rm)
                res = 0.5 * flux - viscosity * sums + inside + damp * fields[p] - forcing
                rest.append((start, res))
            for p in range(2):
                start, res = rest[p]
                turned = -freq if p == 0 else freq
                res = res + turned * fields[1 - p]
                at = pl.ds(pl.multiple_of((2 * h + p) * PR, PR), CT)
                planes[at] = start - dt * res

    @pl.when(jnp.logical_not(has_lo))
    def _():
        own_planes(0)

    @pl.when(jnp.logical_not(has_hi))
    def _():
        own_planes(1)

    def ghosts(side):
        info_copy(side).wait_recv()
        ghost_step[side] = courant / (1.0 + info[side, pl.ds(0, 2 * CX)])
        kind = info[side, pl.ds(2 * CX, 8)]
        masks = [kind == float(k) for k in range(a_theta.shape[1])]
        for v in range(V):
            for w in range(V):
                entry = jnp.zeros((8, NR), jnp.float32)
                for k, mask in enumerate(masks):
                    entry = jnp.where(mask, a_theta[v, k, w], entry)
                ghost_matrix[side, v * V + w] = entry

    def crossed(side):
        return ((side == 1) & (th < T - 1)) | ((side == 0) & (th == 0))

    for side in (1, 0):
        pl.when(crossed(side))(lambda: ghosts(side))

    @pl.when(th == 0)
    def _():
        info_copy(1).start()
        u_copy(1).start()
        first_copy(1).start()
        for side in range(2):
            when_x_target(side, lambda: corner_copy(1, side).start())

    def cross(b, side):
        sign = 1.0 if side == 1 else -1.0
        x = 0 if b == 0 else CX - 1
        inner = 1 if b == 0 else CX - 2
        own_edge, own_next = (CT - 1, CT - 2) if side == 1 else (0, 1)
        ghost_edge, ghost_next = (CT, CT + 1) if side == 1 else (CT + 2, CT + 3)
        kind = stagger[own_edge // CPP]
        G = 8

        def rows_of(ref, which, j):
            return [ref[which, j, pl.ds(w, G, stride=V)] for w in range(V)]

        own_u, own_in, own_first = [rows_of(crit_send, 1 - side, j) for j in range(3)]
        ghost_u, ghost_in, ghost_first = [rows_of(crit, side, j) for j in range(3)]

        def wide(row):
            return jnp.broadcast_to(row, (G, NR))

        own_dt = wide(step[pl.ds(own_edge * CX + x, 1)])
        own_in_dt = wide(step[pl.ds(own_edge * CX + inner, 1)])
        own_next_dt = wide(step[pl.ds(own_next * CX + x, 1)])
        own_sigma = wide(sigma[pl.ds(own_edge * CX + x, 1)])
        ghost_dt = wide(ghost_step[side, pl.ds(x, 1)])
        ghost_in_dt = wide(ghost_step[side, pl.ds(inner, 1)])
        ghost_next_dt = wide(ghost_step[side, pl.ds(CX + x, 1)])
        ghost_sigma = wide(info[side, pl.ds(x, 1)])

        def own_matrix(v, w):
            return a_theta[v, kind, w]

        matrix = [[ghost_matrix[side, v * V + w] for w in range(V)] for v in range(V)]

        def changes(values, matrix, sign, dt):
            return [(-0.5 * dt) * term for term in halo_terms(values, matrix, sign)]

        def other_matrix(v, w):
            return matrix[v][w]

        own_d = changes(ghost_u, own_matrix, sign, own_dt)
        own_in_d = changes(ghost_in, own_matrix, sign, own_in_dt)
        ghost_d = changes(own_u, other_matrix, -sign, ghost_dt)
        ghost_in_d = changes(own_in, other_matrix, -sign, ghost_in_dt)
        ls = [l_rows[b, w] for w in range(V)]

        def contract(weights, values):
            total = weights[0] * values[0]
            for w in range(1, V):
                total = total + weights[w] * values[w]
            return total

        def column(matrix, w):
            total = ls[0] * matrix(0, w)
            for v in range(1, V):
                total = total + ls[v] * matrix(v, w)
            return total

        own_w = [(sign * 0.5) * column(own_matrix, w) - viscosity * ls[w] for w in range(V)]
        ghost_w = [(-sign * 0.5) * column(other_matrix, w) - viscosity * ls[w] for w in range(V)]
        flip = 0.5 if b == 0 else -0.5
        near_w = [
            flip * column(lambda v, w: a_axial[v, w], w) - viscosity * ls[w] for w in range(V)
        ]
        radial_w = [column(lambda v, w: a_radial[v, w], w) for w in range(V)]
        rows = lax.broadcasted_iota(jnp.int32, (G, NR), 0)
        lanes = lax.broadcasted_iota(jnp.int32, (G, NR), 1)
        odd = rows % 2 == 1
        freq = base_frequency * (rows // 2 + 1).astype(jnp.float32)
        freq = jnp.where(odd, freq, -freq)
        left, right = lanes == 0, lanes == NR - 1

        def local(d, d_in, damping):
            radial = contract(radial_w, d)
            fields = contract(ls, d)
            swapped = jnp.where(odd, pltpu.roll(fields, 1, 0), pltpu.roll(fields, G - 1, 0))
            total = contract(near_w, d_in) + freq * swapped
            total = total + (damping + 6.0 * viscosity) * fields
            for value, weight, sign in ((radial, 0.5, -1.0), (fields, -viscosity, 1.0)):
                rm = jnp.where(left, 0.0, pltpu.roll(value, 1, 1))
                rp = jnp.where(right, 0.0, pltpu.roll(value, NR - 1, 1))
                total = total + weight * (rp + sign * rm)
            return total

        total_ghost = [a + d for a, d in zip(ghost_first, ghost_d)]
        total_own = [a + d for a, d in zip(own_first, own_d)]
        found = {
            own_next: own_next_dt * contract(own_w, own_d),
            own_edge: own_dt * (local(own_d, own_in_d, own_sigma) + contract(own_w, total_ghost)),
            ghost_edge: ghost_dt
            * (local(ghost_d, ghost_in_d, ghost_sigma) + contract(ghost_w, total_own)),
            ghost_next: ghost_next_dt * contract(ghost_w, ghost_d),
        }
        for row, value in found.items():
            at = pl.ds(row, HP, stride=PR)
            planes[at, :] = planes[at, :] - value[:HP]

    def project(b):
        for h in range(H):
            projected = dot(planes[pl.ds(2 * h * PR, 2 * PR)], phi[h])
            real, imag = projected[:PR], projected[PR:]
            weight = jnp.where(mode_plane[pl.ds(h, 1)] == b, scale, 0.0)
            part_real = jnp.sum(real * cosines[h] + imag * sines[h], axis=0, keepdims=True)
            part_imag = jnp.sum(imag * cosines[h] - real * sines[h], axis=0, keepdims=True)
            part[pl.ds(2 * h, 1)] = weight * part_real
            part[pl.ds(2 * h + 1, 1)] = weight * part_imag

    def finish_plane(b):
        @pl.when(th < T - 1)
        def _():
            crit_copy(1).wait_recv()
            cross(b, 1)

        @pl.when(th == 0)
        def _():
            crit_copy(0).wait_recv()
            cross(b, 0)

        project(b)

    @pl.when(jnp.logical_not(has_lo))
    def _():
        finish_plane(0)

    @pl.when(jnp.logical_not(has_hi))
    def _():
        finish_plane(1)

    def share(t, x):
        pltpu.make_async_remote_copy(
            src_ref=part.at[pl.ds(0, HP)],
            dst_ref=parts.at[me, pl.ds(0, HP)],
            send_sem=psend_sem,
            recv_sem=precv_sem,
            device_id=(t, x),
            device_id_type=MESH,
        ).start()

    for_others(ROOTS, share)
    parts[me] = part[...]
    for side in (0, 1):
        pl.when(jnp.logical_not(crossed(side)))(lambda: ghosts(side))

    for side in range(2):

        def _():
            x_copy(XU, side).wait_recv()
            x = 0 if side == 0 else CX - 1
            dt = 0.5 * step[x_rows(x), :]

            @pl.loop(0, HP)
            def _(hp):
                values = [xuhalo[side, hp * V + w] for w in range(V)]
                terms = halo_terms(
                    values, lambda v, w: a_axial[v, w], -1.0 if side == 0 else 1.0
                )
                for v in range(V):
                    at = (hp * V + v, x_rows(CX + x), slice(None))
                    first[at] = first[at] - dt * terms[v]

        when_x_source(side, _)

    def t_fix(side):
        u_copy(side).wait_recv()
        t = 0 if side == 0 else CT - 1
        kind = stagger[t // CPP]
        dt = 0.5 * step[pl.ds(t * CX, CX)]

        @pl.loop(0, HP)
        def _(hp):
            values = [uhalo[side, hp * V + w] for w in range(V)]
            terms = halo_terms(
                values, lambda v, w: a_theta[v, kind, w], -1.0 if side == 0 else 1.0
            )
            for v in range(V):
                at = (hp * V + v, pl.ds(CX + t * CX, CX))
                first[at] = first[at] - dt * terms[v]

    @pl.loop(0, blocks)
    def _(i):
        t = BLOCK * jnp.where(i + 1 >= blocks, i + 1 - blocks, i + 1)

        @pl.when(i == blocks - 2)
        def _():
            t_fix(1)

        @pl.when(i == blocks - 1)
        def _():
            t_fix(0)

        @pl.loop(0, H)
        def _(h):
            update(first, out, 0, 1.0, t, h)

    def corner_fix(side, x_side):
        corner_copy(side, x_side).wait_recv()
        t = 0 if side == 0 else CT - 1
        x = 0 if x_side == 0 else CX - 1
        kind = stagger[t // CPP]
        line_dt = 0.5 * courant / (1.0 + xinfo[x_side, pl.ds(t, 1)])
        edge_dt = 0.5 * ghost_step[side, pl.ds(x, 1)]

        @pl.loop(0, HP)
        def _(hp):
            values = [corner[side, x_side, pl.ds(hp * V + w, 1)] for w in range(V)]
            along_t = halo_terms(
                values, lambda v, w: a_theta[v, kind, w], -1.0 if side == 0 else 1.0
            )
            along_x = halo_terms(
                values, lambda v, w: a_axial[v, w], -1.0 if x_side == 0 else 1.0
            )
            for v in range(V):
                at = (x_side, hp * V + v, pl.ds(t, 1))
                xfhalo[at] = xfhalo[at] - line_dt * along_t[v]
                at = (side, hp * V + v, pl.ds(x, 1))
                fhalo[at] = fhalo[at] - edge_dt * along_x[v]

    def x_finish(side):
        x = 0 if side == 0 else CX - 1
        ghost_dt = 0.5 * courant / (1.0 + xinfo[side])
        dt = step[x_rows(x), :]
        away = -1.0 if side == 0 else 1.0

        @pl.loop(0, HP)
        def _(hp):
            mine = [state[hp * V + w, x_rows(CX + x), :] for w in range(V)]
            terms = halo_terms(mine, lambda v, w: a_axial[v, w], -away)
            values = [xfhalo[side, hp * V + v] - ghost_dt * terms[v] for v in range(V)]
            terms = halo_terms(values, lambda v, w: a_axial[v, w], away)
            for v in range(V):
                at = (hp * V + v, x_rows(x), slice(None))
                out[at] = out[at] - dt * terms[v]

    def t_finish(side):
        t = 0 if side == 0 else CT - 1
        kind = stagger[t // CPP]
        ghost_dt = 0.5 * ghost_step[side, pl.ds(0, CX)]
        dt = step[pl.ds(t * CX, CX)]
        away = -1.0 if side == 0 else 1.0

        @pl.loop(0, HP)
        def _(hp):
            mine = [state[hp * V + w, pl.ds(CX + t * CX, CX)] for w in range(V)]
            terms = halo_terms(mine, lambda v, w: ghost_matrix[side, v * V + w], -away)
            values = [fhalo[side, hp * V + v] - ghost_dt * terms[v] for v in range(V)]
            terms = halo_terms(values, lambda v, w: a_theta[v, kind, w], away)
            for v in range(V):
                at = (hp * V + v, pl.ds(t * CX, CX))
                out[at] = out[at] - dt * terms[v]

    for x_side in range(2):

        def _():
            x_copy(XF, x_side).wait_recv()
            x_copy(XINFO, x_side).wait_recv()

        when_x_source(x_side, _)
    for side in (1, 0):
        first_copy(side).wait_recv()
        for x_side in range(2):
            when_x_source(x_side, lambda: corner_fix(side, x_side))
        t_finish(side)
    for x_side in range(2):
        when_x_source(x_side, lambda: x_finish(x_side))

    def shares(count):
        return pltpu.make_async_remote_copy(
            src_ref=parts.at[pl.ds(0, count), pl.ds(0, HP)],
            dst_ref=parts.at[pl.ds(0, count), pl.ds(0, HP)],
            send_sem=psend_sem,
            recv_sem=precv_sem,
            device_id=(up, xr),
            device_id_type=MESH,
        )

    def total_copy(j):
        return pltpu.make_async_remote_copy(
            src_ref=whole,
            dst_ref=whole,
            send_sem=wsend_sem.at[j],
            recv_sem=wrecv_sem,
            device_id=(th + Q + j * Q, xr),
            device_id_type=MESH,
        )

    serves = (th >= Q) & (th < 2 * Q)

    @pl.when(is_root)
    def _():
        shares(N - 1).wait_recv()
        total = parts[0]
        if N <= 64:
            for i in range(1, N):
                total = total + parts[i]
        else:
            total = lax.fori_loop(1, N, lambda i, acc: acc + parts[i], total)
        whole[...] = total

        @pl.when(serves)
        def _():
            for j in range(2):
                total_copy(j).start()

    @pl.when(jnp.logical_not(is_root))
    def _():
        total_copy(0).wait_recv()

    total = whole[...]
    part_rows = [total[i : i + 1] for i in range(2 * H)]
    for h in range(H):
        for b in range(2):
            mine = mode_plane[pl.ds(h, 1)] == b
            for p in range(2):
                amps[h, b, pl.ds(p, 1)] = jnp.where(mine, part_rows[2 * h + p], 0.0)

    def correct(b, h):
        x = 0 if b == 0 else CX - 1
        weight = jnp.where(mode_plane[pl.ds(h, 1)] == b, scale, 0.0)
        real = weight * (part_rows[2 * h] - gust[h, pl.ds(0, 1)])
        imag = weight * (part_rows[2 * h + 1] - gust[h, pl.ds(1, 1)])
        cos, sin = cosines[h, pl.ds(0, CT)], sines[h, pl.ds(0, CT)]
        coef = jnp.concatenate(
            [real * cos - imag * sin, real * sin + imag * cos], axis=0
        )
        q = dot(coef, phi[h], (((1,), (1,)), ((), ())))
        for p in range(2):
            for v in range(V):
                at = (h * F + p * V + v, x_rows(x), slice(None))
                out[at] = out[at] - r_cols[b, v] * q[p * CT : (p + 1) * CT]

    @pl.when(jnp.logical_not(has_lo))
    def _():
        for h in range(H):
            correct(0, h)

    @pl.when(jnp.logical_not(has_hi))
    def _():
        for h in range(H):
            correct(1, h)

    @pl.when(is_root)
    def _():
        shares(ROOTS * X - 1).wait_send()

        @pl.when(serves)
        def _():
            for j in range(2):
                total_copy(j).wait_send()

    @pl.when(jnp.logical_not(is_root))
    def _():
        shares(ROOTS * X).wait_send()

    @pl.when(on_plane & (th > 0))
    def _():
        crit_copy(1).wait_send()

    @pl.when(on_plane & (th == T - 1))
    def _():
        crit_copy(0).wait_send()

    for side in range(2):
        info_copy(side).wait_send()
        u_copy(side).wait_send()
        first_copy(side).wait_send()

        def _():
            for kind in (XU, XF, XINFO):
                x_copy(kind, side).wait_send()
            for t_side in range(2):
                corner_copy(t_side, side).wait_send()

        when_x_target(side, _)


def store_kernel(fields, amps, fields_out, amps_out, sems):
    copies = [
        pltpu.make_async_copy(fields, fields_out, sems.at[0]),
        pltpu.make_async_copy(amps, amps_out, sems.at[1]),
    ]
    for copy in copies:
        copy.start()
    for copy in copies:
        copy.wait()


def store(fields, amps):
    vmem = pl.BlockSpec(memory_space=pl.ANY)
    hbm = pl.BlockSpec(memory_space=pltpu.HBM)
    return pl.pallas_call(
        store_kernel,
        out_shape=tuple(jax.ShapeDtypeStruct(a.shape, a.dtype) for a in (fields, amps)),
        in_specs=(vmem, vmem),
        out_specs=(hbm, hbm),
        compiler_params=pltpu.CompilerParams(vmem_limit_bytes=2**20),
        scratch_shapes=[pltpu.SemaphoreType.DMA((2,))],
        name="store",
    )(fields, amps)


def local(T, X, *args):
    state, source, sigma, stagger = args[:4]
    H, two, V, CT, CX, NR = state.shape
    F = two * V
    HF = H * F
    NMODE = args[7].shape[1]
    dims = (T, X, H, V, CT, CX, NR, stagger.shape[0], NMODE)
    N = T * X
    rows = CT * CX
    f32 = jnp.float32
    hbm = pl.BlockSpec(memory_space=pl.ANY)
    vmem = pl.BlockSpec(memory_space=pltpu.VMEM)
    DMA = pltpu.SemaphoreType.DMA
    stagger, a_theta, a_axial, a_radial, orders, radial, planes, gust, l_rows, r_cols = args[3:]
    small = [stagger, jnp.swapaxes(a_theta, 0, 1), a_axial, a_radial, l_rows, r_cols]
    small += [orders, radial, planes, gust]
    pad = -(-2 * H // 8) * 8
    sides = [
        (HF, CX, NR),
        (HF, CX, NR),
        (HF, CX, NR),
        (HF, CT, NR),
        (HF, CT, NR),
        (HF, CT, NR),
        (HF, CT, NR),
        (CT, NR),
        (CT, NR),
        (2, -(-HF // 8) * 8, NR),
        (2, -(-HF // 8) * 8, NR),
        (3, 8 * V, NR),
        (3, 8 * V, NR),
        (2 * CX + 8, NR),
        (2 * CX + 8, NR),
        (2 * CX, NR),
        (V * V, 8, NR),
    ]
    fields, amplitudes = pl.pallas_call(
        functools.partial(kernel, dims),
        out_shape=(
            jax.ShapeDtypeStruct((HF, rows, NR), f32),
            jax.ShapeDtypeStruct((H, 2, 2, NMODE), f32),
        ),
        in_specs=[hbm] * 13,
        out_specs=(vmem, vmem),
        scratch_shapes=[pltpu.SMEM(a.shape, a.dtype) for a in small[:6]]
        + [pltpu.VMEM(a.shape, a.dtype) for a in small[6:]]
        + [
            pltpu.VMEM((HF, rows + 2 * CX, NR), f32),
            pltpu.VMEM((HF, rows, NR), f32),
            pltpu.VMEM((rows, NR), f32),
            pltpu.VMEM((HF, rows + 2 * CX, NR), f32),
            pltpu.VMEM((rows, NR), f32),
        ]
        + [pltpu.VMEM((2, *shape), f32) for shape in sides]
        + [
            pltpu.VMEM((2 * H * 2 * CT, NR), f32),
            pltpu.VMEM((H, NR, NMODE), f32),
            pltpu.VMEM((H, 2 * CT, NMODE), f32),
            pltpu.VMEM((H, 2 * CT, NMODE), f32),
            pltpu.VMEM((pad, NMODE), f32),
            pltpu.VMEM((N, pad, NMODE), f32),
            DMA((3,)),
            DMA((10,)),
            DMA((7, 2)),
            DMA((7, 2)),
            DMA((2, 2)),
            DMA((2, 2)),
            DMA,
            DMA,
            pltpu.VMEM((pad, NMODE), f32),
            DMA((2,)),
            DMA,
        ],
        compiler_params=pltpu.CompilerParams(
            collective_id=0, has_side_effects=True, vmem_limit_bytes=16 * 2**20
        ),
        name="wake",
    )(
        *(pltpu.with_memory_space_constraint(a, pltpu.HBM) for a in (state.reshape(HF, rows, NR),
        source.reshape(HF, rows, NR),
        sigma.reshape(rows, NR),
        *small)),
    )
    fields, amplitudes = store(fields, amplitudes)
    return fields.reshape(state.shape), amplitudes


def solution(mesh):
    field = P(None, None, None, "theta", "xr", None)
    placed = (field, field, P("theta", "xr", None), P("theta")) + (P(),) * 9
    return jax.shard_map(
        functools.partial(local, mesh.shape["theta"], mesh.shape["xr"]),
        mesh=mesh,
        in_specs=placed,
        out_specs=(field, P()),
        check_vma=False,
    )
```

```python
import functools
import math

import jax
import jax.numpy as jnp
from jax import lax
from jax.experimental import pallas as pl
from jax.experimental.pallas import tpu as pltpu
from jax.sharding import PartitionSpec as P

courant = 0.5
viscosity = 0.1
base_frequency = 0.5
highest = lax.Precision.HIGHEST
MESH = pl.DeviceIdType.MESH


def kernel(
    dims,
    state_hbm,
    source_hbm,
    sigma_hbm,
    *refs,
):
    small_hbm, refs = refs[:10], refs[10:]
    out, amps, refs = refs[0], refs[1], refs[2:]
    small, refs = refs[:10], refs[10:]
    stagger, a_theta, a_axial, a_radial, l_rows, r_cols = small[:6]
    mode_order, mode_radial, mode_plane, gust = small[6:]
    (
        state,
        source,
        sigma,
        first,
        step,
        uhalo,
        fhalo,
        fsend,
        xuhalo,
        xusend,
        xfhalo,
        xfsend,
        xinfo,
        xinfo_send,
        corner,
        corner_send,
        crit,
        crit_send,
        info,
        info_send,
        ghost_step,
        ghost_matrix,
        planes,
        beside,
        phi,
        phi_high,
        phi_low,
        cosines,
        sines,
        part,
        parts,
        load_sem,
        small_sem,
        send_sem,
        recv_sem,
        csend_sem,
        crecv_sem,
        psend_sem,
        precv_sem,
        whole,
        wsend_sem,
        wrecv_sem,
    ) = refs
    T, X, H, V, CT, CX, NR, NPASS, NMODE = dims
    F = 2 * V
    HF = H * F
    CPP = CT // NPASS
    N = T * X
    HP = 2 * H
    PR = 2 * CT
    th = lax.axis_index("theta")
    xr = lax.axis_index("xr")
    me = th * X + xr
    up = lax.rem(th + 1, T)
    down = lax.rem(th + T - 1, T)
    has_lo = xr > 0
    has_hi = xr < X - 1
    on_plane = jnp.logical_not(has_lo & has_hi)
    total_theta = CT * T
    scale = 1.0 / math.sqrt(total_theta * NR)
    U, FIRST, INFO, CRIT, XU, XF, XINFO = range(7)

    barrier = pltpu.get_barrier_semaphore()

    Q = T // 4
    ROOTS = 2 * Q
    is_root = th < ROOTS

    def for_others(count, act):
        def ring(t):
            for x in range(X):

                @pl.when((t != th) | (x != xr))
                def _():
                    act(t, x)

        if count * X <= 64:
            for t in range(count):
                ring(t)
        else:
            pl.loop(0, count)(ring)

    def ordered(shift, act):
        def ring(i):
            t = lax.rem(i + shift, ROOTS)
            for x in range(X):

                @pl.when((t != th) | (x != xr))
                def _():
                    act(t, x)

        if ROOTS * X <= 64:
            for i in range(ROOTS):
                ring(i)
        else:
            pl.loop(0, ROOTS)(ring)

    def greet(t, x):
        pl.semaphore_signal(barrier, inc=1, device_id=(t, x), device_id_type=MESH)

    def greet_all():
        greeters = ROOTS * X - is_root.astype(jnp.int32)
        for dt in (-1, 0, 1):
            for dx in (-1, 0, 1):
                t, x = th + dt, xr + dx
                inside = (t >= 0) & (t < T) & (x >= 0) & (x < X)
                if dt or dx:
                    greeters += (inside & (t >= ROOTS)).astype(jnp.int32)
                    pl.when(inside & jnp.logical_not(is_root))(lambda: greet(t, x))

        @pl.when(is_root)
        def _():
            for_others(T, greet)

        return greeters

    little = [
        pltpu.make_async_copy(src, dst, small_sem.at[i])
        for i, (src, dst) in enumerate(zip(small_hbm, small))
    ]
    def span(source_ref, target, offset, start, count, sem):
        return pltpu.make_async_copy(
            source_ref.at[:, pl.ds(start * CX, count * CX)],
            target.at[:, pl.ds(offset + start * CX, count * CX)],
            load_sem.at[sem],
        )

    loads = [
        pltpu.make_async_copy(sigma_hbm, sigma, load_sem.at[0]),
        span(state_hbm, state, CX, 0, 2, 1),
        span(source_hbm, source, 0, 0, 1, 2),
        span(state_hbm, state, CX, CT - 2, 2, 3),
        span(source_hbm, source, 0, CT - 1, 1, 4),
        span(state_hbm, state, CX, 2, CT - 4, 5),
        span(source_hbm, source, 0, 1, CT - 2, 6),
    ]
    for copy in loads[:1] + little + loads[1:]:
        copy.start()
    greeters = greet_all()

    zero = jnp.zeros((HF, CX, NR), jnp.float32)
    for buf in (state, first):
        buf[:, pl.ds(0, CX)] = zero
        buf[:, pl.ds(CX + CT * CX, CX)] = zero
    planes[...] = jnp.zeros_like(planes)
    part[...] = jnp.zeros_like(part)
    crit_rows = -(-HF // 8) * 8
    crit_send[...] = jnp.zeros_like(crit_send)
    beside[...] = jnp.zeros_like(beside)
    state_rows = state.reshape(HF * (CT + 2) * CX, NR)
    source_rows = source.reshape(HF * CT * CX, NR)
    if crit.shape[2] > crit_rows:
        rest = crit.shape[2] - crit_rows
        crit[:, :, pl.ds(crit_rows, rest)] = jnp.zeros((2, 3, rest, NR), jnp.float32)

    def x_rows(row):
        return pl.ds(row, CT, stride=CX)

    def neighbour(side):
        return (up if side == 0 else down, xr)

    def message(kind, side, src, dst, target):
        return pltpu.make_async_remote_copy(
            src_ref=src,
            dst_ref=dst,
            send_sem=send_sem.at[kind, side],
            recv_sem=recv_sem.at[kind, side],
            device_id=target,
            device_id_type=MESH,
        )

    def u_copy(side):
        rows = pl.ds(CX + ((CT - 1) * CX if side == 0 else 0), CX)
        return message(U, side, state.at[:, rows], uhalo.at[side], neighbour(side))

    def first_copy(side):
        return message(FIRST, side, fsend.at[side], fhalo.at[side], neighbour(side))

    def info_copy(side):
        return message(INFO, side, info_send.at[side], info.at[side], neighbour(side))

    def crit_copy(side):
        rows = pl.ds(0, crit_rows)
        return message(
            CRIT, side, crit_send.at[side, :, rows], crit.at[side, :, rows], neighbour(side)
        )

    def x_neighbour(side):
        return (th, xr + 1 if side == 0 else xr - 1)

    def x_copy(kind, side):
        src, dst = {
            XU: (xusend, xuhalo),
            XF: (xfsend, xfhalo),
            XINFO: (xinfo_send, xinfo),
        }[kind]
        return message(kind, side, src.at[side], dst.at[side], x_neighbour(side))

    def corner_copy(side, x_side):
        return pltpu.make_async_remote_copy(
            src_ref=corner_send.at[side, x_side, pl.ds(0, crit_rows)],
            dst_ref=corner.at[side, x_side, pl.ds(0, crit_rows)],
            send_sem=csend_sem.at[side, x_side],
            recv_sem=crecv_sem.at[side, x_side],
            device_id=(up if side == 0 else down, xr + 1 if x_side == 0 else xr - 1),
            device_id_type=MESH,
        )

    def when_x_target(side, act):
        pl.when(has_hi if side == 0 else has_lo)(act)

    def when_x_source(side, act):
        pl.when(has_lo if side == 0 else has_hi)(act)

    row_id = lax.broadcasted_iota(jnp.int32, (CX, NR), 0)
    lane_id = lax.broadcasted_iota(jnp.int32, (CX, NR), 1)
    first_row = row_id == 0
    last_row = row_id == CX - 1
    first_lane = lane_id == 0
    last_lane = lane_id == NR - 1

    BLOCK = 2
    SPAN = 128
    cells = lax.broadcasted_iota(jnp.int32, (PR, SPAN), 0)
    cells = th * CT + jnp.where(cells >= CT + 2, CT + 1 - cells, cells)
    orders = lax.broadcasted_iota(jnp.int32, (PR, SPAN), 1) - SPAN // 2
    turns = (orders * cells).astype(jnp.float32)
    turns = turns - jnp.floor(turns / total_theta) * total_theta
    angle = (2.0 * math.pi) * turns / total_theta
    def thirds(a):
        high = a.astype(jnp.bfloat16)
        rest = a - high.astype(jnp.float32)
        middle = rest.astype(jnp.bfloat16)
        low = (rest - middle.astype(jnp.float32)).astype(jnp.bfloat16)
        return jnp.concatenate([high, middle, low], axis=0)

    waves = thirds(jnp.concatenate([jnp.cos(angle), jnp.sin(angle)], axis=0))
    radial = lax.broadcasted_iota(jnp.int32, (8, NR), 0)
    radial_pos = lax.broadcasted_iota(jnp.int32, (8, NR), 1).astype(jnp.float32) + 0.5
    phi_table = jnp.where(
        radial == 0,
        1.0,
        math.sqrt(2.0) * jnp.cos(math.pi * radial.astype(jnp.float32) * radial_pos / NR),
    )

    def dot(a, b, dims=(((1,), (0,)), ((), ()))):
        return lax.dot_general(
            a, b, dims, precision=highest, preferred_element_type=jnp.float32
        )

    for copy in little:
        copy.wait()
    order_id = lax.broadcasted_iota(jnp.int32, (SPAN, NMODE), 0) - SPAN // 2
    radial_id = lax.broadcasted_iota(jnp.int32, (8, NMODE), 0)
    loads[0].wait()
    step[...] = courant / (1.0 + sigma[...])
    for side in range(2):
        edge, second = (CT - 1, CT - 2) if side == 0 else (0, 1)
        info_send[side, pl.ds(0, CX)] = sigma[pl.ds(edge * CX, CX)]
        info_send[side, pl.ds(CX, CX)] = sigma[pl.ds(second * CX, CX)]
        kind = stagger[NPASS - 1 if side == 0 else 0].astype(jnp.float32)
        info_send[side, pl.ds(2 * CX, 8)] = jnp.full((8, NR), kind, jnp.float32)
    for copy in loads[1:5]:
        copy.wait()

    def update(field, result, result_offset, factor, t, h):
        freq = base_frequency * (h + 1).astype(jnp.float32)
        bases = [pl.multiple_of((t + j) * CX, CX) for j in range(BLOCK)]
        kind = stagger[t // CPP]
        damps = [2.0 * sigma[pl.ds(base, CX)] + 12.0 * viscosity for base in bases]
        groups = [(j, p) for j in range(BLOCK) for p in range(2)]
        flux = {g: [None] * V for g in groups}
        for w in range(V):
            values = {}
            for j, p in groups:
                f = h * F + p * V + w
                u, tm, tp = [field[f, pl.ds(bases[j] + k * CX, CX)] for k in (1, 0, 2)]
                xm = jnp.where(first_row, 0.0, pltpu.roll(u, 1, 0))
                xp = jnp.where(last_row, 0.0, pltpu.roll(u, CX - 1, 0))
                rm = jnp.where(first_lane, 0.0, pltpu.roll(u, 1, 1))
                rp = jnp.where(last_lane, 0.0, pltpu.roll(u, NR - 1, 1))
                sums = ((tp + tm) + (xp + xm)) + (rp + rm)
                values[j, p] = (u, tp - tm, xp - xm, rp - rm, sums)
            for v in range(V):
                at, ax, ar = a_theta[v, kind, w], a_axial[v, w], a_radial[v, w]
                for j, p in groups:
                    u, dth, dx, dr, sums = values[j, p]
                    term = at * dth + ax * dx + ar * dr
                    if v == w:
                        turned = 2.0 * freq if p == 1 else -2.0 * freq
                        term = term + (damps[j] * u - (2.0 * viscosity) * sums)
                        term = term + turned * values[j, 1 - p][0]
                    old = flux[j, p][v]
                    flux[j, p][v] = term if old is None else old + term
        for j, p in groups:
            dt = factor * step[pl.ds(bases[j], CX)]
            half = 0.5 * dt
            for v in range(V):
                f = h * F + p * V + v
                start = state[f, pl.ds(bases[j] + CX, CX)] + dt * source[f, pl.ds(bases[j], CX)]
                result[f, pl.ds(bases[j] + result_offset, CX)] = start - half * flux[j, p][v]

    def halo_terms(values, matrix, sign):
        terms = []
        for v in range(V):
            total = matrix(v, 0) * values[0]
            for w in range(1, V):
                total = total + matrix(v, w) * values[w]
            terms.append((sign * 0.5) * total - viscosity * values[v])
        return terms

    def each_terms(values, matrix, sign, use):
        for v in range(V):
            totals = [0.0] * len(values)
            for w in range(V):
                entry = (sign * 0.5) * matrix(v, w)
                if v == w:
                    entry = entry - viscosity
                for i, value in enumerate(values):
                    totals[i] = totals[i] + entry * value[w]
            for i, total in enumerate(totals):
                use(i * V + v, total)

    def grouped(read):
        return [[read(hp * V + w) for w in range(V)] for hp in range(HP)]

    G = 8

    def edge_values(side):
        t, beyond = (CT - 1, CT - 2) if side == 0 else (0, 1)
        kind = stagger[t // CPP]
        sign_t = -1.0 if side == 0 else 1.0

        def fill(b):
            x, inner = (0, 1) if b == 0 else (CX - 1, CX - 2)
            for w in range(V):
                at = pl.ds(w, HP, stride=V)
                pitch = CT * CX + 2 * CX
                for target, row in (
                    (crit_send.at[side, 0], CX + t * CX + x),
                    (crit_send.at[side, 1], CX + t * CX + inner),
                    (beside.at[0], CX + beyond * CX + x),
                ):
                    target[at] = state_rows[pl.ds(w * pitch + row, HP, stride=V * pitch)]
                pitch = CT * CX
                beside[1, at] = source_rows[
                    pl.ds(w * pitch + t * CX + x, HP, stride=V * pitch)
                ]
            packed = [pl.ds(w, G, stride=V) for w in range(V)]
            edge = [crit_send[side, 0, at] for at in packed]
            near = [crit_send[side, 1, at] for at in packed]
            after = [beside[0, at] for at in packed]
            force = [beside[1, at] for at in packed]
            rows = lax.broadcasted_iota(jnp.int32, (G, NR), 0)
            lanes = lax.broadcasted_iota(jnp.int32, (G, NR), 1)
            odd = rows % 2 == 1
            freq = base_frequency * (rows // 2 + 1).astype(jnp.float32)
            freq = jnp.where(odd, freq, -freq)
            slopes, sums = [], []
            for w in range(V):
                rm = jnp.where(lanes == 0, 0.0, pltpu.roll(edge[w], 1, 1))
                rp = jnp.where(lanes == NR - 1, 0.0, pltpu.roll(edge[w], NR - 1, 1))
                slopes.append(rp - rm)
                sums.append(rp + rm)
            along_t = halo_terms(after, lambda v, w: a_theta[v, kind, w], sign_t)
            along_x = halo_terms(near, lambda v, w: a_axial[v, w], 1.0 if b == 0 else -1.0)
            at = pl.ds(t * CX + x, 1)
            damp = jnp.broadcast_to(sigma[at] + 6.0 * viscosity, (G, NR))
            dt = jnp.broadcast_to(0.5 * step[at], (G, NR))
            for v in range(V):
                total = a_radial[v, 0] * slopes[0]
                for w in range(1, V):
                    total = total + a_radial[v, w] * slopes[w]
                swapped = jnp.where(odd, pltpu.roll(edge[v], 1, 0), pltpu.roll(edge[v], G - 1, 0))
                res = 0.5 * total - viscosity * sums[v] + along_t[v] + along_x[v]
                res = res + damp * edge[v] + freq * swapped - force[v]
                crit_send[side, 2, packed[v]] = edge[v] - dt * res

        @pl.when(jnp.logical_not(has_lo))
        def _():
            fill(0)

        @pl.when(jnp.logical_not(has_hi))
        def _():
            fill(1)

    def open_sends():
        pl.semaphore_wait(barrier, greeters)

        @pl.when(on_plane & (th == T - 1))
        def _():
            crit_copy(0).start()

        @pl.when(on_plane & (th > 0))
        def _():
            crit_copy(1).start()

        info_copy(0).start()

        @pl.when(th > 0)
        def _():
            info_copy(1).start()

    def line_sends():
        for side in range(2):

            def _():
                x = CX - 1 if side == 0 else 0
                for f in range(HF):
                    xusend[side, f] = state[f, x_rows(CX + x), :]
                xinfo_send[side] = sigma[x_rows(x), :]
                x_copy(XU, side).start()
                x_copy(XINFO, side).start()

            when_x_target(side, _)

    def u_sends():
        @pl.when(th > 0)
        def _():
            u_copy(1).start()

        u_copy(0).start()

    def edge_sends():
        for side in range(2):
            rows = pl.ds(CX + ((CT - 1) * CX if side == 0 else 0), CX)
            fsend[side] = first[:, rows].reshape(HF * CX, NR)
        @pl.when(th == T - 1)
        def _():
            first_copy(0).start()

        for side in range(2):

            def _():
                x = CX - 1 if side == 0 else 0
                for t_side in range(2):
                    row = CX + ((CT - 1) * CX if t_side == 0 else 0) + x
                    for f in range(HF):
                        corner_send[t_side, side, pl.ds(f, 1)] = state[f, pl.ds(row, 1)]
                corner_copy(0, side).start()

                @pl.when(th > 0)
                def _():
                    corner_copy(1, side).start()

            when_x_target(side, _)

    def tables():
        for h in range(H):
            chosen = (mode_order[pl.ds(h, 1)] == order_id).astype(jnp.float32)
            picked = jnp.dot(
                waves, chosen.astype(jnp.bfloat16), preferred_element_type=jnp.float32
            )
            picked = picked[: 2 * PR] + picked[2 * PR : 4 * PR] + picked[4 * PR :]
            cosines[h] = picked[:PR]
            sines[h] = picked[PR:]
            chosen = (mode_radial[pl.ds(h, 1)] == radial_id).astype(jnp.float32)
            phi[h] = dot(phi_table, chosen, (((0,), (0,)), ((), ())))
            phi_high[h] = phi[h].astype(jnp.bfloat16)
            phi_low[h] = (phi[h] - phi_high[h].astype(jnp.float32)).astype(jnp.bfloat16)

    for side in (1, 0):
        edge_values(side)
    blocks = CT // BLOCK
    early = (th < 2) & (xr == 0)
    open_at = jnp.where(early, blocks, 0)
    edge_at = jnp.where(early, blocks, 2)

    @pl.loop(0, blocks + 1)
    def _(i):
        pl.when(i == open_at)(open_sends)

        @pl.when(i == 0)
        def _():
            for copy in loads[5:]:
                copy.wait()

        pl.when(i == open_at)(line_sends)
        pl.when(i == jnp.where(early, blocks, 1))(u_sends)
        pl.when(i == 1)(tables)
        pl.when(i == edge_at)(edge_sends)

        @pl.when(i < blocks)
        def _():
            t = BLOCK * jnp.where(i == 0, 0, jnp.where(i == 1, blocks - 1, i - 1))

            @pl.loop(0, H)
            def _(h):
                update(state, first, CX, 0.5, t, h)

    for side in range(2):

        def _():
            x = CX - 1 if side == 0 else 0
            for f in range(HF):
                xfsend[side, pl.ds(f * CT, CT)] = first[f, x_rows(CX + x), :]
            x_copy(XF, side).start()

        when_x_target(side, _)

    def own_planes(b):
        x = 0 if b == 0 else CX - 1
        inner = 1 if b == 0 else CX - 2
        lines = lax.broadcasted_iota(jnp.int32, (CT, NR), 0)
        lanes = lax.broadcasted_iota(jnp.int32, (CT, NR), 1)
        top, bottom = lines == 0, lines == CT - 1
        left, right = lanes == 0, lanes == NR - 1
        ls, gxs, grs, gts = [], [], [], []
        for w in range(V):
            ls.append(l_rows[b, w])
            gx = gr = 0.0
            for v in range(V):
                gx = gx + l_rows[b, v] * a_axial[v, w]
                gr = gr + l_rows[b, v] * a_radial[v, w]
            gt = None
            for k in range(NPASS):
                row = 0.0
                for v in range(V):
                    row = row + l_rows[b, v] * a_theta[v, stagger[k], w]
                gt = row if gt is None else jnp.where(lines >= k * CPP, row, gt)
            gxs.append(gx)
            grs.append(gr)
            gts.append(gt)
        damp = sigma[x_rows(x), :] + 6.0 * viscosity
        dt = step[x_rows(x), :]

        @pl.loop(0, H)
        def _(h):
            freq = base_frequency * (h + 1).astype(jnp.float32)
            fields = [0.0, 0.0]
            rest = []
            for p in range(2):
                along_t = start = forcing = inside = radial = 0.0
                flux = sums = 0.0
                for w in range(V):
                    f = h * F + p * V + w
                    u = first[f, x_rows(CX + x), :]
                    near = first[f, x_rows(CX + inner), :]
                    tm = jnp.where(top, 0.0, pltpu.roll(u, 1, 0))
                    tp = jnp.where(bottom, 0.0, pltpu.roll(u, CT - 1, 0))
                    dx = near if b == 0 else -near
                    flux = flux + (gts[w] * (tp - tm) + gxs[w] * dx)
                    sums = sums + ls[w] * ((tp + tm) + near)
                    fields[p] = fields[p] + ls[w] * u
                    radial = radial + grs[w] * u
                    forcing = forcing + ls[w] * source[f, x_rows(x), :]
                    start = start + ls[w] * state[f, x_rows(CX + x), :]
                for value, weight, sign in ((radial, 0.5, -1.0), (fields[p], -viscosity, 1.0)):
                    rm = jnp.where(left, 0.0, pltpu.roll(value, 1, 1))
                    rp = jnp.where(right, 0.0, pltpu.roll(value, NR - 1, 1))
                    inside = inside + weight * (rp + sign * rm)
                res = 0.5 * flux - viscosity * sums + inside + damp * fields[p] - forcing
                rest.append((start, res))
            for p in range(2):
                start, res = rest[p]
                turned = -freq if p == 0 else freq
                res = res + turned * fields[1 - p]
                at = pl.ds(pl.multiple_of((2 * h + p) * PR, PR), CT)
                planes[at] = start - dt * res

    @pl.when(jnp.logical_not(has_lo))
    def _():
        own_planes(0)

    @pl.when(jnp.logical_not(has_hi))
    def _():
        own_planes(1)

    def ghosts(side):
        info_copy(side).wait_recv()
        ghost_step[side] = courant / (1.0 + info[side, pl.ds(0, 2 * CX)])
        kind = info[side, pl.ds(2 * CX, 8)]
        masks = [kind == float(k) for k in range(a_theta.shape[1])]
        for v in range(V):
            for w in range(V):
                entry = jnp.zeros((8, NR), jnp.float32)
                for k, mask in enumerate(masks):
                    entry = jnp.where(mask, a_theta[v, k, w], entry)
                ghost_matrix[side, v * V + w] = entry

    def crossed(side):
        return ((side == 1) & (th < T - 1)) | ((side == 0) & (th == 0))

    for side in (1, 0):
        pl.when(crossed(side))(lambda: ghosts(side))

    @pl.when(th == 0)
    def _():
        info_copy(1).start()
        u_copy(1).start()
        first_copy(1).start()
        for side in range(2):
            when_x_target(side, lambda: corner_copy(1, side).start())

    def cross(b, side):
        sign = 1.0 if side == 1 else -1.0
        x = 0 if b == 0 else CX - 1
        inner = 1 if b == 0 else CX - 2
        own_edge, own_next = (CT - 1, CT - 2) if side == 1 else (0, 1)
        ghost_edge, ghost_next = (CT, CT + 1) if side == 1 else (CT + 2, CT + 3)
        kind = stagger[own_edge // CPP]
        def rows_of(ref, which, j):
            return [ref[which, j, pl.ds(w, G, stride=V)] for w in range(V)]

        own_u, own_in, own_first = [rows_of(crit_send, 1 - side, j) for j in range(3)]
        ghost_u, ghost_in, ghost_first = [rows_of(crit, side, j) for j in range(3)]

        def wide(row):
            return jnp.broadcast_to(row, (G, NR))

        own_dt = wide(step[pl.ds(own_edge * CX + x, 1)])
        own_in_dt = wide(step[pl.ds(own_edge * CX + inner, 1)])
        own_next_dt = wide(step[pl.ds(own_next * CX + x, 1)])
        own_sigma = wide(sigma[pl.ds(own_edge * CX + x, 1)])
        ghost_dt = wide(ghost_step[side, pl.ds(x, 1)])
        ghost_in_dt = wide(ghost_step[side, pl.ds(inner, 1)])
        ghost_next_dt = wide(ghost_step[side, pl.ds(CX + x, 1)])
        ghost_sigma = wide(info[side, pl.ds(x, 1)])

        def own_matrix(v, w):
            return a_theta[v, kind, w]

        matrix = [[ghost_matrix[side, v * V + w] for w in range(V)] for v in range(V)]

        def changes(values, matrix, sign, dt):
            return [(-0.5 * dt) * term for term in halo_terms(values, matrix, sign)]

        def other_matrix(v, w):
            return matrix[v][w]

        own_d = changes(ghost_u, own_matrix, sign, own_dt)
        own_in_d = changes(ghost_in, own_matrix, sign, own_in_dt)
        ghost_d = changes(own_u, other_matrix, -sign, ghost_dt)
        ghost_in_d = changes(own_in, other_matrix, -sign, ghost_in_dt)
        ls = [l_rows[b, w] for w in range(V)]

        def contract(weights, values):
            total = weights[0] * values[0]
            for w in range(1, V):
                total = total + weights[w] * values[w]
            return total

        def column(matrix, w):
            total = ls[0] * matrix(0, w)
            for v in range(1, V):
                total = total + ls[v] * matrix(v, w)
            return total

        own_w = [(sign * 0.5) * column(own_matrix, w) - viscosity * ls[w] for w in range(V)]
        ghost_w = [(-sign * 0.5) * column(other_matrix, w) - viscosity * ls[w] for w in range(V)]
        flip = 0.5 if b == 0 else -0.5
        near_w = [
            flip * column(lambda v, w: a_axial[v, w], w) - viscosity * ls[w] for w in range(V)
        ]
        radial_w = [column(lambda v, w: a_radial[v, w], w) for w in range(V)]
        rows = lax.broadcasted_iota(jnp.int32, (G, NR), 0)
        lanes = lax.broadcasted_iota(jnp.int32, (G, NR), 1)
        odd = rows % 2 == 1
        freq = base_frequency * (rows // 2 + 1).astype(jnp.float32)
        freq = jnp.where(odd, freq, -freq)
        left, right = lanes == 0, lanes == NR - 1

        def local(d, d_in, damping):
            radial = contract(radial_w, d)
            fields = contract(ls, d)
            swapped = jnp.where(odd, pltpu.roll(fields, 1, 0), pltpu.roll(fields, G - 1, 0))
            total = contract(near_w, d_in) + freq * swapped
            total = total + (damping + 6.0 * viscosity) * fields
            for value, weight, sign in ((radial, 0.5, -1.0), (fields, -viscosity, 1.0)):
                rm = jnp.where(left, 0.0, pltpu.roll(value, 1, 1))
                rp = jnp.where(right, 0.0, pltpu.roll(value, NR - 1, 1))
                total = total + weight * (rp + sign * rm)
            return total

        total_ghost = [a + d for a, d in zip(ghost_first, ghost_d)]
        total_own = [a + d for a, d in zip(own_first, own_d)]
        found = {
            own_next: own_next_dt * contract(own_w, own_d),
            own_edge: own_dt * (local(own_d, own_in_d, own_sigma) + contract(own_w, total_ghost)),
            ghost_edge: ghost_dt
            * (local(ghost_d, ghost_in_d, ghost_sigma) + contract(ghost_w, total_own)),
            ghost_next: ghost_next_dt * contract(ghost_w, ghost_d),
        }
        for row, value in found.items():
            at = pl.ds(row, HP, stride=PR)
            planes[at, :] = planes[at, :] - value[:HP]

    def project(b):
        for h in range(H):
            projected = dot(planes[pl.ds(2 * h * PR, 2 * PR)], phi[h])
            real, imag = projected[:PR], projected[PR:]
            weight = jnp.where(mode_plane[pl.ds(h, 1)] == b, scale, 0.0)
            part_real = jnp.sum(real * cosines[h] + imag * sines[h], axis=0, keepdims=True)
            part_imag = jnp.sum(imag * cosines[h] - real * sines[h], axis=0, keepdims=True)
            part[pl.ds(2 * h, 1)] = weight * part_real
            part[pl.ds(2 * h + 1, 1)] = weight * part_imag

    def finish_plane(b):
        @pl.when(th < T - 1)
        def _():
            crit_copy(1).wait_recv()
            cross(b, 1)

        @pl.when(th == 0)
        def _():
            crit_copy(0).wait_recv()
            cross(b, 0)

        project(b)

    @pl.when(jnp.logical_not(has_lo))
    def _():
        finish_plane(0)

    @pl.when(jnp.logical_not(has_hi))
    def _():
        finish_plane(1)

    def share(t, x):
        pltpu.make_async_remote_copy(
            src_ref=part.at[pl.ds(0, HP)],
            dst_ref=parts.at[me, pl.ds(0, HP)],
            send_sem=psend_sem,
            recv_sem=precv_sem,
            device_id=(t, x),
            device_id_type=MESH,
        ).start()

    shift = jnp.where(th < Q, Q, 0)
    ordered(shift, share)

    @pl.when(th > 0)
    def _():
        first_copy(1).start()

    @pl.when(th < T - 1)
    def _():
        first_copy(0).start()

    parts[me] = part[...]
    for side in (0, 1):
        pl.when(jnp.logical_not(crossed(side)))(lambda: ghosts(side))

    for side in range(2):

        def _():
            x_copy(XU, side).wait_recv()
            x = 0 if side == 0 else CX - 1
            dt = 0.5 * step[x_rows(x), :]

            def use(f, term):
                at = (f, x_rows(CX + x), slice(None))
                first[at] = first[at] - dt * term

            sign = -1.0 if side == 0 else 1.0
            each_terms(grouped(lambda f: xuhalo[side, f]), lambda v, w: a_axial[v, w], sign, use)

        when_x_source(side, _)

    def t_fix(side):
        u_copy(side).wait_recv()
        t = 0 if side == 0 else CT - 1
        kind = stagger[t // CPP]
        dt = 0.5 * step[pl.ds(t * CX, CX)]

        def use(f, term):
            at = (f, pl.ds(CX + t * CX, CX))
            first[at] = first[at] - dt * term

        sign = -1.0 if side == 0 else 1.0
        each_terms(grouped(lambda f: uhalo[side, f]), lambda v, w: a_theta[v, kind, w], sign, use)

    @pl.loop(0, blocks)
    def _(i):
        t = BLOCK * jnp.where(i + 1 >= blocks, i + 1 - blocks, i + 1)

        @pl.when(i == blocks - 2)
        def _():
            t_fix(1)

        @pl.when(i == blocks - 1)
        def _():
            t_fix(0)

        @pl.loop(0, H)
        def _(h):
            update(first, out, 0, 1.0, t, h)

    def corner_fix(side, x_side):
        corner_copy(side, x_side).wait_recv()
        t = 0 if side == 0 else CT - 1
        x = 0 if x_side == 0 else CX - 1
        kind = stagger[t // CPP]
        line_dt = 0.5 * courant / (1.0 + xinfo[x_side, pl.ds(t, 1)])
        edge_dt = 0.5 * ghost_step[side, pl.ds(x, 1)]

        values = [corner[side, x_side, pl.ds(w, 8, stride=V)] for w in range(V)]
        along_t = halo_terms(
            values, lambda v, w: a_theta[v, kind, w], -1.0 if side == 0 else 1.0
        )
        along_x = halo_terms(values, lambda v, w: a_axial[v, w], -1.0 if x_side == 0 else 1.0)
        for v in range(V):
            at = (x_side, pl.ds(v * CT + t, HP, stride=V * CT))
            xfhalo[at] = xfhalo[at] - (line_dt * along_t[v])[:HP]
            at = (side, pl.ds(v * CX + x, HP, stride=V * CX))
            fhalo[at] = fhalo[at] - (edge_dt * along_x[v])[:HP]

    def x_finish(side):
        x = 0 if side == 0 else CX - 1
        ghost_dt = 0.5 * courant / (1.0 + xinfo[side])
        dt = step[x_rows(x), :]
        away = -1.0 if side == 0 else 1.0

        ghosts = {}

        def keep(f, term):
            ghosts[f] = xfhalo[side, pl.ds(f * CT, CT)] - ghost_dt * term

        def use(f, term):
            at = (f, x_rows(x), slice(None))
            out[at] = out[at] - dt * term

        mine = grouped(lambda f: state[f, x_rows(CX + x), :])
        each_terms(mine, lambda v, w: a_axial[v, w], -away, keep)
        each_terms(grouped(lambda f: ghosts[f]), lambda v, w: a_axial[v, w], away, use)

    def t_finish(side):
        t = 0 if side == 0 else CT - 1
        kind = stagger[t // CPP]
        ghost_dt = 0.5 * ghost_step[side, pl.ds(0, CX)]
        dt = step[pl.ds(t * CX, CX)]
        away = -1.0 if side == 0 else 1.0

        values = {}

        def keep(f, term):
            values[f] = fhalo[side, pl.ds(f * CX, CX)] - ghost_dt * term

        def use(f, term):
            at = (f, pl.ds(t * CX, CX))
            out[at] = out[at] - dt * term

        mine = grouped(lambda f: state[f, pl.ds(CX + t * CX, CX)])
        each_terms(mine, lambda v, w: ghost_matrix[side, v * V + w], -away, keep)
        each_terms(grouped(lambda f: values[f]), lambda v, w: a_theta[v, kind, w], away, use)

    def shares(count):
        return pltpu.make_async_remote_copy(
            src_ref=parts.at[pl.ds(0, count), pl.ds(0, HP)],
            dst_ref=parts.at[pl.ds(0, count), pl.ds(0, HP)],
            send_sem=psend_sem,
            recv_sem=precv_sem,
            device_id=(up, xr),
            device_id_type=MESH,
        )

    def total_copy(j):
        return pltpu.make_async_remote_copy(
            src_ref=whole,
            dst_ref=whole,
            send_sem=wsend_sem.at[j],
            recv_sem=wrecv_sem,
            device_id=(th + Q + j * Q, xr),
            device_id_type=MESH,
        )

    serves = (th >= Q) & (th < 2 * Q)

    def gather():
        shares(N - 1).wait_recv()
        total = parts[0]
        if N <= 64:
            for i in range(1, N):
                total = total + parts[i]
        else:
            total = lax.fori_loop(1, N, lambda i, acc: acc + parts[i], total)
        whole[...] = total

    @pl.when(serves)
    def _():
        gather()
        for j in range(2):
            total_copy(j).start()

    for x_side in range(2):

        def _():
            x_copy(XF, x_side).wait_recv()
            x_copy(XINFO, x_side).wait_recv()

        when_x_source(x_side, _)
    for side in (1, 0):
        first_copy(side).wait_recv()
        for x_side in range(2):
            when_x_source(x_side, lambda: corner_fix(side, x_side))
        t_finish(side)
    for x_side in range(2):
        when_x_source(x_side, lambda: x_finish(x_side))

    pl.when(is_root & jnp.logical_not(serves))(gather)

    @pl.when(jnp.logical_not(is_root))
    def _():
        total_copy(0).wait_recv()

    total = whole[...]
    part_rows = [total[i : i + 1] for i in range(2 * H)]
    for h in range(H):
        for b in range(2):
            mine = mode_plane[pl.ds(h, 1)] == b
            for p in range(2):
                amps[h, b, pl.ds(p, 1)] = jnp.where(mine, part_rows[2 * h + p], 0.0)

    def correct(b, h):
        x = 0 if b == 0 else CX - 1
        weight = jnp.where(mode_plane[pl.ds(h, 1)] == b, scale, 0.0)
        real = weight * (part_rows[2 * h] - gust[h, pl.ds(0, 1)])
        imag = weight * (part_rows[2 * h + 1] - gust[h, pl.ds(1, 1)])
        cos, sin = cosines[h, pl.ds(0, CT)], sines[h, pl.ds(0, CT)]
        coef = jnp.concatenate(
            [real * cos - imag * sin, real * sin + imag * cos], axis=0
        )
        high = coef.astype(jnp.bfloat16)
        low = (coef - high.astype(jnp.float32)).astype(jnp.bfloat16)
        along = (((1,), (1,)), ((), ()))
        both = lax.dot_general(
            jnp.concatenate([high, low], axis=0),
            phi_high[h],
            along,
            preferred_element_type=jnp.float32,
        )
        q = both[: 2 * CT] + both[2 * CT :]
        q = q + lax.dot_general(
            high, phi_low[h], along, preferred_element_type=jnp.float32
        )
        for p in range(2):
            for v in range(V):
                at = (h * F + p * V + v, x_rows(x), slice(None))
                out[at] = out[at] - r_cols[b, v] * q[p * CT : (p + 1) * CT]

    @pl.when(jnp.logical_not(has_lo))
    def _():
        for h in range(H):
            correct(0, h)

    @pl.when(jnp.logical_not(has_hi))
    def _():
        for h in range(H):
            correct(1, h)

    @pl.when(is_root)
    def _():
        shares(ROOTS * X - 1).wait_send()

        @pl.when(serves)
        def _():
            for j in range(2):
                total_copy(j).wait_send()

    @pl.when(jnp.logical_not(is_root))
    def _():
        shares(ROOTS * X).wait_send()

    @pl.when(on_plane & (th > 0))
    def _():
        crit_copy(1).wait_send()

    @pl.when(on_plane & (th == T - 1))
    def _():
        crit_copy(0).wait_send()

    for side in range(2):
        info_copy(side).wait_send()
        u_copy(side).wait_send()
        first_copy(side).wait_send()

        def _():
            for kind in (XU, XF, XINFO):
                x_copy(kind, side).wait_send()
            for t_side in range(2):
                corner_copy(t_side, side).wait_send()

        when_x_target(side, _)


def store_kernel(fields, amps, fields_out, amps_out, sems):
    copies = [
        pltpu.make_async_copy(fields, fields_out, sems.at[0]),
        pltpu.make_async_copy(amps, amps_out, sems.at[1]),
    ]
    for copy in copies:
        copy.start()
    for copy in copies:
        copy.wait()


def store(fields, amps):
    vmem = pl.BlockSpec(memory_space=pl.ANY)
    hbm = pl.BlockSpec(memory_space=pltpu.HBM)
    return pl.pallas_call(
        store_kernel,
        out_shape=tuple(jax.ShapeDtypeStruct(a.shape, a.dtype) for a in (fields, amps)),
        in_specs=(vmem, vmem),
        out_specs=(hbm, hbm),
        compiler_params=pltpu.CompilerParams(vmem_limit_bytes=2**20),
        scratch_shapes=[pltpu.SemaphoreType.DMA((2,))],
        name="store",
    )(fields, amps)


def local(T, X, *args):
    state, source, sigma, stagger = args[:4]
    H, two, V, CT, CX, NR = state.shape
    F = two * V
    HF = H * F
    NMODE = args[7].shape[1]
    dims = (T, X, H, V, CT, CX, NR, stagger.shape[0], NMODE)
    N = T * X
    rows = CT * CX
    f32 = jnp.float32
    hbm = pl.BlockSpec(memory_space=pl.ANY)
    vmem = pl.BlockSpec(memory_space=pltpu.VMEM)
    DMA = pltpu.SemaphoreType.DMA
    stagger, a_theta, a_axial, a_radial, orders, radial, planes, gust, l_rows, r_cols = args[3:]
    small = [stagger, jnp.swapaxes(a_theta, 0, 1), a_axial, a_radial, l_rows, r_cols]
    small += [orders, radial, planes, gust]
    pad = -(-2 * H // 8) * 8
    sides = [
        (HF, CX, NR),
        (HF * CX, NR),
        (HF * CX, NR),
        (HF, CT, NR),
        (HF, CT, NR),
        (HF * CT, NR),
        (HF * CT, NR),
        (CT, NR),
        (CT, NR),
        (2, 8 * V, NR),
        (2, 8 * V, NR),
        (3, 8 * V, NR),
        (3, 8 * V, NR),
        (2 * CX + 8, NR),
        (2 * CX + 8, NR),
        (2 * CX, NR),
        (V * V, 8, NR),
    ]
    fields, amplitudes = pl.pallas_call(
        functools.partial(kernel, dims),
        out_shape=(
            jax.ShapeDtypeStruct((HF, rows, NR), f32),
            jax.ShapeDtypeStruct((H, 2, 2, NMODE), f32),
        ),
        in_specs=[hbm] * 13,
        out_specs=(vmem, vmem),
        scratch_shapes=[pltpu.SMEM(a.shape, a.dtype) for a in small[:6]]
        + [pltpu.VMEM(a.shape, a.dtype) for a in small[6:]]
        + [
            pltpu.VMEM((HF, rows + 2 * CX, NR), f32),
            pltpu.VMEM((HF, rows, NR), f32),
            pltpu.VMEM((rows, NR), f32),
            pltpu.VMEM((HF, rows + 2 * CX, NR), f32),
            pltpu.VMEM((rows, NR), f32),
        ]
        + [pltpu.VMEM((2, *shape), f32) for shape in sides]
        + [
            pltpu.VMEM((2 * H * 2 * CT, NR), f32),
            pltpu.VMEM((2, 8 * V, NR), f32),
            pltpu.VMEM((H, NR, NMODE), f32),
            pltpu.VMEM((H, NR, NMODE), jnp.bfloat16),
            pltpu.VMEM((H, NR, NMODE), jnp.bfloat16),
            pltpu.VMEM((H, 2 * CT, NMODE), f32),
            pltpu.VMEM((H, 2 * CT, NMODE), f32),
            pltpu.VMEM((pad, NMODE), f32),
            pltpu.VMEM((N, pad, NMODE), f32),
            DMA((7,)),
            DMA((10,)),
            DMA((7, 2)),
            DMA((7, 2)),
            DMA((2, 2)),
            DMA((2, 2)),
            DMA,
            DMA,
            pltpu.VMEM((pad, NMODE), f32),
            DMA((2,)),
            DMA,
        ],
        compiler_params=pltpu.CompilerParams(
            collective_id=0, has_side_effects=True, vmem_limit_bytes=16 * 2**20
        ),
        name="wake",
    )(
        *(pltpu.with_memory_space_constraint(a, pltpu.HBM) for a in (state.reshape(HF, rows, NR),
        source.reshape(HF, rows, NR),
        sigma.reshape(rows, NR),
        *small)),
    )
    fields, amplitudes = store(fields, amplitudes)
    return fields.reshape(state.shape), amplitudes


def solution(mesh):
    field = P(None, None, None, "theta", "xr", None)
    placed = (field, field, P("theta", "xr", None), P("theta")) + (P(),) * 9
    return jax.shard_map(
        functools.partial(local, mesh.shape["theta"], mesh.shape["xr"]),
        mesh=mesh,
        in_specs=placed,
        out_specs=(field, P()),
        check_vma=False,
    )
```

```python
import functools
import math

import jax
import jax.numpy as jnp
from jax import lax
from jax.experimental import pallas as pl
from jax.experimental.pallas import tpu as pltpu
from jax.sharding import PartitionSpec as P

courant = 0.5
viscosity = 0.1
base_frequency = 0.5
highest = lax.Precision.HIGHEST
MESH = pl.DeviceIdType.MESH


def kernel(
    dims,
    state_hbm,
    source_hbm,
    sigma_hbm,
    *refs,
):
    small_hbm, refs = refs[:10], refs[10:]
    out, amps, refs = refs[0], refs[1], refs[2:]
    small, refs = refs[:10], refs[10:]
    stagger, a_theta, a_axial, a_radial, l_rows, r_cols = small[:6]
    mode_order, mode_radial, mode_plane, gust = small[6:]
    (
        state,
        source,
        sigma,
        first,
        step,
        uhalo,
        fhalo,
        fsend,
        xuhalo,
        xusend,
        xfhalo,
        xfsend,
        xinfo,
        xinfo_send,
        corner,
        corner_send,
        crit,
        crit_send,
        info,
        info_send,
        ghost_step,
        ghost_matrix,
        planes,
        beside,
        phi,
        phi_high,
        phi_low,
        cosines,
        sines,
        part,
        parts,
        load_sem,
        small_sem,
        send_sem,
        recv_sem,
        csend_sem,
        crecv_sem,
        psend_sem,
        precv_sem,
        whole,
        wsend_sem,
        wrecv_sem,
        zrecv_sem,
    ) = refs
    T, X, H, V, CT, CX, NR, NPASS, NMODE = dims
    F = 2 * V
    HF = H * F
    CPP = CT // NPASS
    N = T * X
    HP = 2 * H
    PR = 2 * CT
    th = lax.axis_index("theta")
    xr = lax.axis_index("xr")
    me = th * X + xr
    up = lax.rem(th + 1, T)
    down = lax.rem(th + T - 1, T)
    has_lo = xr > 0
    has_hi = xr < X - 1
    on_plane = jnp.logical_not(has_lo & has_hi)
    total_theta = CT * T
    scale = 1.0 / math.sqrt(total_theta * NR)
    U, FIRST, INFO, CRIT, XU, XF, XINFO = range(7)

    barrier = pltpu.get_barrier_semaphore()

    Q = T // 4
    ROOTS = 2 * Q
    is_root = th < ROOTS

    def for_others(count, act):
        def ring(t):
            for x in range(X):

                @pl.when((t != th) | (x != xr))
                def _():
                    act(t, x)

        if count * X <= 64:
            for t in range(count):
                ring(t)
        else:
            pl.loop(0, count)(ring)

    def ordered(shift, act):
        def ring(i):
            t = lax.rem(i + shift, ROOTS)
            for x in range(X):

                @pl.when((t != th) | (x != xr))
                def _():
                    act(t, x)

        if ROOTS * X <= 64:
            for i in range(ROOTS):
                ring(i)
        else:
            pl.loop(0, ROOTS)(ring)

    def late_first(act):
        def ring(i):
            for x in range(X):

                @pl.when((i != 0) | (x != xr))
                def _():
                    act(lax.rem(T - i, T) if N > 64 else (T - i) % T, x)

        if N <= 64:
            for i in range(T):
                ring(i)
        else:
            pl.loop(0, T)(ring)

    def greet(t, x):
        pl.semaphore_signal(barrier, inc=1, device_id=(t, x), device_id_type=MESH)

    def greet_all():
        greeters = ROOTS * X - is_root.astype(jnp.int32)
        for dt in (-1, 0, 1):
            for dx in (-1, 0, 1):
                t, x = th + dt, xr + dx
                inside = (t >= 0) & (t < T) & (x >= 0) & (x < X)
                if dt or dx:
                    greeters += (inside & (t >= ROOTS)).astype(jnp.int32)
                    pl.when(inside & jnp.logical_not(is_root))(lambda: greet(t, x))

        @pl.when(is_root)
        def _():
            for_others(T, greet)

        @pl.when(jnp.logical_not(is_root))
        def _():
            for x in range(X):
                greet(0, x)

        return jnp.where(th == 0, N - 1, greeters)

    little = [
        pltpu.make_async_copy(src, dst, small_sem.at[i])
        for i, (src, dst) in enumerate(zip(small_hbm, small))
    ]
    def span(source_ref, target, offset, start, count, sem):
        return pltpu.make_async_copy(
            source_ref.at[:, pl.ds(start * CX, count * CX)],
            target.at[:, pl.ds(offset + start * CX, count * CX)],
            load_sem.at[sem],
        )

    loads = [
        pltpu.make_async_copy(sigma_hbm, sigma, load_sem.at[0]),
        span(state_hbm, state, CX, 0, 2, 1),
        span(source_hbm, source, 0, 0, 1, 2),
        span(state_hbm, state, CX, CT - 2, 2, 3),
        span(source_hbm, source, 0, CT - 1, 1, 4),
        span(state_hbm, state, CX, 2, CT - 4, 5),
        span(source_hbm, source, 0, 1, CT - 2, 6),
    ]
    for copy in loads[:1] + little + loads[1:]:
        copy.start()
    greeters = greet_all()

    zero = jnp.zeros((HF, CX, NR), jnp.float32)
    for buf in (state, first):
        buf[:, pl.ds(0, CX)] = zero
        buf[:, pl.ds(CX + CT * CX, CX)] = zero
    planes[...] = jnp.zeros_like(planes)
    part[...] = jnp.zeros_like(part)
    crit_rows = -(-HF // 8) * 8
    crit_send[...] = jnp.zeros_like(crit_send)
    beside[...] = jnp.zeros_like(beside)
    state_rows = state.reshape(HF * (CT + 2) * CX, NR)
    source_rows = source.reshape(HF * CT * CX, NR)
    if crit.shape[2] > crit_rows:
        rest = crit.shape[2] - crit_rows
        crit[:, :, pl.ds(crit_rows, rest)] = jnp.zeros((2, 3, rest, NR), jnp.float32)

    def x_rows(row):
        return pl.ds(row, CT, stride=CX)

    def neighbour(side):
        return (up if side == 0 else down, xr)

    def message(kind, side, src, dst, target):
        return pltpu.make_async_remote_copy(
            src_ref=src,
            dst_ref=dst,
            send_sem=send_sem.at[kind, side],
            recv_sem=recv_sem.at[kind, side],
            device_id=target,
            device_id_type=MESH,
        )

    def u_copy(side):
        rows = pl.ds(CX + ((CT - 1) * CX if side == 0 else 0), CX)
        return message(U, side, state.at[:, rows], uhalo.at[side], neighbour(side))

    def first_copy(side):
        return message(FIRST, side, fsend.at[side], fhalo.at[side], neighbour(side))

    def info_copy(side):
        return message(INFO, side, info_send.at[side], info.at[side], neighbour(side))

    def crit_copy(side):
        rows = pl.ds(0, crit_rows)
        return message(
            CRIT, side, crit_send.at[side, :, rows], crit.at[side, :, rows], neighbour(side)
        )

    def x_neighbour(side):
        return (th, xr + 1 if side == 0 else xr - 1)

    def x_copy(kind, side):
        src, dst = {
            XU: (xusend, xuhalo),
            XF: (xfsend, xfhalo),
            XINFO: (xinfo_send, xinfo),
        }[kind]
        return message(kind, side, src.at[side], dst.at[side], x_neighbour(side))

    def corner_copy(side, x_side):
        return pltpu.make_async_remote_copy(
            src_ref=corner_send.at[side, x_side, pl.ds(0, crit_rows)],
            dst_ref=corner.at[side, x_side, pl.ds(0, crit_rows)],
            send_sem=csend_sem.at[side, x_side],
            recv_sem=crecv_sem.at[side, x_side],
            device_id=(up if side == 0 else down, xr + 1 if x_side == 0 else xr - 1),
            device_id_type=MESH,
        )

    def when_x_target(side, act):
        pl.when(has_hi if side == 0 else has_lo)(act)

    def when_x_source(side, act):
        pl.when(has_lo if side == 0 else has_hi)(act)

    row_id = lax.broadcasted_iota(jnp.int32, (CX, NR), 0)
    lane_id = lax.broadcasted_iota(jnp.int32, (CX, NR), 1)
    first_row = row_id == 0
    last_row = row_id == CX - 1
    first_lane = lane_id == 0
    last_lane = lane_id == NR - 1

    BLOCK = 2
    SPAN = 128
    cells = lax.broadcasted_iota(jnp.int32, (PR, SPAN), 0)
    cells = th * CT + jnp.where(cells >= CT + 2, CT + 1 - cells, cells)
    orders = lax.broadcasted_iota(jnp.int32, (PR, SPAN), 1) - SPAN // 2
    turns = (orders * cells).astype(jnp.float32)
    turns = turns - jnp.floor(turns / total_theta) * total_theta
    angle = (2.0 * math.pi) * turns / total_theta
    def thirds(a):
        high = a.astype(jnp.bfloat16)
        rest = a - high.astype(jnp.float32)
        middle = rest.astype(jnp.bfloat16)
        low = (rest - middle.astype(jnp.float32)).astype(jnp.bfloat16)
        return jnp.concatenate([high, middle, low], axis=0)

    waves = thirds(jnp.concatenate([jnp.cos(angle), jnp.sin(angle)], axis=0))
    radial = lax.broadcasted_iota(jnp.int32, (8, NR), 0)
    radial_pos = lax.broadcasted_iota(jnp.int32, (8, NR), 1).astype(jnp.float32) + 0.5
    phi_table = jnp.where(
        radial == 0,
        1.0,
        math.sqrt(2.0) * jnp.cos(math.pi * radial.astype(jnp.float32) * radial_pos / NR),
    )

    def dot(a, b, dims=(((1,), (0,)), ((), ()))):
        return lax.dot_general(
            a, b, dims, precision=highest, preferred_element_type=jnp.float32
        )

    for copy in little:
        copy.wait()
    order_id = lax.broadcasted_iota(jnp.int32, (SPAN, NMODE), 0) - SPAN // 2
    radial_id = lax.broadcasted_iota(jnp.int32, (8, NMODE), 0)
    loads[0].wait()
    step[...] = courant / (1.0 + sigma[...])
    for side in range(2):
        edge, second = (CT - 1, CT - 2) if side == 0 else (0, 1)
        info_send[side, pl.ds(0, CX)] = sigma[pl.ds(edge * CX, CX)]
        info_send[side, pl.ds(CX, CX)] = sigma[pl.ds(second * CX, CX)]
        kind = stagger[NPASS - 1 if side == 0 else 0].astype(jnp.float32)
        info_send[side, pl.ds(2 * CX, 8)] = jnp.full((8, NR), kind, jnp.float32)
    for copy in loads[1:5]:
        copy.wait()

    def update(field, result, result_offset, factor, t, h):
        freq = base_frequency * (h + 1).astype(jnp.float32)
        bases = [pl.multiple_of((t + j) * CX, CX) for j in range(BLOCK)]
        kind = stagger[t // CPP]
        damps = [2.0 * sigma[pl.ds(base, CX)] + 12.0 * viscosity for base in bases]
        groups = [(j, p) for j in range(BLOCK) for p in range(2)]
        flux = {g: [None] * V for g in groups}
        for w in range(V):
            values = {}
            for j, p in groups:
                f = h * F + p * V + w
                u, tm, tp = [field[f, pl.ds(bases[j] + k * CX, CX)] for k in (1, 0, 2)]
                xm = jnp.where(first_row, 0.0, pltpu.roll(u, 1, 0))
                xp = jnp.where(last_row, 0.0, pltpu.roll(u, CX - 1, 0))
                rm = jnp.where(first_lane, 0.0, pltpu.roll(u, 1, 1))
                rp = jnp.where(last_lane, 0.0, pltpu.roll(u, NR - 1, 1))
                sums = ((tp + tm) + (xp + xm)) + (rp + rm)
                values[j, p] = (u, tp - tm, xp - xm, rp - rm, sums)
            for v in range(V):
                at, ax, ar = a_theta[v, kind, w], a_axial[v, w], a_radial[v, w]
                for j, p in groups:
                    u, dth, dx, dr, sums = values[j, p]
                    term = at * dth + ax * dx + ar * dr
                    if v == w:
                        turned = 2.0 * freq if p == 1 else -2.0 * freq
                        term = term + (damps[j] * u - (2.0 * viscosity) * sums)
                        term = term + turned * values[j, 1 - p][0]
                    old = flux[j, p][v]
                    flux[j, p][v] = term if old is None else old + term
        for j, p in groups:
            dt = factor * step[pl.ds(bases[j], CX)]
            half = 0.5 * dt
            for v in range(V):
                f = h * F + p * V + v
                start = state[f, pl.ds(bases[j] + CX, CX)] + dt * source[f, pl.ds(bases[j], CX)]
                result[f, pl.ds(bases[j] + result_offset, CX)] = start - half * flux[j, p][v]

    def halo_terms(values, matrix, sign):
        terms = []
        for v in range(V):
            total = matrix(v, 0) * values[0]
            for w in range(1, V):
                total = total + matrix(v, w) * values[w]
            terms.append((sign * 0.5) * total - viscosity * values[v])
        return terms

    def each_terms(values, matrix, sign, use):
        for v in range(V):
            totals = [0.0] * len(values)
            for w in range(V):
                entry = (sign * 0.5) * matrix(v, w)
                if v == w:
                    entry = entry - viscosity
                for i, value in enumerate(values):
                    totals[i] = totals[i] + entry * value[w]
            for i, total in enumerate(totals):
                use(i * V + v, total)

    def grouped(read):
        return [[read(hp * V + w) for w in range(V)] for hp in range(HP)]

    G = 8

    def edge_values(side):
        t, beyond = (CT - 1, CT - 2) if side == 0 else (0, 1)
        kind = stagger[t // CPP]
        sign_t = -1.0 if side == 0 else 1.0

        def fill(b):
            x, inner = (0, 1) if b == 0 else (CX - 1, CX - 2)
            for w in range(V):
                at = pl.ds(w, HP, stride=V)
                pitch = CT * CX + 2 * CX
                for target, row in (
                    (crit_send.at[side, 0], CX + t * CX + x),
                    (crit_send.at[side, 1], CX + t * CX + inner),
                    (beside.at[0], CX + beyond * CX + x),
                ):
                    target[at] = state_rows[pl.ds(w * pitch + row, HP, stride=V * pitch)]
                pitch = CT * CX
                beside[1, at] = source_rows[
                    pl.ds(w * pitch + t * CX + x, HP, stride=V * pitch)
                ]
            packed = [pl.ds(w, G, stride=V) for w in range(V)]
            edge = [crit_send[side, 0, at] for at in packed]
            near = [crit_send[side, 1, at] for at in packed]
            after = [beside[0, at] for at in packed]
            force = [beside[1, at] for at in packed]
            rows = lax.broadcasted_iota(jnp.int32, (G, NR), 0)
            lanes = lax.broadcasted_iota(jnp.int32, (G, NR), 1)
            odd = rows % 2 == 1
            freq = base_frequency * (rows // 2 + 1).astype(jnp.float32)
            freq = jnp.where(odd, freq, -freq)
            slopes, sums = [], []
            for w in range(V):
                rm = jnp.where(lanes == 0, 0.0, pltpu.roll(edge[w], 1, 1))
                rp = jnp.where(lanes == NR - 1, 0.0, pltpu.roll(edge[w], NR - 1, 1))
                slopes.append(rp - rm)
                sums.append(rp + rm)
            along_t = halo_terms(after, lambda v, w: a_theta[v, kind, w], sign_t)
            along_x = halo_terms(near, lambda v, w: a_axial[v, w], 1.0 if b == 0 else -1.0)
            at = pl.ds(t * CX + x, 1)
            damp = jnp.broadcast_to(sigma[at] + 6.0 * viscosity, (G, NR))
            dt = jnp.broadcast_to(0.5 * step[at], (G, NR))
            for v in range(V):
                total = a_radial[v, 0] * slopes[0]
                for w in range(1, V):
                    total = total + a_radial[v, w] * slopes[w]
                swapped = jnp.where(odd, pltpu.roll(edge[v], 1, 0), pltpu.roll(edge[v], G - 1, 0))
                res = 0.5 * total - viscosity * sums[v] + along_t[v] + along_x[v]
                res = res + damp * edge[v] + freq * swapped - force[v]
                crit_send[side, 2, packed[v]] = edge[v] - dt * res

        @pl.when(jnp.logical_not(has_lo))
        def _():
            fill(0)

        @pl.when(jnp.logical_not(has_hi))
        def _():
            fill(1)

    def open_sends():
        pl.semaphore_wait(barrier, greeters)

        @pl.when(on_plane & (th == T - 1))
        def _():
            crit_copy(0).start()

        @pl.when(on_plane & (th > 0))
        def _():
            crit_copy(1).start()

        info_copy(0).start()

        @pl.when(th > 0)
        def _():
            info_copy(1).start()

    def line_sends():
        for side in range(2):

            def _():
                x = CX - 1 if side == 0 else 0
                for f in range(HF):
                    xusend[side, f] = state[f, x_rows(CX + x), :]
                xinfo_send[side] = sigma[x_rows(x), :]
                x_copy(XU, side).start()
                x_copy(XINFO, side).start()

            when_x_target(side, _)

    def u_sends():
        @pl.when(th > 0)
        def _():
            u_copy(1).start()

        u_copy(0).start()

    def edge_sends():
        for side in range(2):
            rows = pl.ds(CX + ((CT - 1) * CX if side == 0 else 0), CX)
            fsend[side] = first[:, rows].reshape(HF * CX, NR)
        @pl.when(th == T - 1)
        def _():
            first_copy(0).start()

        for side in range(2):

            def _():
                x = CX - 1 if side == 0 else 0
                for t_side in range(2):
                    row = CX + ((CT - 1) * CX if t_side == 0 else 0) + x
                    for f in range(HF):
                        corner_send[t_side, side, pl.ds(f, 1)] = state[f, pl.ds(row, 1)]
                corner_copy(0, side).start()

                @pl.when(th > 0)
                def _():
                    corner_copy(1, side).start()

            when_x_target(side, _)

    def tables():
        for h in range(H):
            chosen = (mode_order[pl.ds(h, 1)] == order_id).astype(jnp.float32)
            picked = jnp.dot(
                waves, chosen.astype(jnp.bfloat16), preferred_element_type=jnp.float32
            )
            picked = picked[: 2 * PR] + picked[2 * PR : 4 * PR] + picked[4 * PR :]
            cosines[h] = picked[:PR]
            sines[h] = picked[PR:]
            chosen = (mode_radial[pl.ds(h, 1)] == radial_id).astype(jnp.float32)
            phi[h] = dot(phi_table, chosen, (((0,), (0,)), ((), ())))
            phi_high[h] = phi[h].astype(jnp.bfloat16)
            phi_low[h] = (phi[h] - phi_high[h].astype(jnp.float32)).astype(jnp.bfloat16)

    for side in (1, 0):
        edge_values(side)
    blocks = CT // BLOCK
    early = (th < 2) & (xr == 0)
    open_at = jnp.where(early, blocks, 0)
    edge_at = jnp.where(early, blocks, 2)

    @pl.loop(0, blocks + 1)
    def _(i):
        pl.when(i == open_at)(open_sends)

        @pl.when(i == 0)
        def _():
            for copy in loads[5:]:
                copy.wait()

        pl.when(i == open_at)(line_sends)
        pl.when(i == jnp.where(early, blocks, 1))(u_sends)
        pl.when(i == 1)(tables)
        pl.when(i == edge_at)(edge_sends)

        @pl.when(i < blocks)
        def _():
            t = BLOCK * jnp.where(i == 0, 0, jnp.where(i == 1, blocks - 1, i - 1))

            @pl.loop(0, H)
            def _(h):
                update(state, first, CX, 0.5, t, h)

    for side in range(2):

        def _():
            x = CX - 1 if side == 0 else 0
            for f in range(HF):
                xfsend[side, pl.ds(f * CT, CT)] = first[f, x_rows(CX + x), :]
            x_copy(XF, side).start()

        when_x_target(side, _)

    def own_planes(b):
        x = 0 if b == 0 else CX - 1
        inner = 1 if b == 0 else CX - 2
        lines = lax.broadcasted_iota(jnp.int32, (CT, NR), 0)
        lanes = lax.broadcasted_iota(jnp.int32, (CT, NR), 1)
        top, bottom = lines == 0, lines == CT - 1
        left, right = lanes == 0, lanes == NR - 1
        ls, gxs, grs, gts = [], [], [], []
        for w in range(V):
            ls.append(l_rows[b, w])
            gx = gr = 0.0
            for v in range(V):
                gx = gx + l_rows[b, v] * a_axial[v, w]
                gr = gr + l_rows[b, v] * a_radial[v, w]
            gt = None
            for k in range(NPASS):
                row = 0.0
                for v in range(V):
                    row = row + l_rows[b, v] * a_theta[v, stagger[k], w]
                gt = row if gt is None else jnp.where(lines >= k * CPP, row, gt)
            gxs.append(gx)
            grs.append(gr)
            gts.append(gt)
        damp = sigma[x_rows(x), :] + 6.0 * viscosity
        dt = step[x_rows(x), :]

        @pl.loop(0, H)
        def _(h):
            freq = base_frequency * (h + 1).astype(jnp.float32)
            fields = [0.0, 0.0]
            rest = []
            for p in range(2):
                along_t = start = forcing = inside = radial = 0.0
                flux = sums = 0.0
                for w in range(V):
                    f = h * F + p * V + w
                    u = first[f, x_rows(CX + x), :]
                    near = first[f, x_rows(CX + inner), :]
                    tm = jnp.where(top, 0.0, pltpu.roll(u, 1, 0))
                    tp = jnp.where(bottom, 0.0, pltpu.roll(u, CT - 1, 0))
                    dx = near if b == 0 else -near
                    flux = flux + (gts[w] * (tp - tm) + gxs[w] * dx)
                    sums = sums + ls[w] * ((tp + tm) + near)
                    fields[p] = fields[p] + ls[w] * u
                    radial = radial + grs[w] * u
                    forcing = forcing + ls[w] * source[f, x_rows(x), :]
                    start = start + ls[w] * state[f, x_rows(CX + x), :]
                for value, weight, sign in ((radial, 0.5, -1.0), (fields[p], -viscosity, 1.0)):
                    rm = jnp.where(left, 0.0, pltpu.roll(value, 1, 1))
                    rp = jnp.where(right, 0.0, pltpu.roll(value, NR - 1, 1))
                    inside = inside + weight * (rp + sign * rm)
                res = 0.5 * flux - viscosity * sums + inside + damp * fields[p] - forcing
                rest.append((start, res))
            for p in range(2):
                start, res = rest[p]
                turned = -freq if p == 0 else freq
                res = res + turned * fields[1 - p]
                at = pl.ds(pl.multiple_of((2 * h + p) * PR, PR), CT)
                planes[at] = start - dt * res

    @pl.when(jnp.logical_not(has_lo))
    def _():
        own_planes(0)

    @pl.when(jnp.logical_not(has_hi))
    def _():
        own_planes(1)

    def ghosts(side):
        info_copy(side).wait_recv()
        ghost_step[side] = courant / (1.0 + info[side, pl.ds(0, 2 * CX)])
        kind = info[side, pl.ds(2 * CX, 8)]
        masks = [kind == float(k) for k in range(a_theta.shape[1])]
        for v in range(V):
            for w in range(V):
                entry = jnp.zeros((8, NR), jnp.float32)
                for k, mask in enumerate(masks):
                    entry = jnp.where(mask, a_theta[v, k, w], entry)
                ghost_matrix[side, v * V + w] = entry

    def crossed(side):
        return ((side == 1) & (th < T - 1)) | ((side == 0) & (th == 0))

    for side in (1, 0):
        pl.when(crossed(side))(lambda: ghosts(side))

    @pl.when(th == 0)
    def _():
        info_copy(1).start()
        u_copy(1).start()
        first_copy(1).start()
        for side in range(2):
            when_x_target(side, lambda: corner_copy(1, side).start())

    def cross(b, side):
        sign = 1.0 if side == 1 else -1.0
        x = 0 if b == 0 else CX - 1
        inner = 1 if b == 0 else CX - 2
        own_edge, own_next = (CT - 1, CT - 2) if side == 1 else (0, 1)
        ghost_edge, ghost_next = (CT, CT + 1) if side == 1 else (CT + 2, CT + 3)
        kind = stagger[own_edge // CPP]
        def rows_of(ref, which, j):
            return [ref[which, j, pl.ds(w, G, stride=V)] for w in range(V)]

        own_u, own_in, own_first = [rows_of(crit_send, 1 - side, j) for j in range(3)]
        ghost_u, ghost_in, ghost_first = [rows_of(crit, side, j) for j in range(3)]

        def wide(row):
            return jnp.broadcast_to(row, (G, NR))

        own_dt = wide(step[pl.ds(own_edge * CX + x, 1)])
        own_in_dt = wide(step[pl.ds(own_edge * CX + inner, 1)])
        own_next_dt = wide(step[pl.ds(own_next * CX + x, 1)])
        own_sigma = wide(sigma[pl.ds(own_edge * CX + x, 1)])
        ghost_dt = wide(ghost_step[side, pl.ds(x, 1)])
        ghost_in_dt = wide(ghost_step[side, pl.ds(inner, 1)])
        ghost_next_dt = wide(ghost_step[side, pl.ds(CX + x, 1)])
        ghost_sigma = wide(info[side, pl.ds(x, 1)])

        def own_matrix(v, w):
            return a_theta[v, kind, w]

        matrix = [[ghost_matrix[side, v * V + w] for w in range(V)] for v in range(V)]

        def changes(values, matrix, sign, dt):
            return [(-0.5 * dt) * term for term in halo_terms(values, matrix, sign)]

        def other_matrix(v, w):
            return matrix[v][w]

        own_d = changes(ghost_u, own_matrix, sign, own_dt)
        own_in_d = changes(ghost_in, own_matrix, sign, own_in_dt)
        ghost_d = changes(own_u, other_matrix, -sign, ghost_dt)
        ghost_in_d = changes(own_in, other_matrix, -sign, ghost_in_dt)
        ls = [l_rows[b, w] for w in range(V)]

        def contract(weights, values):
            total = weights[0] * values[0]
            for w in range(1, V):
                total = total + weights[w] * values[w]
            return total

        def column(matrix, w):
            total = ls[0] * matrix(0, w)
            for v in range(1, V):
                total = total + ls[v] * matrix(v, w)
            return total

        own_w = [(sign * 0.5) * column(own_matrix, w) - viscosity * ls[w] for w in range(V)]
        ghost_w = [(-sign * 0.5) * column(other_matrix, w) - viscosity * ls[w] for w in range(V)]
        flip = 0.5 if b == 0 else -0.5
        near_w = [
            flip * column(lambda v, w: a_axial[v, w], w) - viscosity * ls[w] for w in range(V)
        ]
        radial_w = [column(lambda v, w: a_radial[v, w], w) for w in range(V)]
        rows = lax.broadcasted_iota(jnp.int32, (G, NR), 0)
        lanes = lax.broadcasted_iota(jnp.int32, (G, NR), 1)
        odd = rows % 2 == 1
        freq = base_frequency * (rows // 2 + 1).astype(jnp.float32)
        freq = jnp.where(odd, freq, -freq)
        left, right = lanes == 0, lanes == NR - 1

        def local(d, d_in, damping):
            radial = contract(radial_w, d)
            fields = contract(ls, d)
            swapped = jnp.where(odd, pltpu.roll(fields, 1, 0), pltpu.roll(fields, G - 1, 0))
            total = contract(near_w, d_in) + freq * swapped
            total = total + (damping + 6.0 * viscosity) * fields
            for value, weight, sign in ((radial, 0.5, -1.0), (fields, -viscosity, 1.0)):
                rm = jnp.where(left, 0.0, pltpu.roll(value, 1, 1))
                rp = jnp.where(right, 0.0, pltpu.roll(value, NR - 1, 1))
                total = total + weight * (rp + sign * rm)
            return total

        total_ghost = [a + d for a, d in zip(ghost_first, ghost_d)]
        total_own = [a + d for a, d in zip(own_first, own_d)]
        found = {
            own_next: own_next_dt * contract(own_w, own_d),
            own_edge: own_dt * (local(own_d, own_in_d, own_sigma) + contract(own_w, total_ghost)),
            ghost_edge: ghost_dt
            * (local(ghost_d, ghost_in_d, ghost_sigma) + contract(ghost_w, total_own)),
            ghost_next: ghost_next_dt * contract(ghost_w, ghost_d),
        }
        for row, value in found.items():
            at = pl.ds(row, HP, stride=PR)
            planes[at, :] = planes[at, :] - value[:HP]

    def project(b):
        for h in range(H):
            projected = dot(planes[pl.ds(2 * h * PR, 2 * PR)], phi[h])
            real, imag = projected[:PR], projected[PR:]
            weight = jnp.where(mode_plane[pl.ds(h, 1)] == b, scale, 0.0)
            part_real = jnp.sum(real * cosines[h] + imag * sines[h], axis=0, keepdims=True)
            part_imag = jnp.sum(imag * cosines[h] - real * sines[h], axis=0, keepdims=True)
            part[pl.ds(2 * h, 1)] = weight * part_real
            part[pl.ds(2 * h + 1, 1)] = weight * part_imag

    def finish_plane(b):
        @pl.when(th < T - 1)
        def _():
            crit_copy(1).wait_recv()
            cross(b, 1)

        @pl.when(th == 0)
        def _():
            crit_copy(0).wait_recv()
            cross(b, 0)

        project(b)

    @pl.when(jnp.logical_not(has_lo))
    def _():
        finish_plane(0)

    @pl.when(jnp.logical_not(has_hi))
    def _():
        finish_plane(1)

    def share(sem, t, x):
        pltpu.make_async_remote_copy(
            src_ref=part.at[pl.ds(0, HP)],
            dst_ref=parts.at[me, pl.ds(0, HP)],
            send_sem=psend_sem,
            recv_sem=sem,
            device_id=(t, x),
            device_id_type=MESH,
        ).start()

    shift = jnp.where(th < Q, Q, 0)

    @pl.when(th > 0)
    def _():
        ordered(shift, functools.partial(share, precv_sem))

    @pl.when(th == 0)
    def _():
        late_first(functools.partial(share, zrecv_sem))


    @pl.when(th > 0)
    def _():
        first_copy(1).start()

    @pl.when(th < T - 1)
    def _():
        first_copy(0).start()

    parts[me] = part[...]
    for side in (0, 1):
        pl.when(jnp.logical_not(crossed(side)))(lambda: ghosts(side))

    for side in range(2):

        def _():
            x_copy(XU, side).wait_recv()
            x = 0 if side == 0 else CX - 1
            dt = 0.5 * step[x_rows(x), :]

            def use(f, term):
                at = (f, x_rows(CX + x), slice(None))
                first[at] = first[at] - dt * term

            sign = -1.0 if side == 0 else 1.0
            each_terms(grouped(lambda f: xuhalo[side, f]), lambda v, w: a_axial[v, w], sign, use)

        when_x_source(side, _)

    def t_fix(side):
        u_copy(side).wait_recv()
        t = 0 if side == 0 else CT - 1
        kind = stagger[t // CPP]
        dt = 0.5 * step[pl.ds(t * CX, CX)]

        def use(f, term):
            at = (f, pl.ds(CX + t * CX, CX))
            first[at] = first[at] - dt * term

        sign = -1.0 if side == 0 else 1.0
        each_terms(grouped(lambda f: uhalo[side, f]), lambda v, w: a_theta[v, kind, w], sign, use)

    @pl.loop(0, blocks)
    def _(i):
        t = BLOCK * jnp.where(i + 1 >= blocks, i + 1 - blocks, i + 1)

        @pl.when(i == blocks - 2)
        def _():
            t_fix(1)

        @pl.when(i == blocks - 1)
        def _():
            t_fix(0)

        @pl.loop(0, H)
        def _(h):
            update(first, out, 0, 1.0, t, h)

    def corner_fix(side, x_side):
        corner_copy(side, x_side).wait_recv()
        t = 0 if side == 0 else CT - 1
        x = 0 if x_side == 0 else CX - 1
        kind = stagger[t // CPP]
        line_dt = 0.5 * courant / (1.0 + xinfo[x_side, pl.ds(t, 1)])
        edge_dt = 0.5 * ghost_step[side, pl.ds(x, 1)]

        values = [corner[side, x_side, pl.ds(w, 8, stride=V)] for w in range(V)]
        along_t = halo_terms(
            values, lambda v, w: a_theta[v, kind, w], -1.0 if side == 0 else 1.0
        )
        along_x = halo_terms(values, lambda v, w: a_axial[v, w], -1.0 if x_side == 0 else 1.0)
        for v in range(V):
            at = (x_side, pl.ds(v * CT + t, HP, stride=V * CT))
            xfhalo[at] = xfhalo[at] - (line_dt * along_t[v])[:HP]
            at = (side, pl.ds(v * CX + x, HP, stride=V * CX))
            fhalo[at] = fhalo[at] - (edge_dt * along_x[v])[:HP]

    def x_finish(side):
        x = 0 if side == 0 else CX - 1
        ghost_dt = 0.5 * courant / (1.0 + xinfo[side])
        dt = step[x_rows(x), :]
        away = -1.0 if side == 0 else 1.0

        ghosts = {}

        def keep(f, term):
            ghosts[f] = xfhalo[side, pl.ds(f * CT, CT)] - ghost_dt * term

        def use(f, term):
            at = (f, x_rows(x), slice(None))
            out[at] = out[at] - dt * term

        mine = grouped(lambda f: state[f, x_rows(CX + x), :])
        each_terms(mine, lambda v, w: a_axial[v, w], -away, keep)
        each_terms(grouped(lambda f: ghosts[f]), lambda v, w: a_axial[v, w], away, use)

    def t_finish(side):
        t = 0 if side == 0 else CT - 1
        kind = stagger[t // CPP]
        ghost_dt = 0.5 * ghost_step[side, pl.ds(0, CX)]
        dt = step[pl.ds(t * CX, CX)]
        away = -1.0 if side == 0 else 1.0

        values = {}

        def keep(f, term):
            values[f] = fhalo[side, pl.ds(f * CX, CX)] - ghost_dt * term

        def use(f, term):
            at = (f, pl.ds(t * CX, CX))
            out[at] = out[at] - dt * term

        mine = grouped(lambda f: state[f, pl.ds(CX + t * CX, CX)])
        each_terms(mine, lambda v, w: ghost_matrix[side, v * V + w], -away, keep)
        each_terms(grouped(lambda f: values[f]), lambda v, w: a_theta[v, kind, w], away, use)

    def shares(count, sem):
        return pltpu.make_async_remote_copy(
            src_ref=parts.at[pl.ds(0, count), pl.ds(0, HP)],
            dst_ref=parts.at[pl.ds(0, count), pl.ds(0, HP)],
            send_sem=psend_sem,
            recv_sem=sem,
            device_id=(up, xr),
            device_id_type=MESH,
        )

    def total_copy(j):
        return pltpu.make_async_remote_copy(
            src_ref=whole,
            dst_ref=whole,
            send_sem=wsend_sem.at[j],
            recv_sem=wrecv_sem,
            device_id=(th + Q + j * Q, xr),
            device_id_type=MESH,
        )

    serves = (th >= Q) & (th < 2 * Q)

    def gather(count):
        shares(count, precv_sem).wait_recv()
        total = parts[X]
        if N <= 64:
            for i in range(X + 1, N):
                total = total + parts[i]
        else:
            total = lax.fori_loop(X + 1, N, lambda i, acc: acc + parts[i], total)
        whole[...] = total

    @pl.when(serves)
    def _():
        gather(N - X - 1)
        for j in range(2):
            total_copy(j).start()

    for x_side in range(2):

        def _():
            x_copy(XF, x_side).wait_recv()
            x_copy(XINFO, x_side).wait_recv()

        when_x_source(x_side, _)
    for side in (1, 0):
        first_copy(side).wait_recv()
        for x_side in range(2):
            when_x_source(x_side, lambda: corner_fix(side, x_side))
        t_finish(side)
    for x_side in range(2):
        when_x_source(x_side, lambda: x_finish(x_side))

    @pl.when(th == 0)
    def _():
        gather(N - X)
        shares(X - 1, zrecv_sem).wait_recv()

    @pl.when(th > 0)
    def _():
        @pl.when(is_root & jnp.logical_not(serves))
        def _():
            gather(N - X - 1)

        @pl.when(jnp.logical_not(is_root))
        def _():
            total_copy(0).wait_recv()

        shares(X, zrecv_sem).wait_recv()

    total = whole[...]
    for x in range(X):
        total = total + parts[x]
    part_rows = [total[i : i + 1] for i in range(2 * H)]
    for h in range(H):
        for b in range(2):
            mine = mode_plane[pl.ds(h, 1)] == b
            for p in range(2):
                amps[h, b, pl.ds(p, 1)] = jnp.where(mine, part_rows[2 * h + p], 0.0)

    def correct(b, h):
        x = 0 if b == 0 else CX - 1
        weight = jnp.where(mode_plane[pl.ds(h, 1)] == b, scale, 0.0)
        real = weight * (part_rows[2 * h] - gust[h, pl.ds(0, 1)])
        imag = weight * (part_rows[2 * h + 1] - gust[h, pl.ds(1, 1)])
        cos, sin = cosines[h, pl.ds(0, CT)], sines[h, pl.ds(0, CT)]
        coef = jnp.concatenate(
            [real * cos - imag * sin, real * sin + imag * cos], axis=0
        )
        high = coef.astype(jnp.bfloat16)
        low = (coef - high.astype(jnp.float32)).astype(jnp.bfloat16)
        along = (((1,), (1,)), ((), ()))
        both = lax.dot_general(
            jnp.concatenate([high, low], axis=0),
            phi_high[h],
            along,
            preferred_element_type=jnp.float32,
        )
        q = both[: 2 * CT] + both[2 * CT :]
        q = q + lax.dot_general(
            high, phi_low[h], along, preferred_element_type=jnp.float32
        )
        for p in range(2):
            for v in range(V):
                at = (h * F + p * V + v, x_rows(x), slice(None))
                out[at] = out[at] - r_cols[b, v] * q[p * CT : (p + 1) * CT]

    @pl.when(jnp.logical_not(has_lo))
    def _():
        for h in range(H):
            correct(0, h)

    @pl.when(jnp.logical_not(has_hi))
    def _():
        for h in range(H):
            correct(1, h)

    @pl.when(th == 0)
    def _():
        shares(N - 1, precv_sem).wait_send()

    @pl.when((th > 0) & is_root)
    def _():
        shares(ROOTS * X - 1, precv_sem).wait_send()

    @pl.when(serves)
    def _():
        for j in range(2):
            total_copy(j).wait_send()

    @pl.when(jnp.logical_not(is_root))
    def _():
        shares(ROOTS * X, precv_sem).wait_send()

    @pl.when(on_plane & (th > 0))
    def _():
        crit_copy(1).wait_send()

    @pl.when(on_plane & (th == T - 1))
    def _():
        crit_copy(0).wait_send()

    for side in range(2):
        info_copy(side).wait_send()
        u_copy(side).wait_send()
        first_copy(side).wait_send()

        def _():
            for kind in (XU, XF, XINFO):
                x_copy(kind, side).wait_send()
            for t_side in range(2):
                corner_copy(t_side, side).wait_send()

        when_x_target(side, _)


def store_kernel(fields, amps, fields_out, amps_out, sems):
    copies = [
        pltpu.make_async_copy(fields, fields_out, sems.at[0]),
        pltpu.make_async_copy(amps, amps_out, sems.at[1]),
    ]
    for copy in copies:
        copy.start()
    for copy in copies:
        copy.wait()


def store(fields, amps):
    vmem = pl.BlockSpec(memory_space=pl.ANY)
    hbm = pl.BlockSpec(memory_space=pltpu.HBM)
    return pl.pallas_call(
        store_kernel,
        out_shape=tuple(jax.ShapeDtypeStruct(a.shape, a.dtype) for a in (fields, amps)),
        in_specs=(vmem, vmem),
        out_specs=(hbm, hbm),
        compiler_params=pltpu.CompilerParams(vmem_limit_bytes=2**20),
        scratch_shapes=[pltpu.SemaphoreType.DMA((2,))],
        name="store",
    )(fields, amps)


def local(T, X, *args):
    state, source, sigma, stagger = args[:4]
    H, two, V, CT, CX, NR = state.shape
    F = two * V
    HF = H * F
    NMODE = args[7].shape[1]
    dims = (T, X, H, V, CT, CX, NR, stagger.shape[0], NMODE)
    N = T * X
    rows = CT * CX
    f32 = jnp.float32
    hbm = pl.BlockSpec(memory_space=pl.ANY)
    vmem = pl.BlockSpec(memory_space=pltpu.VMEM)
    DMA = pltpu.SemaphoreType.DMA
    stagger, a_theta, a_axial, a_radial, orders, radial, planes, gust, l_rows, r_cols = args[3:]
    small = [stagger, jnp.swapaxes(a_theta, 0, 1), a_axial, a_radial, l_rows, r_cols]
    small += [orders, radial, planes, gust]
    pad = -(-2 * H // 8) * 8
    sides = [
        (HF, CX, NR),
        (HF * CX, NR),
        (HF * CX, NR),
        (HF, CT, NR),
        (HF, CT, NR),
        (HF * CT, NR),
        (HF * CT, NR),
        (CT, NR),
        (CT, NR),
        (2, 8 * V, NR),
        (2, 8 * V, NR),
        (3, 8 * V, NR),
        (3, 8 * V, NR),
        (2 * CX + 8, NR),
        (2 * CX + 8, NR),
        (2 * CX, NR),
        (V * V, 8, NR),
    ]
    fields, amplitudes = pl.pallas_call(
        functools.partial(kernel, dims),
        out_shape=(
            jax.ShapeDtypeStruct((HF, rows, NR), f32),
            jax.ShapeDtypeStruct((H, 2, 2, NMODE), f32),
        ),
        in_specs=[hbm] * 13,
        out_specs=(vmem, vmem),
        scratch_shapes=[pltpu.SMEM(a.shape, a.dtype) for a in small[:6]]
        + [pltpu.VMEM(a.shape, a.dtype) for a in small[6:]]
        + [
            pltpu.VMEM((HF, rows + 2 * CX, NR), f32),
            pltpu.VMEM((HF, rows, NR), f32),
            pltpu.VMEM((rows, NR), f32),
            pltpu.VMEM((HF, rows + 2 * CX, NR), f32),
            pltpu.VMEM((rows, NR), f32),
        ]
        + [pltpu.VMEM((2, *shape), f32) for shape in sides]
        + [
            pltpu.VMEM((2 * H * 2 * CT, NR), f32),
            pltpu.VMEM((2, 8 * V, NR), f32),
            pltpu.VMEM((H, NR, NMODE), f32),
            pltpu.VMEM((H, NR, NMODE), jnp.bfloat16),
            pltpu.VMEM((H, NR, NMODE), jnp.bfloat16),
            pltpu.VMEM((H, 2 * CT, NMODE), f32),
            pltpu.VMEM((H, 2 * CT, NMODE), f32),
            pltpu.VMEM((pad, NMODE), f32),
            pltpu.VMEM((N, pad, NMODE), f32),
            DMA((7,)),
            DMA((10,)),
            DMA((7, 2)),
            DMA((7, 2)),
            DMA((2, 2)),
            DMA((2, 2)),
            DMA,
            DMA,
            pltpu.VMEM((pad, NMODE), f32),
            DMA((2,)),
            DMA,
            DMA,
        ],
        compiler_params=pltpu.CompilerParams(
            collective_id=0, has_side_effects=True, vmem_limit_bytes=16 * 2**20
        ),
        name="wake",
    )(
        *(pltpu.with_memory_space_constraint(a, pltpu.HBM) for a in (state.reshape(HF, rows, NR),
        source.reshape(HF, rows, NR),
        sigma.reshape(rows, NR),
        *small)),
    )
    fields, amplitudes = store(fields, amplitudes)
    return fields.reshape(state.shape), amplitudes


def solution(mesh):
    field = P(None, None, None, "theta", "xr", None)
    placed = (field, field, P("theta", "xr", None), P("theta")) + (P(),) * 9
    return jax.shard_map(
        functools.partial(local, mesh.shape["theta"], mesh.shape["xr"]),
        mesh=mesh,
        in_specs=placed,
        out_specs=(field, P()),
        check_vma=False,
    )
```

```python
import functools
import math

import jax
import jax.numpy as jnp
from jax import lax
from jax.experimental import pallas as pl
from jax.experimental.pallas import tpu as pltpu
from jax.sharding import PartitionSpec as P

courant = 0.5
viscosity = 0.1
base_frequency = 0.5
highest = lax.Precision.HIGHEST
MESH = pl.DeviceIdType.MESH


def kernel(
    dims,
    state_hbm,
    source_hbm,
    sigma_hbm,
    *refs,
):
    small_hbm, refs = refs[:10], refs[10:]
    out, amps, refs = refs[0], refs[1], refs[2:]
    small, refs = refs[:10], refs[10:]
    stagger, a_theta, a_axial, a_radial, l_rows, r_cols = small[:6]
    mode_order, mode_radial, mode_plane, gust = small[6:]
    (
        state,
        source,
        sigma,
        first,
        step,
        uhalo,
        fhalo,
        fsend,
        xuhalo,
        xusend,
        xfhalo,
        xfsend,
        xinfo,
        xinfo_send,
        corner,
        corner_send,
        crit,
        crit_send,
        info,
        info_send,
        ghost_step,
        ghost_matrix,
        planes,
        beside,
        phi,
        phi_high,
        phi_low,
        cosines,
        sines,
        part,
        parts,
        load_sem,
        small_sem,
        send_sem,
        recv_sem,
        csend_sem,
        crecv_sem,
        psend_sem,
        precv_sem,
        whole,
        wsend_sem,
        wrecv_sem,
        zrecv_sem,
    ) = refs
    T, X, H, V, CT, CX, NR, NPASS, NMODE = dims
    F = 2 * V
    HF = H * F
    CPP = CT // NPASS
    N = T * X
    HP = 2 * H
    PR = 2 * CT
    th = lax.axis_index("theta")
    xr = lax.axis_index("xr")
    me = th * X + xr
    up = lax.rem(th + 1, T)
    down = lax.rem(th + T - 1, T)
    has_lo = xr > 0
    has_hi = xr < X - 1
    on_plane = jnp.logical_not(has_lo & has_hi)
    total_theta = CT * T
    scale = 1.0 / math.sqrt(total_theta * NR)
    U, FIRST, INFO, CRIT, XU, XF, XINFO = range(7)

    barrier = pltpu.get_barrier_semaphore()

    Q = T // 4
    ROOTS = 2 * Q
    is_root = th < ROOTS

    def for_others(count, act):
        def ring(t):
            for x in range(X):

                @pl.when((t != th) | (x != xr))
                def _():
                    act(t, x)

        if count * X <= 64:
            for t in range(count):
                ring(t)
        else:
            pl.loop(0, count)(ring)

    def ordered(shift, act):
        def ring(i):
            t = lax.rem(i + shift, ROOTS)
            for x in range(X):

                @pl.when((t != th) | (x != xr))
                def _():
                    act(t, x)

        if ROOTS * X <= 64:
            for i in range(ROOTS):
                ring(i)
        else:
            pl.loop(0, ROOTS)(ring)

    def late_first(act):
        def ring(i):
            for x in range(X):

                @pl.when((i != 0) | (x != xr))
                def _():
                    act(lax.rem(T - i, T) if N > 64 else (T - i) % T, x)

        if N <= 64:
            for i in range(T):
                ring(i)
        else:
            pl.loop(0, T)(ring)

    def greet(t, x):
        pl.semaphore_signal(barrier, inc=1, device_id=(t, x), device_id_type=MESH)

    def greet_all():
        greeters = ROOTS * X - is_root.astype(jnp.int32)
        for dt in (-1, 0, 1):
            for dx in (-1, 0, 1):
                t, x = th + dt, xr + dx
                inside = (t >= 0) & (t < T) & (x >= 0) & (x < X)
                if dt or dx:
                    greeters += (inside & (t >= ROOTS)).astype(jnp.int32)
                    pl.when(inside & jnp.logical_not(is_root))(lambda: greet(t, x))

        @pl.when(is_root)
        def _():
            for_others(T, greet)

        @pl.when(jnp.logical_not(is_root))
        def _():
            for x in range(X):
                greet(0, x)

        return jnp.where(th == 0, N - 1, greeters)

    little = [
        pltpu.make_async_copy(src, dst, small_sem.at[i])
        for i, (src, dst) in enumerate(zip(small_hbm, small))
    ]
    def span(source_ref, target, offset, start, count, sem):
        return pltpu.make_async_copy(
            source_ref.at[:, pl.ds(start * CX, count * CX)],
            target.at[:, pl.ds(offset + start * CX, count * CX)],
            load_sem.at[sem],
        )

    loads = [
        pltpu.make_async_copy(sigma_hbm, sigma, load_sem.at[0]),
        span(state_hbm, state, CX, 0, 2, 1),
        span(source_hbm, source, 0, 0, 1, 2),
        span(state_hbm, state, CX, CT - 2, 2, 3),
        span(source_hbm, source, 0, CT - 1, 1, 4),
        span(state_hbm, state, CX, 2, CT - 4, 5),
        span(source_hbm, source, 0, 1, CT - 2, 6),
    ]
    for copy in loads[:1] + little + loads[1:]:
        copy.start()
    greeters = greet_all()

    zero = jnp.zeros((HF, CX, NR), jnp.float32)
    for buf in (state, first):
        buf[:, pl.ds(0, CX)] = zero
        buf[:, pl.ds(CX + CT * CX, CX)] = zero
    planes[...] = jnp.zeros_like(planes)
    part[...] = jnp.zeros_like(part)
    crit_rows = -(-HF // 8) * 8
    crit_send[...] = jnp.zeros_like(crit_send)
    beside[...] = jnp.zeros_like(beside)
    state_rows = state.reshape(HF * (CT + 2) * CX, NR)
    source_rows = source.reshape(HF * CT * CX, NR)
    if crit.shape[2] > crit_rows:
        rest = crit.shape[2] - crit_rows
        crit[:, :, pl.ds(crit_rows, rest)] = jnp.zeros((2, 3, rest, NR), jnp.float32)

    def x_rows(row):
        return pl.ds(row, CT, stride=CX)

    def neighbour(side):
        return (up if side == 0 else down, xr)

    def message(kind, side, src, dst, target):
        return pltpu.make_async_remote_copy(
            src_ref=src,
            dst_ref=dst,
            send_sem=send_sem.at[kind, side],
            recv_sem=recv_sem.at[kind, side],
            device_id=target,
            device_id_type=MESH,
        )

    def u_copy(side):
        rows = pl.ds(CX + ((CT - 1) * CX if side == 0 else 0), CX)
        return message(U, side, state.at[:, rows], uhalo.at[side], neighbour(side))

    def first_copy(side):
        return message(FIRST, side, fsend.at[side], fhalo.at[side], neighbour(side))

    def info_copy(side):
        return message(INFO, side, info_send.at[side], info.at[side], neighbour(side))

    def crit_copy(side):
        rows = pl.ds(0, crit_rows)
        return message(
            CRIT, side, crit_send.at[side, :, rows], crit.at[side, :, rows], neighbour(side)
        )

    def x_neighbour(side):
        return (th, xr + 1 if side == 0 else xr - 1)

    def x_copy(kind, side):
        src, dst = {
            XU: (xusend, xuhalo),
            XF: (xfsend, xfhalo),
            XINFO: (xinfo_send, xinfo),
        }[kind]
        return message(kind, side, src.at[side], dst.at[side], x_neighbour(side))

    def corner_copy(side, x_side):
        return pltpu.make_async_remote_copy(
            src_ref=corner_send.at[side, x_side, pl.ds(0, crit_rows)],
            dst_ref=corner.at[side, x_side, pl.ds(0, crit_rows)],
            send_sem=csend_sem.at[side, x_side],
            recv_sem=crecv_sem.at[side, x_side],
            device_id=(up if side == 0 else down, xr + 1 if x_side == 0 else xr - 1),
            device_id_type=MESH,
        )

    def when_x_target(side, act):
        pl.when(has_hi if side == 0 else has_lo)(act)

    def when_x_source(side, act):
        pl.when(has_lo if side == 0 else has_hi)(act)

    row_id = lax.broadcasted_iota(jnp.int32, (CX, NR), 0)
    lane_id = lax.broadcasted_iota(jnp.int32, (CX, NR), 1)
    first_row = row_id == 0
    last_row = row_id == CX - 1
    first_lane = lane_id == 0
    last_lane = lane_id == NR - 1

    BLOCK = 2
    SPAN = 128
    cells = lax.broadcasted_iota(jnp.int32, (PR, SPAN), 0)
    cells = th * CT + jnp.where(cells >= CT + 2, CT + 1 - cells, cells)
    orders = lax.broadcasted_iota(jnp.int32, (PR, SPAN), 1) - SPAN // 2
    turns = (orders * cells).astype(jnp.float32)
    turns = turns - jnp.floor(turns / total_theta) * total_theta
    angle = (2.0 * math.pi) * turns / total_theta
    def thirds(a):
        high = a.astype(jnp.bfloat16)
        rest = a - high.astype(jnp.float32)
        middle = rest.astype(jnp.bfloat16)
        low = (rest - middle.astype(jnp.float32)).astype(jnp.bfloat16)
        return jnp.concatenate([high, middle, low], axis=0)

    waves = thirds(jnp.concatenate([jnp.cos(angle), jnp.sin(angle)], axis=0))
    radial = lax.broadcasted_iota(jnp.int32, (8, NR), 0)
    radial_pos = lax.broadcasted_iota(jnp.int32, (8, NR), 1).astype(jnp.float32) + 0.5
    phi_table = jnp.where(
        radial == 0,
        1.0,
        math.sqrt(2.0) * jnp.cos(math.pi * radial.astype(jnp.float32) * radial_pos / NR),
    )

    def dot(a, b, dims=(((1,), (0,)), ((), ()))):
        return lax.dot_general(
            a, b, dims, precision=highest, preferred_element_type=jnp.float32
        )

    for copy in little:
        copy.wait()
    order_id = lax.broadcasted_iota(jnp.int32, (SPAN, NMODE), 0) - SPAN // 2
    radial_id = lax.broadcasted_iota(jnp.int32, (8, NMODE), 0)
    loads[0].wait()
    step[...] = courant / (1.0 + sigma[...])
    for side in range(2):
        edge, second = (CT - 1, CT - 2) if side == 0 else (0, 1)
        info_send[side, pl.ds(0, CX)] = sigma[pl.ds(edge * CX, CX)]
        info_send[side, pl.ds(CX, CX)] = sigma[pl.ds(second * CX, CX)]
        kind = stagger[NPASS - 1 if side == 0 else 0].astype(jnp.float32)
        info_send[side, pl.ds(2 * CX, 8)] = jnp.full((8, NR), kind, jnp.float32)
    for copy in loads[1:5]:
        copy.wait()

    def update(field, result, result_offset, factor, t, h):
        freq = base_frequency * (h + 1).astype(jnp.float32)
        bases = [pl.multiple_of((t + j) * CX, CX) for j in range(BLOCK)]
        kind = stagger[t // CPP]
        damps = [2.0 * sigma[pl.ds(base, CX)] + 12.0 * viscosity for base in bases]
        groups = [(j, p) for j in range(BLOCK) for p in range(2)]
        flux = {g: [None] * V for g in groups}
        for w in range(V):
            values = {}
            for j, p in groups:
                f = h * F + p * V + w
                u, tm, tp = [field[f, pl.ds(bases[j] + k * CX, CX)] for k in (1, 0, 2)]
                xm = jnp.where(first_row, 0.0, pltpu.roll(u, 1, 0))
                xp = jnp.where(last_row, 0.0, pltpu.roll(u, CX - 1, 0))
                rm = jnp.where(first_lane, 0.0, pltpu.roll(u, 1, 1))
                rp = jnp.where(last_lane, 0.0, pltpu.roll(u, NR - 1, 1))
                sums = ((tp + tm) + (xp + xm)) + (rp + rm)
                values[j, p] = (u, tp - tm, xp - xm, rp - rm, sums)
            for v in range(V):
                at, ax, ar = a_theta[v, kind, w], a_axial[v, w], a_radial[v, w]
                for j, p in groups:
                    u, dth, dx, dr, sums = values[j, p]
                    term = at * dth + ax * dx + ar * dr
                    if v == w:
                        turned = 2.0 * freq if p == 1 else -2.0 * freq
                        term = term + (damps[j] * u - (2.0 * viscosity) * sums)
                        term = term + turned * values[j, 1 - p][0]
                    old = flux[j, p][v]
                    flux[j, p][v] = term if old is None else old + term
        for j, p in groups:
            dt = factor * step[pl.ds(bases[j], CX)]
            half = 0.5 * dt
            for v in range(V):
                f = h * F + p * V + v
                start = state[f, pl.ds(bases[j] + CX, CX)] + dt * source[f, pl.ds(bases[j], CX)]
                result[f, pl.ds(bases[j] + result_offset, CX)] = start - half * flux[j, p][v]

    def halo_terms(values, matrix, sign):
        terms = []
        for v in range(V):
            total = matrix(v, 0) * values[0]
            for w in range(1, V):
                total = total + matrix(v, w) * values[w]
            terms.append((sign * 0.5) * total - viscosity * values[v])
        return terms

    def each_terms(values, matrix, sign, use):
        for v in range(V):
            totals = [0.0] * len(values)
            for w in range(V):
                entry = (sign * 0.5) * matrix(v, w)
                if v == w:
                    entry = entry - viscosity
                for i, value in enumerate(values):
                    totals[i] = totals[i] + entry * value[w]
            for i, total in enumerate(totals):
                use(i * V + v, total)

    def grouped(read):
        return [[read(hp * V + w) for w in range(V)] for hp in range(HP)]

    G = 8

    def edge_values(side):
        t, beyond = (CT - 1, CT - 2) if side == 0 else (0, 1)
        kind = stagger[t // CPP]
        sign_t = -1.0 if side == 0 else 1.0

        def fill(b):
            x, inner = (0, 1) if b == 0 else (CX - 1, CX - 2)
            for w in range(V):
                at = pl.ds(w, HP, stride=V)
                pitch = CT * CX + 2 * CX
                for target, row in (
                    (crit_send.at[side, 0], CX + t * CX + x),
                    (crit_send.at[side, 1], CX + t * CX + inner),
                    (beside.at[0], CX + beyond * CX + x),
                ):
                    target[at] = state_rows[pl.ds(w * pitch + row, HP, stride=V * pitch)]
                pitch = CT * CX
                beside[1, at] = source_rows[
                    pl.ds(w * pitch + t * CX + x, HP, stride=V * pitch)
                ]
            packed = [pl.ds(w, G, stride=V) for w in range(V)]
            edge = [crit_send[side, 0, at] for at in packed]
            near = [crit_send[side, 1, at] for at in packed]
            after = [beside[0, at] for at in packed]
            force = [beside[1, at] for at in packed]
            rows = lax.broadcasted_iota(jnp.int32, (G, NR), 0)
            lanes = lax.broadcasted_iota(jnp.int32, (G, NR), 1)
            odd = rows % 2 == 1
            freq = base_frequency * (rows // 2 + 1).astype(jnp.float32)
            freq = jnp.where(odd, freq, -freq)
            slopes, sums = [], []
            for w in range(V):
                rm = jnp.where(lanes == 0, 0.0, pltpu.roll(edge[w], 1, 1))
                rp = jnp.where(lanes == NR - 1, 0.0, pltpu.roll(edge[w], NR - 1, 1))
                slopes.append(rp - rm)
                sums.append(rp + rm)
            along_t = halo_terms(after, lambda v, w: a_theta[v, kind, w], sign_t)
            along_x = halo_terms(near, lambda v, w: a_axial[v, w], 1.0 if b == 0 else -1.0)
            at = pl.ds(t * CX + x, 1)
            damp = jnp.broadcast_to(sigma[at] + 6.0 * viscosity, (G, NR))
            dt = jnp.broadcast_to(0.5 * step[at], (G, NR))
            for v in range(V):
                total = a_radial[v, 0] * slopes[0]
                for w in range(1, V):
                    total = total + a_radial[v, w] * slopes[w]
                swapped = jnp.where(odd, pltpu.roll(edge[v], 1, 0), pltpu.roll(edge[v], G - 1, 0))
                res = 0.5 * total - viscosity * sums[v] + along_t[v] + along_x[v]
                res = res + damp * edge[v] + freq * swapped - force[v]
                crit_send[side, 2, packed[v]] = edge[v] - dt * res

        @pl.when(jnp.logical_not(has_lo))
        def _():
            fill(0)

        @pl.when(jnp.logical_not(has_hi))
        def _():
            fill(1)

    def open_sends():
        pl.semaphore_wait(barrier, greeters)

        @pl.when(on_plane & (th == T - 1))
        def _():
            crit_copy(0).start()

        @pl.when(on_plane & (th > 0))
        def _():
            crit_copy(1).start()

        info_copy(0).start()

        @pl.when(th > 0)
        def _():
            info_copy(1).start()

    def line_sends():
        for side in range(2):

            def _():
                x = CX - 1 if side == 0 else 0
                for f in range(HF):
                    xusend[side, f] = state[f, x_rows(CX + x), :]
                xinfo_send[side] = sigma[x_rows(x), :]
                x_copy(XU, side).start()
                x_copy(XINFO, side).start()

            when_x_target(side, _)

    def u_sends():
        @pl.when(th > 0)
        def _():
            u_copy(1).start()

        u_copy(0).start()

    def edge_sends():
        for side in range(2):
            rows = pl.ds(CX + ((CT - 1) * CX if side == 0 else 0), CX)
            fsend[side] = first[:, rows].reshape(HF * CX, NR)
        @pl.when(th == T - 1)
        def _():
            first_copy(0).start()

        for side in range(2):

            def _():
                x = CX - 1 if side == 0 else 0
                for t_side in range(2):
                    row = CX + ((CT - 1) * CX if t_side == 0 else 0) + x
                    for f in range(HF):
                        corner_send[t_side, side, pl.ds(f, 1)] = state[f, pl.ds(row, 1)]
                corner_copy(0, side).start()

                @pl.when(th > 0)
                def _():
                    corner_copy(1, side).start()

            when_x_target(side, _)

    def tables():
        for h in range(H):
            chosen = (mode_order[pl.ds(h, 1)] == order_id).astype(jnp.float32)
            picked = jnp.dot(
                waves, chosen.astype(jnp.bfloat16), preferred_element_type=jnp.float32
            )
            picked = picked[: 2 * PR] + picked[2 * PR : 4 * PR] + picked[4 * PR :]
            cosines[h] = picked[:PR]
            sines[h] = picked[PR:]
            chosen = (mode_radial[pl.ds(h, 1)] == radial_id).astype(jnp.float32)
            phi[h] = dot(phi_table, chosen, (((0,), (0,)), ((), ())))
            phi_high[h] = phi[h].astype(jnp.bfloat16)
            phi_low[h] = (phi[h] - phi_high[h].astype(jnp.float32)).astype(jnp.bfloat16)

    for side in (1, 0):
        edge_values(side)
    blocks = CT // BLOCK
    early = (th < 2) & (xr == 0)
    open_at = jnp.where(early, blocks, 0)
    edge_at = jnp.where(early, blocks, 2)

    @pl.loop(0, blocks + 1)
    def _(i):
        pl.when(i == open_at)(open_sends)

        @pl.when(i == 0)
        def _():
            for copy in loads[5:]:
                copy.wait()

        pl.when(i == open_at)(line_sends)
        pl.when(i == jnp.where(early, blocks, 1))(u_sends)
        pl.when(i == 1)(tables)
        pl.when(i == edge_at)(edge_sends)

        @pl.when(i < blocks)
        def _():
            t = BLOCK * jnp.where(i == 0, 0, jnp.where(i == 1, blocks - 1, i - 1))

            @pl.loop(0, H)
            def _(h):
                update(state, first, CX, 0.5, t, h)

    for side in range(2):

        def _():
            x = CX - 1 if side == 0 else 0
            for f in range(HF):
                xfsend[side, pl.ds(f * CT, CT)] = first[f, x_rows(CX + x), :]
            x_copy(XF, side).start()

        when_x_target(side, _)

    def own_planes(b):
        x = 0 if b == 0 else CX - 1
        inner = 1 if b == 0 else CX - 2
        lines = lax.broadcasted_iota(jnp.int32, (CT, NR), 0)
        lanes = lax.broadcasted_iota(jnp.int32, (CT, NR), 1)
        top, bottom = lines == 0, lines == CT - 1
        left, right = lanes == 0, lanes == NR - 1
        ls, gxs, grs, gts = [], [], [], []
        for w in range(V):
            ls.append(l_rows[b, w])
            gx = gr = 0.0
            for v in range(V):
                gx = gx + l_rows[b, v] * a_axial[v, w]
                gr = gr + l_rows[b, v] * a_radial[v, w]
            gt = None
            for k in range(NPASS):
                row = 0.0
                for v in range(V):
                    row = row + l_rows[b, v] * a_theta[v, stagger[k], w]
                gt = row if gt is None else jnp.where(lines >= k * CPP, row, gt)
            gxs.append(gx)
            grs.append(gr)
            gts.append(gt)
        damp = sigma[x_rows(x), :] + 6.0 * viscosity
        dt = step[x_rows(x), :]

        @pl.loop(0, H)
        def _(h):
            freq = base_frequency * (h + 1).astype(jnp.float32)
            fields = [0.0, 0.0]
            rest = []
            for p in range(2):
                along_t = start = forcing = inside = radial = 0.0
                flux = sums = 0.0
                for w in range(V):
                    f = h * F + p * V + w
                    u = first[f, x_rows(CX + x), :]
                    near = first[f, x_rows(CX + inner), :]
                    tm = jnp.where(top, 0.0, pltpu.roll(u, 1, 0))
                    tp = jnp.where(bottom, 0.0, pltpu.roll(u, CT - 1, 0))
                    dx = near if b == 0 else -near
                    flux = flux + (gts[w] * (tp - tm) + gxs[w] * dx)
                    sums = sums + ls[w] * ((tp + tm) + near)
                    fields[p] = fields[p] + ls[w] * u
                    radial = radial + grs[w] * u
                    forcing = forcing + ls[w] * source[f, x_rows(x), :]
                    start = start + ls[w] * state[f, x_rows(CX + x), :]
                for value, weight, sign in ((radial, 0.5, -1.0), (fields[p], -viscosity, 1.0)):
                    rm = jnp.where(left, 0.0, pltpu.roll(value, 1, 1))
                    rp = jnp.where(right, 0.0, pltpu.roll(value, NR - 1, 1))
                    inside = inside + weight * (rp + sign * rm)
                res = 0.5 * flux - viscosity * sums + inside + damp * fields[p] - forcing
                rest.append((start, res))
            for p in range(2):
                start, res = rest[p]
                turned = -freq if p == 0 else freq
                res = res + turned * fields[1 - p]
                at = pl.ds(pl.multiple_of((2 * h + p) * PR, PR), CT)
                planes[at] = start - dt * res

    @pl.when(jnp.logical_not(has_lo))
    def _():
        own_planes(0)

    @pl.when(jnp.logical_not(has_hi))
    def _():
        own_planes(1)

    def ghosts(side):
        info_copy(side).wait_recv()
        ghost_step[side] = courant / (1.0 + info[side, pl.ds(0, 2 * CX)])
        kind = info[side, pl.ds(2 * CX, 8)]
        masks = [kind == float(k) for k in range(a_theta.shape[1])]
        for v in range(V):
            for w in range(V):
                entry = jnp.zeros((8, NR), jnp.float32)
                for k, mask in enumerate(masks):
                    entry = jnp.where(mask, a_theta[v, k, w], entry)
                ghost_matrix[side, v * V + w] = entry

    def crossed(side):
        return ((side == 1) & (th < T - 1)) | ((side == 0) & (th == 0))

    for side in (1, 0):
        pl.when(crossed(side))(lambda: ghosts(side))

    @pl.when(th == 0)
    def _():
        info_copy(1).start()
        u_copy(1).start()
        first_copy(1).start()
        for side in range(2):
            when_x_target(side, lambda: corner_copy(1, side).start())

    def cross(b, side):
        sign = 1.0 if side == 1 else -1.0
        x = 0 if b == 0 else CX - 1
        inner = 1 if b == 0 else CX - 2
        own_edge, own_next = (CT - 1, CT - 2) if side == 1 else (0, 1)
        ghost_edge, ghost_next = (CT, CT + 1) if side == 1 else (CT + 2, CT + 3)
        kind = stagger[own_edge // CPP]
        def rows_of(ref, which, j):
            return [ref[which, j, pl.ds(w, G, stride=V)] for w in range(V)]

        own_u, own_in, own_first = [rows_of(crit_send, 1 - side, j) for j in range(3)]
        ghost_u, ghost_in, ghost_first = [rows_of(crit, side, j) for j in range(3)]

        def wide(row):
            return jnp.broadcast_to(row, (G, NR))

        own_dt = wide(step[pl.ds(own_edge * CX + x, 1)])
        own_in_dt = wide(step[pl.ds(own_edge * CX + inner, 1)])
        own_next_dt = wide(step[pl.ds(own_next * CX + x, 1)])
        own_sigma = wide(sigma[pl.ds(own_edge * CX + x, 1)])
        ghost_dt = wide(ghost_step[side, pl.ds(x, 1)])
        ghost_in_dt = wide(ghost_step[side, pl.ds(inner, 1)])
        ghost_next_dt = wide(ghost_step[side, pl.ds(CX + x, 1)])
        ghost_sigma = wide(info[side, pl.ds(x, 1)])

        def own_matrix(v, w):
            return a_theta[v, kind, w]

        matrix = [[ghost_matrix[side, v * V + w] for w in range(V)] for v in range(V)]

        def changes(values, matrix, sign, dt):
            return [(-0.5 * dt) * term for term in halo_terms(values, matrix, sign)]

        def other_matrix(v, w):
            return matrix[v][w]

        own_d = changes(ghost_u, own_matrix, sign, own_dt)
        own_in_d = changes(ghost_in, own_matrix, sign, own_in_dt)
        ghost_d = changes(own_u, other_matrix, -sign, ghost_dt)
        ghost_in_d = changes(own_in, other_matrix, -sign, ghost_in_dt)
        ls = [l_rows[b, w] for w in range(V)]

        def contract(weights, values):
            total = weights[0] * values[0]
            for w in range(1, V):
                total = total + weights[w] * values[w]
            return total

        def column(matrix, w):
            total = ls[0] * matrix(0, w)
            for v in range(1, V):
                total = total + ls[v] * matrix(v, w)
            return total

        own_w = [(sign * 0.5) * column(own_matrix, w) - viscosity * ls[w] for w in range(V)]
        ghost_w = [(-sign * 0.5) * column(other_matrix, w) - viscosity * ls[w] for w in range(V)]
        flip = 0.5 if b == 0 else -0.5
        near_w = [
            flip * column(lambda v, w: a_axial[v, w], w) - viscosity * ls[w] for w in range(V)
        ]
        radial_w = [column(lambda v, w: a_radial[v, w], w) for w in range(V)]
        rows = lax.broadcasted_iota(jnp.int32, (G, NR), 0)
        lanes = lax.broadcasted_iota(jnp.int32, (G, NR), 1)
        odd = rows % 2 == 1
        freq = base_frequency * (rows // 2 + 1).astype(jnp.float32)
        freq = jnp.where(odd, freq, -freq)
        left, right = lanes == 0, lanes == NR - 1

        def local(d, d_in, damping):
            radial = contract(radial_w, d)
            fields = contract(ls, d)
            swapped = jnp.where(odd, pltpu.roll(fields, 1, 0), pltpu.roll(fields, G - 1, 0))
            total = contract(near_w, d_in) + freq * swapped
            total = total + (damping + 6.0 * viscosity) * fields
            for value, weight, sign in ((radial, 0.5, -1.0), (fields, -viscosity, 1.0)):
                rm = jnp.where(left, 0.0, pltpu.roll(value, 1, 1))
                rp = jnp.where(right, 0.0, pltpu.roll(value, NR - 1, 1))
                total = total + weight * (rp + sign * rm)
            return total

        total_ghost = [a + d for a, d in zip(ghost_first, ghost_d)]
        total_own = [a + d for a, d in zip(own_first, own_d)]
        found = {
            own_next: own_next_dt * contract(own_w, own_d),
            own_edge: own_dt * (local(own_d, own_in_d, own_sigma) + contract(own_w, total_ghost)),
            ghost_edge: ghost_dt
            * (local(ghost_d, ghost_in_d, ghost_sigma) + contract(ghost_w, total_own)),
            ghost_next: ghost_next_dt * contract(ghost_w, ghost_d),
        }
        for row, value in found.items():
            at = pl.ds(row, HP, stride=PR)
            planes[at, :] = planes[at, :] - value[:HP]

    def project(b):
        for h in range(H):
            values = planes[pl.ds(2 * h * PR, 2 * PR)]
            high = values.astype(jnp.bfloat16)
            low = (values - high.astype(jnp.float32)).astype(jnp.bfloat16)
            both = jnp.dot(
                jnp.concatenate([high, low], axis=0),
                phi_high[h],
                preferred_element_type=jnp.float32,
            )
            projected = both[: 2 * PR] + both[2 * PR :]
            projected = projected + jnp.dot(
                high, phi_low[h], preferred_element_type=jnp.float32
            )
            real, imag = projected[:PR], projected[PR:]
            weight = jnp.where(mode_plane[pl.ds(h, 1)] == b, scale, 0.0)
            part_real = jnp.sum(real * cosines[h] + imag * sines[h], axis=0, keepdims=True)
            part_imag = jnp.sum(imag * cosines[h] - real * sines[h], axis=0, keepdims=True)
            part[pl.ds(2 * h, 1)] = weight * part_real
            part[pl.ds(2 * h + 1, 1)] = weight * part_imag

    def finish_plane(b):
        @pl.when(th < T - 1)
        def _():
            crit_copy(1).wait_recv()
            cross(b, 1)

        @pl.when(th == 0)
        def _():
            crit_copy(0).wait_recv()
            cross(b, 0)

        project(b)

    @pl.when(jnp.logical_not(has_lo))
    def _():
        finish_plane(0)

    @pl.when(jnp.logical_not(has_hi))
    def _():
        finish_plane(1)

    def share(sem, t, x):
        pltpu.make_async_remote_copy(
            src_ref=part.at[pl.ds(0, HP)],
            dst_ref=parts.at[me, pl.ds(0, HP)],
            send_sem=psend_sem,
            recv_sem=sem,
            device_id=(t, x),
            device_id_type=MESH,
        ).start()

    shift = jnp.where(th < Q, Q, 0)

    @pl.when(th > 0)
    def _():
        ordered(shift, functools.partial(share, precv_sem))

    @pl.when(th == 0)
    def _():
        late_first(functools.partial(share, zrecv_sem))


    @pl.when(th > 0)
    def _():
        first_copy(1).start()

    @pl.when(th < T - 1)
    def _():
        first_copy(0).start()

    parts[me] = part[...]
    for side in (0, 1):
        pl.when(jnp.logical_not(crossed(side)))(lambda: ghosts(side))

    for side in range(2):

        def _():
            x_copy(XU, side).wait_recv()
            x = 0 if side == 0 else CX - 1
            dt = 0.5 * step[x_rows(x), :]

            def use(f, term):
                at = (f, x_rows(CX + x), slice(None))
                first[at] = first[at] - dt * term

            sign = -1.0 if side == 0 else 1.0
            each_terms(grouped(lambda f: xuhalo[side, f]), lambda v, w: a_axial[v, w], sign, use)

        when_x_source(side, _)

    def t_fix(side):
        u_copy(side).wait_recv()
        t = 0 if side == 0 else CT - 1
        kind = stagger[t // CPP]
        dt = 0.5 * step[pl.ds(t * CX, CX)]

        def use(f, term):
            at = (f, pl.ds(CX + t * CX, CX))
            first[at] = first[at] - dt * term

        sign = -1.0 if side == 0 else 1.0
        each_terms(grouped(lambda f: uhalo[side, f]), lambda v, w: a_theta[v, kind, w], sign, use)

    @pl.loop(0, blocks)
    def _(i):
        t = BLOCK * jnp.where(i + 1 >= blocks, i + 1 - blocks, i + 1)

        @pl.when(i == blocks - 2)
        def _():
            t_fix(1)

        @pl.when(i == blocks - 1)
        def _():
            t_fix(0)

        @pl.loop(0, H)
        def _(h):
            update(first, out, 0, 1.0, t, h)

    def corner_fix(side, x_side):
        corner_copy(side, x_side).wait_recv()
        t = 0 if side == 0 else CT - 1
        x = 0 if x_side == 0 else CX - 1
        kind = stagger[t // CPP]
        line_dt = 0.5 * courant / (1.0 + xinfo[x_side, pl.ds(t, 1)])
        edge_dt = 0.5 * ghost_step[side, pl.ds(x, 1)]

        values = [corner[side, x_side, pl.ds(w, 8, stride=V)] for w in range(V)]
        along_t = halo_terms(
            values, lambda v, w: a_theta[v, kind, w], -1.0 if side == 0 else 1.0
        )
        along_x = halo_terms(values, lambda v, w: a_axial[v, w], -1.0 if x_side == 0 else 1.0)
        for v in range(V):
            at = (x_side, pl.ds(v * CT + t, HP, stride=V * CT))
            xfhalo[at] = xfhalo[at] - (line_dt * along_t[v])[:HP]
            at = (side, pl.ds(v * CX + x, HP, stride=V * CX))
            fhalo[at] = fhalo[at] - (edge_dt * along_x[v])[:HP]

    def x_finish(side):
        x = 0 if side == 0 else CX - 1
        ghost_dt = 0.5 * courant / (1.0 + xinfo[side])
        dt = step[x_rows(x), :]
        away = -1.0 if side == 0 else 1.0

        ghosts = {}

        def keep(f, term):
            ghosts[f] = xfhalo[side, pl.ds(f * CT, CT)] - ghost_dt * term

        def use(f, term):
            at = (f, x_rows(x), slice(None))
            out[at] = out[at] - dt * term

        mine = grouped(lambda f: state[f, x_rows(CX + x), :])
        each_terms(mine, lambda v, w: a_axial[v, w], -away, keep)
        each_terms(grouped(lambda f: ghosts[f]), lambda v, w: a_axial[v, w], away, use)

    def t_finish(side):
        t = 0 if side == 0 else CT - 1
        kind = stagger[t // CPP]
        ghost_dt = 0.5 * ghost_step[side, pl.ds(0, CX)]
        dt = step[pl.ds(t * CX, CX)]
        away = -1.0 if side == 0 else 1.0

        values = {}

        def keep(f, term):
            values[f] = fhalo[side, pl.ds(f * CX, CX)] - ghost_dt * term

        def use(f, term):
            at = (f, pl.ds(t * CX, CX))
            out[at] = out[at] - dt * term

        mine = grouped(lambda f: state[f, pl.ds(CX + t * CX, CX)])
        each_terms(mine, lambda v, w: ghost_matrix[side, v * V + w], -away, keep)
        each_terms(grouped(lambda f: values[f]), lambda v, w: a_theta[v, kind, w], away, use)

    def shares(count, sem):
        return pltpu.make_async_remote_copy(
            src_ref=parts.at[pl.ds(0, count), pl.ds(0, HP)],
            dst_ref=parts.at[pl.ds(0, count), pl.ds(0, HP)],
            send_sem=psend_sem,
            recv_sem=sem,
            device_id=(up, xr),
            device_id_type=MESH,
        )

    def total_copy(j):
        return pltpu.make_async_remote_copy(
            src_ref=whole,
            dst_ref=whole,
            send_sem=wsend_sem.at[j],
            recv_sem=wrecv_sem,
            device_id=(th + Q + j * Q, xr),
            device_id_type=MESH,
        )

    serves = (th >= Q) & (th < 2 * Q)

    def gather(count):
        shares(count, precv_sem).wait_recv()
        total = parts[X]
        if N <= 64:
            for i in range(X + 1, N):
                total = total + parts[i]
        else:
            total = lax.fori_loop(X + 1, N, lambda i, acc: acc + parts[i], total)
        whole[...] = total

    @pl.when(serves)
    def _():
        gather(N - X - 1)
        for j in range(2):
            total_copy(j).start()

    for x_side in range(2):

        def _():
            x_copy(XF, x_side).wait_recv()
            x_copy(XINFO, x_side).wait_recv()

        when_x_source(x_side, _)
    for side in (1, 0):
        first_copy(side).wait_recv()
        for x_side in range(2):
            when_x_source(x_side, lambda: corner_fix(side, x_side))
        t_finish(side)
    for x_side in range(2):
        when_x_source(x_side, lambda: x_finish(x_side))

    @pl.when(th == 0)
    def _():
        gather(N - X)
        shares(X - 1, zrecv_sem).wait_recv()

    @pl.when(th > 0)
    def _():
        @pl.when(is_root & jnp.logical_not(serves))
        def _():
            gather(N - X - 1)

        @pl.when(jnp.logical_not(is_root))
        def _():
            total_copy(0).wait_recv()

        shares(X, zrecv_sem).wait_recv()

    total = whole[...]
    for x in range(X):
        total = total + parts[x]
    part_rows = [total[i : i + 1] for i in range(2 * H)]
    for h in range(H):
        for b in range(2):
            mine = mode_plane[pl.ds(h, 1)] == b
            for p in range(2):
                amps[h, b, pl.ds(p, 1)] = jnp.where(mine, part_rows[2 * h + p], 0.0)

    def correct(b, h):
        x = 0 if b == 0 else CX - 1
        weight = jnp.where(mode_plane[pl.ds(h, 1)] == b, scale, 0.0)
        real = weight * (part_rows[2 * h] - gust[h, pl.ds(0, 1)])
        imag = weight * (part_rows[2 * h + 1] - gust[h, pl.ds(1, 1)])
        cos, sin = cosines[h, pl.ds(0, CT)], sines[h, pl.ds(0, CT)]
        coef = jnp.concatenate(
            [real * cos - imag * sin, real * sin + imag * cos], axis=0
        )
        high = coef.astype(jnp.bfloat16)
        low = (coef - high.astype(jnp.float32)).astype(jnp.bfloat16)
        along = (((1,), (1,)), ((), ()))
        both = lax.dot_general(
            jnp.concatenate([high, low], axis=0),
            phi_high[h],
            along,
            preferred_element_type=jnp.float32,
        )
        q = both[: 2 * CT] + both[2 * CT :]
        q = q + lax.dot_general(
            high, phi_low[h], along, preferred_element_type=jnp.float32
        )
        for p in range(2):
            for v in range(V):
                at = (h * F + p * V + v, x_rows(x), slice(None))
                out[at] = out[at] - r_cols[b, v] * q[p * CT : (p + 1) * CT]

    @pl.when(jnp.logical_not(has_lo))
    def _():
        for h in range(H):
            correct(0, h)

    @pl.when(jnp.logical_not(has_hi))
    def _():
        for h in range(H):
            correct(1, h)

    @pl.when(th == 0)
    def _():
        shares(N - 1, precv_sem).wait_send()

    @pl.when((th > 0) & is_root)
    def _():
        shares(ROOTS * X - 1, precv_sem).wait_send()

    @pl.when(serves)
    def _():
        for j in range(2):
            total_copy(j).wait_send()

    @pl.when(jnp.logical_not(is_root))
    def _():
        shares(ROOTS * X, precv_sem).wait_send()

    @pl.when(on_plane & (th > 0))
    def _():
        crit_copy(1).wait_send()

    @pl.when(on_plane & (th == T - 1))
    def _():
        crit_copy(0).wait_send()

    for side in range(2):
        info_copy(side).wait_send()
        u_copy(side).wait_send()
        first_copy(side).wait_send()

        def _():
            for kind in (XU, XF, XINFO):
                x_copy(kind, side).wait_send()
            for t_side in range(2):
                corner_copy(t_side, side).wait_send()

        when_x_target(side, _)


def store_kernel(fields, amps, fields_out, amps_out, sems):
    copies = [
        pltpu.make_async_copy(fields, fields_out, sems.at[0]),
        pltpu.make_async_copy(amps, amps_out, sems.at[1]),
    ]
    for copy in copies:
        copy.start()
    for copy in copies:
        copy.wait()


def store(fields, amps):
    vmem = pl.BlockSpec(memory_space=pl.ANY)
    hbm = pl.BlockSpec(memory_space=pltpu.HBM)
    return pl.pallas_call(
        store_kernel,
        out_shape=tuple(jax.ShapeDtypeStruct(a.shape, a.dtype) for a in (fields, amps)),
        in_specs=(vmem, vmem),
        out_specs=(hbm, hbm),
        compiler_params=pltpu.CompilerParams(vmem_limit_bytes=2**20),
        scratch_shapes=[pltpu.SemaphoreType.DMA((2,))],
        name="store",
    )(fields, amps)


def local(T, X, *args):
    state, source, sigma, stagger = args[:4]
    H, two, V, CT, CX, NR = state.shape
    F = two * V
    HF = H * F
    NMODE = args[7].shape[1]
    dims = (T, X, H, V, CT, CX, NR, stagger.shape[0], NMODE)
    N = T * X
    rows = CT * CX
    f32 = jnp.float32
    hbm = pl.BlockSpec(memory_space=pl.ANY)
    vmem = pl.BlockSpec(memory_space=pltpu.VMEM)
    DMA = pltpu.SemaphoreType.DMA
    stagger, a_theta, a_axial, a_radial, orders, radial, planes, gust, l_rows, r_cols = args[3:]
    small = [stagger, jnp.swapaxes(a_theta, 0, 1), a_axial, a_radial, l_rows, r_cols]
    small += [orders, radial, planes, gust]
    pad = -(-2 * H // 8) * 8
    sides = [
        (HF, CX, NR),
        (HF * CX, NR),
        (HF * CX, NR),
        (HF, CT, NR),
        (HF, CT, NR),
        (HF * CT, NR),
        (HF * CT, NR),
        (CT, NR),
        (CT, NR),
        (2, 8 * V, NR),
        (2, 8 * V, NR),
        (3, 8 * V, NR),
        (3, 8 * V, NR),
        (2 * CX + 8, NR),
        (2 * CX + 8, NR),
        (2 * CX, NR),
        (V * V, 8, NR),
    ]
    fields, amplitudes = pl.pallas_call(
        functools.partial(kernel, dims),
        out_shape=(
            jax.ShapeDtypeStruct((HF, rows, NR), f32),
            jax.ShapeDtypeStruct((H, 2, 2, NMODE), f32),
        ),
        in_specs=[hbm] * 13,
        out_specs=(vmem, vmem),
        scratch_shapes=[pltpu.SMEM(a.shape, a.dtype) for a in small[:6]]
        + [pltpu.VMEM(a.shape, a.dtype) for a in small[6:]]
        + [
            pltpu.VMEM((HF, rows + 2 * CX, NR), f32),
            pltpu.VMEM((HF, rows, NR), f32),
            pltpu.VMEM((rows, NR), f32),
            pltpu.VMEM((HF, rows + 2 * CX, NR), f32),
            pltpu.VMEM((rows, NR), f32),
        ]
        + [pltpu.VMEM((2, *shape), f32) for shape in sides]
        + [
            pltpu.VMEM((2 * H * 2 * CT, NR), f32),
            pltpu.VMEM((2, 8 * V, NR), f32),
            pltpu.VMEM((H, NR, NMODE), f32),
            pltpu.VMEM((H, NR, NMODE), jnp.bfloat16),
            pltpu.VMEM((H, NR, NMODE), jnp.bfloat16),
            pltpu.VMEM((H, 2 * CT, NMODE), f32),
            pltpu.VMEM((H, 2 * CT, NMODE), f32),
            pltpu.VMEM((pad, NMODE), f32),
            pltpu.VMEM((N, pad, NMODE), f32),
            DMA((7,)),
            DMA((10,)),
            DMA((7, 2)),
            DMA((7, 2)),
            DMA((2, 2)),
            DMA((2, 2)),
            DMA,
            DMA,
            pltpu.VMEM((pad, NMODE), f32),
            DMA((2,)),
            DMA,
            DMA,
        ],
        compiler_params=pltpu.CompilerParams(
            collective_id=0, has_side_effects=True, vmem_limit_bytes=16 * 2**20
        ),
        name="wake",
    )(
        *(pltpu.with_memory_space_constraint(a, pltpu.HBM) for a in (state.reshape(HF, rows, NR),
        source.reshape(HF, rows, NR),
        sigma.reshape(rows, NR),
        *small)),
    )
    fields, amplitudes = store(fields, amplitudes)
    return fields.reshape(state.shape), amplitudes


def solution(mesh):
    field = P(None, None, None, "theta", "xr", None)
    placed = (field, field, P("theta", "xr", None), P("theta")) + (P(),) * 9
    return jax.shard_map(
        functools.partial(local, mesh.shape["theta"], mesh.shape["xr"]),
        mesh=mesh,
        in_specs=placed,
        out_specs=(field, P()),
        check_vma=False,
    )
```
